32 devices in a mesh: wide: 16 (over z, x, core), grp: 2 (over y).
Axes of the slice: x: 2, y: 2, z: 4, core: 2. Of those that a mesh axis runs over, the one named last changes fastest.
Arguments:
- tokens: bfloat16 [2, 32, 196, 768], P(None, ('wide', 'grp')), may hold values from -6 to 6
- cotangent: bfloat16 [2, 32, 196, 768], P(None, ('wide', 'grp')), may hold values from -6 to 6
- window_place: int32 [2, 32], P(None, ('wide', 'grp')), may hold values from 0 to 25
- master: float32 [55424, 128], P('grp'), may hold values from -2 to 2
- first_moment: float32 [55424, 128], P('grp'), may hold values from -3 to 3
- second_moment: float32 [55424, 128], P('grp'), may hold values from 0.05 to 1
Outputs:
- block_out: bfloat16 [2, 32, 196, 768], P(None, ('wide', 'grp'))
- input_grad: bfloat16 [2, 32, 196, 768], P(None, ('wide', 'grp'))
- grads: float32 [55424, 128], P('grp')
- master_next: float32 [55424, 128], P('grp')
- moment_next: float32 [55424, 128], P('grp')
- second_next: float32 [55424, 128], P('grp')
- weights_next: bfloat16 [55424, 128], replicated
- proj_bias_grad: float32 [768], replicated
The draws below stay inside these ranges and needn't reach their ends.
Inputs may be any that keep to these rules, and one draw needn't show every extreme that they name: `window_place`: place of a slot's window in its image's grid of 5 x 5 windows of 14 x 14 tokens, row by row, over the 64 x 64 token grid zero-padded at its ends; 25 marks an empty slot.
All inputs are finite; a program needn't handle non-finite values.
Results may differ from the reference program's by a relative error of at most 0.018.
Values may be sent and summed in bfloat16 or wider, within the bound.
No kernel may reach another device: no remote copies, remote signals or barrier semaphores. Data moves between devices by JAX's collectives and lax.ppermute only.
A program may use at most 320 MiB of HBM per device.

```python
import math
import jax
import jax.numpy as jnp
from jax import lax

D = 768
FF = 3072
HD = 64
WS = 14
GRID = 64
WTOK = 196
MB = 2
WIN_DEV = 1
SLOTS = 32
ROWS = 55424
ADAM_STEP = 10
N_WIDE = 16
N_GRP = 2


def draw_master(key, part):
    rel_span = 2 * WS - 1
    entries = ROWS * 128
    flat_idx = jnp.arange(entries, dtype=jnp.int32)
    normal_key = jax.random.fold_in(key, 11)
    gain_key = jax.random.fold_in(key, 23)
    normals = jax.random.truncated_normal(normal_key, -3.0, 3.0, (entries,), jnp.float32)
    gains = jax.random.uniform(gain_key, (entries,), jnp.float32, 0.5, 1.5)
    lengths = [D * 3 * D, 2 * D, D * D, D, D * FF, FF, FF * D, D, D, D, D, D, rel_span * HD, rel_span * HD]
    scales = [D ** (-0.5), 0.2, 4.0 * D ** (-0.5), 0.2, D ** (-0.5), 0.2, FF ** (-0.5), 0.2, -1.0, 0.3, -1.0, 0.3, 0.15, 0.15]
    drawn = 0.02 * normals
    offset = 0
    for length, factor in zip(lengths, scales):
        inside = (flat_idx >= offset) & (flat_idx < offset + length)
        if factor < 0:
            drawn = jnp.where(inside, gains, drawn)
        else:
            drawn = jnp.where(inside, normals * factor, drawn)
        offset = offset + length
    return drawn.reshape(ROWS, 128).astype(jnp.float32)


def set_ends(values, key, least, top_value):
    longest = values.shape.index(max(values.shape))
    spots = []
    for shift in (0, 1):
        where = [jax.random.randint(jax.random.fold_in(key, axis), (), 0, length) for axis, length in enumerate(values.shape)]
        where[longest] = (where[longest] + shift) % values.shape[longest]
        spots.append(tuple(where))
    return values.at[spots[0]].set(least).at[spots[1]].set(top_value)


def levels(rng, dims, cuts, least, top_value):
    level, own = 1.0, jax.random.fold_in(rng, 6)
    for axis_at, blocks in cuts:
        steps = jnp.exp(jax.random.uniform(jax.random.fold_in(own, axis_at), (blocks,), jnp.float32, least / len(cuts), top_value / len(cuts)))
        level = level * jnp.repeat(steps, dims[axis_at] // blocks).reshape([-1 if axis == axis_at else 1 for axis in range(len(dims))])
    return level


def normal_values(own_key, dims, scale, bound, split=(), kind=jnp.bfloat16):
    gain = levels(own_key, dims, split, -0.22, 0.18) if split else 1.0
    values = jax.random.normal(own_key, dims, jnp.float32) * scale * gain
    return jnp.minimum(jnp.maximum(values, -bound), bound).astype(kind)


def setup_inputs(seed: int = 0) -> dict:
    streams_of = jax.random.split(jax.random.key(seed), 7)
    return {
        "tokens": normal_values(streams_of[0], (MB, SLOTS, WTOK, D), 1.0, 6.0, ((1, 32),)),
        "cotangent": normal_values(streams_of[1], (MB, SLOTS, WTOK, D), 1.0, 6.0, ((1, 32),)),
        "window_place": set_ends(jax.random.randint(streams_of[2], (MB, SLOTS), 0, 26), jax.random.fold_in(streams_of[2], 1), 0, 25).astype(jnp.int32),
        "master": draw_master(jax.random.fold_in(streams_of[6], 71), 0),
        "first_moment": normal_values(streams_of[4], (ROWS, 128), 0.5, 3.0, ((0, 2),), jnp.float32),
        "second_moment": jnp.clip(jnp.exp(math.log(1.0) - 2.9957323 * jax.random.uniform(streams_of[5], (ROWS, 128), jnp.float32) ** levels(streams_of[5], (ROWS, 128), ((0, 2),), -0.2, 0.2)), 0.05, 1.0),
    }


HIGHEST = lax.Precision.HIGHEST
EPS_NORM = 1e-06
BETA_ONE = 0.9
BETA_TWO = 0.95
ADAM_EPS = 1e-08
LEARN_RATE = 0.02
DECAY_RATE = 0.1

@jax.custom_vjp
def low(v):
    return lax.optimization_barrier(v.astype(jnp.bfloat16)).astype(jnp.float32)

@jax.custom_vjp
def low_back(v):
    return v

def low_keep(v):
    return (low(v), None)

def low_pass(kept, grad):
    return (grad,)

def back_keep(v):
    return (v, None)

def back_low(kept, grad):
    return (low(grad),)
low.defvjp(low_keep, low_pass)
low_back.defvjp(back_keep, back_low)

def layout(feature):
    rel_span = 2 * WS - 1
    return [(feature, 3 * feature), (2 * feature,), (feature, feature), (feature,), (feature, FF), (FF,), (FF, feature), (feature,), (feature,), (feature,), (feature,), (feature,), (rel_span, HD), (rel_span, HD)]

def unpack(flat_vec, feature):
    members = []
    offset = 0
    for dims_of in layout(feature):
        length = math.prod(dims_of)
        members.append(flat_vec[offset:offset + length].reshape(dims_of))
        offset = offset + length
    return tuple(members)

def pack_flat(members, row_count):
    flat_parts = [member.reshape(-1) for member in members]
    filled = sum((part_vec.shape[0] for part_vec in flat_parts))
    flat_parts.append(jnp.zeros((row_count * 128 - filled,), jnp.float32))
    return jnp.concatenate(flat_parts).reshape(row_count, 128)

def token_mask(window_place):
    cells = jnp.arange(WS * WS, dtype=jnp.int32)
    inner_row = cells // WS
    inner_col = cells % WS
    places = window_place[..., None]
    live_slot = places < 25
    row_real = WS * (places // 5) + inner_row < GRID
    col_real = WS * (places % 5) + inner_col < GRID
    return jnp.where(live_slot & row_real & col_real, 1.0, 0.0).astype(jnp.float32)

def rel_index():
    rel_span = 2 * WS - 1
    query_pos = jnp.arange(WS, dtype=jnp.int32)[:, None, None]
    key_pos = jnp.arange(WS, dtype=jnp.int32)[None, :, None]
    offsets = jnp.arange(rel_span, dtype=jnp.int32)[None, None, :]
    return jnp.where(offsets == query_pos - key_pos + WS - 1, 1.0, 0.0).astype(jnp.float32)

def normalize(inputs):
    row_mean = lax.optimization_barrier(jnp.mean(inputs, -1, keepdims=True))
    centred = inputs - row_mean
    return centred * lax.rsqrt(lax.optimization_barrier(jnp.mean(centred * centred, -1, keepdims=True)) + EPS_NORM)

def project(lhs_rows, matrix):
    return jnp.einsum('gtd,de->gte', lhs_rows, matrix, precision=HIGHEST)

def attend(queries, key_rows, values, table_h, table_w, onehot):
    win_count = queries.shape[0]
    head_count = queries.shape[2]
    rel_span = table_h.shape[0]
    score_scale = 1.0 / math.sqrt(HD)
    direct = jnp.einsum('gqhc,gkhc->ghqk', queries, key_rows, precision=HIGHEST) * score_scale
    along_h = jnp.einsum('gqhc,rc->ghqr', queries, table_h, precision=HIGHEST).reshape(win_count, head_count, WS, WS, rel_span)
    along_w = jnp.einsum('gqhc,rc->ghqr', queries, table_w, precision=HIGHEST).reshape(win_count, head_count, WS, WS, rel_span)
    rel_rows = jnp.einsum('ghabr,akr->ghabk', along_h, onehot, precision=HIGHEST)
    rel_cols = jnp.einsum('ghabr,bkr->ghabk', along_w, onehot, precision=HIGHEST)
    scores = direct.reshape(win_count, head_count, WS, WS, WS, WS) + rel_rows[:, :, :, :, :, None] + rel_cols[:, :, :, :, None, :]
    scores = low_back(scores.reshape(win_count, head_count, WTOK, WTOK))
    attn_probs = low(jax.nn.softmax(scores, axis=-1))
    mixed_out = jnp.einsum('ghqk,gkhc->gqhc', attn_probs, values, precision=HIGHEST)
    return mixed_out.reshape(win_count, WTOK, head_count * HD)

def forward(inputs, keep_rows, params, onehot):
    qkv_w, qv_b, proj_w, proj_b, fc1_w, fc1_b, fc2_w, fc2_b, ln1_g, ln1_b, ln2_g, ln2_b, table_h, table_w = params
    win_count = inputs.shape[0]
    head_count = D // HD
    gate_mask = keep_rows[..., None]
    normed_one = low((normalize(inputs) * ln1_g + ln1_b) * gate_mask)
    bias_full = jnp.concatenate([qv_b[:D], jnp.zeros((D,), jnp.float32), qv_b[D:]])
    mixed = low(low_back(project(normed_one, qkv_w) + bias_full))
    queries = mixed[..., :D].reshape(win_count, WTOK, head_count, HD)
    key_rows = mixed[..., D:2 * D].reshape(win_count, WTOK, head_count, HD)
    values = mixed[..., 2 * D:].reshape(win_count, WTOK, head_count, HD)
    attended = jax.checkpoint(attend)(queries, key_rows, values, table_h, table_w, onehot)
    attended = low(low_back(attended))
    branch = low_back(project(attended, proj_w) + proj_b)
    resid = gate_mask * (inputs + branch)
    normed_two = low(normalize(resid) * ln2_g + ln2_b)
    pre_act = low_back(project(normed_two, fc1_w) + fc1_b)
    activation = low(jax.nn.gelu(pre_act, approximate=False))
    mlp_out = low_back(project(activation, fc2_w) + fc2_b)
    return gate_mask * (resid + mlp_out)

def adamw(master, first_moment, second_moment, grads):
    moment_next = BETA_ONE * first_moment + (1.0 - BETA_ONE) * grads
    second_next = BETA_TWO * second_moment + (1.0 - BETA_TWO) * grads * grads
    fix_one = 1.0 - BETA_ONE ** ADAM_STEP
    fix_two = 1.0 - BETA_TWO ** ADAM_STEP
    update = moment_next / fix_one / (jnp.sqrt(second_next / fix_two) + ADAM_EPS) + DECAY_RATE * master
    return (master - LEARN_RATE * update, moment_next, second_next)

def reference(tokens, cotangent, window_place, master, first_moment, second_moment):
    rounded = master.astype(jnp.bfloat16).astype(jnp.float32)
    params = unpack(rounded.reshape(-1), D)
    onehot = rel_index()
    masks = token_mask(window_place)
    per_scan = 4 * WIN_DEV
    steps_count = SLOTS // per_scan
    grad_sums = tuple((jnp.zeros(member.shape, jnp.float32) for member in params))
    block_parts = []
    grad_parts = []
    for micro in range(MB):
        inputs = tokens[micro].astype(jnp.float32).reshape(steps_count, per_scan, WTOK, D)
        cot_rows = cotangent[micro].astype(jnp.float32).reshape(steps_count, per_scan, WTOK, D)
        keep_all = masks[micro].reshape(steps_count, per_scan, WTOK)

        def advance(running, scan_items):
            inputs_g, cot_g, keep_g = scan_items

            def apply_block(inputs_in, params_in):
                return forward(inputs_in, keep_g, params_in, onehot)
            result, pullback = jax.vjp(apply_block, inputs_g, params)
            grad_in, grad_params = pullback(cot_g)
            running = tuple((acc_term + new_term for acc_term, new_term in zip(running, grad_params)))
            return (running, (result.astype(jnp.bfloat16), grad_in.astype(jnp.bfloat16)))
        grad_sums, (result_all, grad_all) = lax.scan(advance, grad_sums, (inputs, cot_rows, keep_all))
        block_parts.append(result_all.reshape(SLOTS, WTOK, D))
        grad_parts.append(grad_all.reshape(SLOTS, WTOK, D))
    block_out = jnp.stack(block_parts)
    input_grad = jnp.stack(grad_parts)
    factor = 1.0 / (MB * N_WIDE * N_GRP)
    grads = pack_flat(grad_sums, ROWS) * factor
    proj_bias_grad = grad_sums[3] * factor
    master_next, moment_next, second_next = adamw(master, first_moment, second_moment, grads)
    weights_next = master_next.astype(jnp.bfloat16)
    return (block_out, input_grad, grads, master_next, moment_next, second_next, weights_next, proj_bias_grad)
```

```python
import functools
import math

import jax
import jax.numpy as jnp
from jax import lax
from jax.experimental import pallas as pl
from jax.experimental.pallas import tpu as pltpu
from jax.sharding import PartitionSpec as P

FF = 3072
HD = 64
WS = 14
GRID = 64
ADAM_STEP = 10


EPS_NORM = 1e-06
BETA_ONE = 0.9
BETA_TWO = 0.95
ADAM_EPS = 1e-08
LEARN_RATE = 0.02
DECAY_RATE = 0.1


def layout(feature):
    rel_span = 2 * WS - 1
    return [
        (feature, 3 * feature),
        (2 * feature,),
        (feature, feature),
        (feature,),
        (feature, FF),
        (FF,),
        (FF, feature),
        (feature,),
        (feature,),
        (feature,),
        (feature,),
        (feature,),
        (rel_span, HD),
        (rel_span, HD),
    ]


def unpack(rows, feature):
    members = []
    row = 0
    dims = layout(feature)
    for dims_of in dims[:8]:
        length = math.prod(dims_of) // 128
        members.append(rows[row : row + length].reshape(dims_of))
        row = row + length
    tail_size = sum(math.prod(dims_of) for dims_of in dims[8:])
    tail = rows[row : row - (-tail_size // 128)].reshape(-1)
    offset = 0
    for dims_of in dims[8:]:
        length = math.prod(dims_of)
        members.append(tail[offset : offset + length].reshape(dims_of))
        offset = offset + length
    return tuple(members)


def token_mask(window_place):
    cells = jnp.arange(WS * WS, dtype=jnp.int32)
    inner_row = cells // WS
    inner_col = cells % WS
    places = window_place[..., None]
    live_slot = places < 25
    row_real = WS * (places // 5) + inner_row < GRID
    col_real = WS * (places % 5) + inner_col < GRID
    return jnp.where(live_slot & row_real & col_real, 1.0, 0.0).astype(jnp.float32)


def normalize(inputs):
    row_mean = jnp.mean(inputs, -1, keepdims=True)
    centred = inputs - row_mean
    inv_scale = lax.rsqrt(jnp.mean(centred * centred, -1, keepdims=True) + EPS_NORM)
    return (centred * inv_scale, inv_scale)


def norm_back(grad_hat, normed_hat, inv_scale):
    first_mean = jnp.mean(grad_hat, -1, keepdims=True)
    second_mean = jnp.mean(grad_hat * normed_hat, -1, keepdims=True)
    return inv_scale * (grad_hat - first_mean - normed_hat * second_mean)


def attend_kernel(q_ref, k_ref, v_ref, table_ref, shift_ref, key_ref, probs_ref, out_ref):
    shift = shift_ref[...]
    key_cells = key_ref[...]
    row_count = shift.shape[0]
    real_key = lax.broadcasted_iota(jnp.int32, (row_count, row_count), 1) < WS * WS
    for part in range(2):
        cut = slice(part * HD, (part + 1) * HD)
        queries = q_ref[:, cut]
        along = jnp.dot(queries, table_ref[...], preferred_element_type=jnp.float32)
        for bit in (1, 2, 4, 8):
            along = jnp.where((shift & bit) != 0, pltpu.roll(along, 128 - bit, 1), along)
        high = along.astype(jnp.bfloat16)
        low = (along - high.astype(jnp.float32)).astype(jnp.bfloat16)
        scores = dot_last(queries, k_ref[:, cut]) * (1.0 / math.sqrt(HD))
        scores = scores + dot_last(high, key_cells) + dot_last(low, key_cells)
        scores = jnp.where(real_key, scores, -1e30)
        powers = jnp.exp(scores - jnp.max(scores, -1, keepdims=True))
        probs = (powers / jnp.sum(powers, -1, keepdims=True)).astype(jnp.bfloat16)
        probs_ref[0, part] = probs
        out_ref[:, cut] = jnp.dot(
            probs, v_ref[:, cut], preferred_element_type=jnp.float32
        ).astype(jnp.bfloat16)


def attend_back_kernel(
    q_ref, k_ref, v_ref, probs_ref, grad_ref, table_ref, shift_ref, key_ref,
    dq_ref, dk_ref, dv_ref, dtable_ref,
):
    shift = shift_ref[...]
    key_cells = key_ref[...]
    scale = 1.0 / math.sqrt(HD)

    @pl.when((pl.program_id(0) == 0) & (pl.program_id(1) == 0))
    def _():
        dtable_ref[...] = jnp.zeros(dtable_ref.shape, jnp.float32)

    for part in range(2):
        cut = slice(part * HD, (part + 1) * HD)
        queries = q_ref[:, cut]
        grad = grad_ref[:, cut]
        probs = probs_ref[0, part]
        dv_ref[:, cut] = dot_first(probs, grad).astype(jnp.bfloat16)
        grad_probs = dot_last(grad, v_ref[:, cut])
        wide_probs = probs.astype(jnp.float32)
        inner = jnp.sum(wide_probs * grad_probs, -1, keepdims=True)
        grad_scores = (wide_probs * (grad_probs - inner)).astype(jnp.bfloat16)
        dk_ref[:, cut] = (dot_first(grad_scores, queries) * scale).astype(jnp.bfloat16)
        along = jnp.dot(grad_scores, key_cells, preferred_element_type=jnp.float32)
        for bit in (1, 2, 4, 8):
            along = jnp.where((shift & bit) != 0, pltpu.roll(along, bit, 1), along)
        high = along.astype(jnp.bfloat16)
        low = (along - high.astype(jnp.float32)).astype(jnp.bfloat16)
        grad_query = jnp.dot(grad_scores, k_ref[:, cut], preferred_element_type=jnp.float32) * scale
        grad_query = grad_query + dot_last(high, table_ref[...]) + dot_last(low, table_ref[...])
        dq_ref[:, cut] = grad_query.astype(jnp.bfloat16)
        dtable_ref[...] += dot_first(queries, high) + dot_first(queries, low)


def window_constants(row_count):
    cells = jnp.arange(row_count, dtype=jnp.int32)[:, None]
    lanes = jnp.arange(128, dtype=jnp.int32)[None, :]
    first = lanes < 64
    shift = jnp.where(first, WS - 1 - cells // WS, WS - 1 - cells % WS)
    live = cells < WS * WS
    shift = jnp.where(live, shift, 0)
    offset = jnp.where(first, lanes, lanes - 64)
    place = jnp.where(first, cells // WS, cells % WS)
    key_cells = jnp.where(live & (offset == place), 1.0, 0.0).astype(jnp.bfloat16)
    return shift, key_cells


def wide_table(table_h, table_w):
    pad = jnp.zeros((HD, 64 - table_h.shape[0]), table_h.dtype)
    return jnp.concatenate([table_h[::-1].T, pad, table_w[::-1].T, pad], 1)


def attend(mixed, table, shift, key_cells, feature):
    rows, pairs = shift.shape[0], feature // 128
    wins = mixed.shape[0] // rows
    whole = lambda shape: pl.BlockSpec(shape, lambda w, h: (0,) * len(shape))
    column = lambda base: pl.BlockSpec((rows, 128), lambda w, h: (w, base * pairs + h))
    return pl.pallas_call(
        attend_kernel,
        grid=(wins, pairs),
        in_specs=[column(0), column(1), column(2), whole((HD, 128)), whole((rows, 128)), whole((rows, 128))],
        out_specs=[
            pl.BlockSpec((1, 2, rows, rows), lambda w, h: (w, h, 0, 0)),
            pl.BlockSpec((rows, 128), lambda w, h: (w, h)),
        ],
        out_shape=[
            jax.ShapeDtypeStruct((wins, 2 * pairs, rows, rows), jnp.bfloat16),
            jax.ShapeDtypeStruct((wins * rows, feature), jnp.bfloat16),
        ],
        name="attend",
    )(mixed, mixed, mixed, table, shift, key_cells)


def attend_back(mixed, probs, grad_att, table, shift, key_cells, feature):
    rows, pairs = shift.shape[0], feature // 128
    wins = mixed.shape[0] // rows
    whole = lambda shape: pl.BlockSpec(shape, lambda w, h: (0,) * len(shape))
    column = lambda base: pl.BlockSpec((rows, 128), lambda w, h: (w, base * pairs + h))
    flat = jax.ShapeDtypeStruct((wins * rows, feature), jnp.bfloat16)
    return pl.pallas_call(
        attend_back_kernel,
        grid=(wins, pairs),
        in_specs=[
            column(0), column(1), column(2),
            pl.BlockSpec((1, 2, rows, rows), lambda w, h: (w, h, 0, 0)),
            column(0),
            whole((HD, 128)), whole((rows, 128)), whole((rows, 128)),
        ],
        out_specs=[column(0), column(0), column(0), whole((HD, 128))],
        out_shape=[flat, flat, flat, jax.ShapeDtypeStruct((HD, 128), jnp.float32)],
        name="attend_back",
    )(mixed, mixed, mixed, probs, grad_att, table, shift, key_cells)


def dot_last(left, right):
    return lax.dot_general(left, right, (((1,), (1,)), ((), ())), preferred_element_type=jnp.float32)


def dot_first(left, right):
    return lax.dot_general(left, right, (((0,), (0,)), ((), ())), preferred_element_type=jnp.float32)


def pack_kernel(
    n1_ref, dq_ref, dk_ref, dv_ref, att_ref, dproj_ref, n2_ref, dpre_ref, act_ref, dout_ref, tail_ref,
    out_ref, rows_ref, stage_ref, bias_ref, stage_sems, bias_sems,
    *, part_rows, share_rows, group_size,
):
    count = n1_ref.shape[0]
    ones = jnp.ones((16, count), jnp.bfloat16)

    def weight(base, left_ref, right_refs):
        width = sum(ref.shape[1] for ref in right_refs) // 128

        def block(f, carry):
            left = left_ref[:, pl.ds(pl.multiple_of(f * 128, 128), 128)]
            column = 0
            for ref in right_refs:
                product = dot_first(left, ref[...])
                for j in range(ref.shape[1] // 128):
                    rows_ref[pl.ds(base + f * 128 * width + column, 128, stride=width), :] = product[
                        :, j * 128 : (j + 1) * 128
                    ]
                    column += 1
            return carry

        lax.fori_loop(0, left_ref.shape[1] // 128, block, 0)
        return base + left_ref.shape[1] * width

    def bias(base, ref):
        total = jnp.dot(ones, ref[...], preferred_element_type=jnp.float32)
        for j in range(ref.shape[1] // 128):
            rows_ref[base + j : base + j + 1, :] = total[0:1, j * 128 : (j + 1) * 128]
        return base + ref.shape[1] // 128

    limit = stage_ref.shape[1]
    chunks = []
    for owner in range(group_size):
        low = 0
        while low < part_rows:
            size = min(limit, part_rows - low)
            chunks.append((owner * part_rows + low, owner * share_rows + low, size))
            low += size
    flying = {}
    sent = 0

    def emit(upto):
        nonlocal sent
        while sent < len(chunks) and chunks[sent][0] + chunks[sent][2] <= upto:
            source, target, size = chunks[sent]
            slot = sent % 2
            if slot in flying:
                flying.pop(slot).wait()
            step = next(s for s in (128, 64, 32, 16) if size % s == 0)

            def convert(i, carry, source=source, slot=slot, step=step):
                at = pl.multiple_of(i * step, step)
                stage_ref[slot, pl.ds(at, step), :] = rows_ref[
                    pl.ds(pl.multiple_of(source + at, 16), step), :
                ].astype(jnp.bfloat16)
                return carry

            lax.fori_loop(0, size // step, convert, 0)
            copy = pltpu.make_async_copy(
                stage_ref.at[slot, pl.ds(0, size), :],
                out_ref.at[pl.ds(target, size), :],
                stage_sems.at[slot],
            )
            copy.start()
            flying[slot] = copy
            sent += 1

    row = weight(0, n1_ref, [dq_ref, dk_ref, dv_ref])
    row = bias(row, dq_ref)
    row = bias(row, dv_ref)
    emit(row)
    row = weight(row, att_ref, [dproj_ref])
    proj_bias = row
    row = bias(row, dproj_ref)
    emit(row)
    bias_size = dproj_ref.shape[1] // 128
    spare = share_rows - part_rows
    bias_ref[...] = jnp.concatenate(
        [
            rows_ref[proj_bias : proj_bias + bias_size, :],
            jnp.zeros((spare - bias_size, 128), jnp.float32),
        ],
        0,
    ).astype(jnp.bfloat16)
    bias_copies = [
        pltpu.make_async_copy(
            bias_ref, out_ref.at[pl.ds(owner * share_rows + part_rows, spare), :], bias_sems.at[owner]
        )
        for owner in range(group_size)
    ]
    for copy in bias_copies:
        copy.start()
    row = weight(row, n2_ref, [dpre_ref])
    row = bias(row, dpre_ref)
    emit(row)
    row = weight(row, act_ref, [dout_ref])
    row = bias(row, dout_ref)
    emit(row)
    rows_ref[row : row + tail_ref.shape[0], :] = tail_ref[...]
    emit(group_size * part_rows)
    for slot in list(flying):
        flying.pop(slot).wait()
    for copy in bias_copies:
        copy.wait()


def pack_shares(factors, tail, part_rows, group_size, wide_size):
    feature = factors[0].shape[1]
    grain = 16 * wide_size
    share_rows = -(-(part_rows + feature // 128) // grain) * grain
    spare = share_rows - part_rows
    whole = pl.BlockSpec(memory_space=pltpu.VMEM)
    packed = pl.pallas_call(
        functools.partial(
            pack_kernel, part_rows=part_rows, share_rows=share_rows, group_size=group_size
        ),
        in_specs=[whole] * (len(factors) + 1),
        out_specs=pl.BlockSpec(memory_space=pl.ANY),
        out_shape=jax.ShapeDtypeStruct((group_size * share_rows, 128), jnp.bfloat16),
        scratch_shapes=[
            pltpu.VMEM((group_size * part_rows, 128), jnp.float32),
            pltpu.VMEM((2, 2048, 128), jnp.bfloat16),
            pltpu.VMEM((spare, 128), jnp.bfloat16),
            pltpu.SemaphoreType.DMA((2,)),
            pltpu.SemaphoreType.DMA((group_size,)),
        ],
        compiler_params=pltpu.CompilerParams(vmem_limit_bytes=60 * 1024 * 1024),
        name="pack_grads",
    )(*factors, tail)
    return packed, share_rows


def gelu_slope(pre_act):
    normal_cdf = 0.5 * (1.0 + jax.scipy.special.erf(pre_act / math.sqrt(2.0)))
    return normal_cdf + pre_act * jnp.exp(-0.5 * pre_act * pre_act) / math.sqrt(2.0 * math.pi)


def window_pass(tokens, cotangent, keep_mask, weights):
    (
        qkv_w,
        qv_b,
        proj_w,
        proj_b,
        fc1_w,
        fc1_b,
        fc2_w,
        fc2_b,
        ln1_g,
        ln1_b,
        ln2_g,
        ln2_b,
        table_h,
        table_w,
    ) = weights
    win_count, tok_count, feature = tokens.shape
    row_count = win_count * tok_count
    inputs = tokens.reshape(row_count, feature).astype(jnp.float32)
    keep_rows = keep_mask.reshape(row_count, 1)
    hat_one, scale_one = normalize(inputs)
    normed_one = (
        (hat_one * ln1_g.astype(jnp.float32) + ln1_b.astype(jnp.float32)) * keep_rows
    ).astype(jnp.bfloat16)
    bias_full = jnp.concatenate(
        [qv_b[:feature], jnp.zeros((feature,), jnp.bfloat16), qv_b[feature:]]
    ).astype(jnp.float32)
    mixed = (jnp.dot(normed_one, qkv_w, preferred_element_type=jnp.float32) + bias_full).astype(
        jnp.bfloat16
    )
    shift, key_cells = window_constants(tok_count)
    table = wide_table(table_h, table_w)
    probs, attended = attend(mixed, table, shift, key_cells, feature)
    resid = keep_rows * (
        inputs
        + jnp.dot(attended, proj_w, preferred_element_type=jnp.float32)
        + proj_b.astype(jnp.float32)
    )
    hat_two, scale_two = normalize(resid)
    normed_two = (hat_two * ln2_g.astype(jnp.float32) + ln2_b.astype(jnp.float32)).astype(
        jnp.bfloat16
    )
    pre_act = jnp.dot(normed_two, fc1_w, preferred_element_type=jnp.float32) + fc1_b.astype(
        jnp.float32
    )
    activation = jax.nn.gelu(pre_act, approximate=False).astype(jnp.bfloat16)
    result = keep_rows * (
        resid
        + jnp.dot(activation, fc2_w, preferred_element_type=jnp.float32)
        + fc2_b.astype(jnp.float32)
    )
    cot_rows = cotangent.reshape(row_count, feature).astype(jnp.float32) * keep_rows
    grad_out = cot_rows.astype(jnp.bfloat16)
    grad_act = jnp.einsum("nd,fd->nf", grad_out, fc2_w, preferred_element_type=jnp.float32)
    grad_pre = (grad_act * gelu_slope(pre_act)).astype(jnp.bfloat16)
    grad_norm_two = jnp.einsum("nf,df->nd", grad_pre, fc1_w, preferred_element_type=jnp.float32)
    grad_ln2_g = jnp.sum(grad_norm_two * hat_two, 0)
    grad_ln2_b = jnp.sum(grad_norm_two, 0)
    grad_resid = cot_rows + norm_back(grad_norm_two * ln2_g.astype(jnp.float32), hat_two, scale_two)
    grad_branch = keep_rows * grad_resid
    grad_proj = grad_branch.astype(jnp.bfloat16)
    grad_att = jnp.einsum(
        "ne,de->nd", grad_proj, proj_w, preferred_element_type=jnp.float32
    ).astype(jnp.bfloat16)
    grad_query, grad_keys, grad_values, grad_table = attend_back(
        mixed, probs, grad_att, table, shift, key_cells, feature
    )
    rel_span = table_h.shape[0]
    grad_table_h = grad_table[:, :rel_span].T[::-1]
    grad_table_w = grad_table[:, 64 : 64 + rel_span].T[::-1]
    grad_mixed = jnp.concatenate([grad_query, grad_keys, grad_values], -1)
    grad_norm_one = keep_rows * jnp.einsum(
        "nf,df->nd", grad_mixed, qkv_w, preferred_element_type=jnp.float32
    )
    grad_ln1_g = jnp.sum(grad_norm_one * hat_one, 0)
    grad_ln1_b = jnp.sum(grad_norm_one, 0)
    grad_input = grad_branch + norm_back(
        grad_norm_one * ln1_g.astype(jnp.float32), hat_one, scale_one
    )
    factors = (
        normed_one,
        grad_query,
        grad_keys,
        grad_values,
        attended,
        grad_proj,
        normed_two,
        grad_pre,
        activation,
        grad_out,
    )
    tail = (grad_ln1_g, grad_ln1_b, grad_ln2_g, grad_ln2_b, grad_table_h, grad_table_w)
    block_part = result.reshape(win_count, tok_count, feature).astype(jnp.bfloat16)
    input_part = grad_input.reshape(win_count, tok_count, feature).astype(jnp.bfloat16)
    return (block_part, input_part, factors, tail)


def body(tokens, cotangent, window_place, master, first_moment, second_moment):
    part_rows = master.shape[0]
    wide_size = lax.axis_size("wide")
    group_size = lax.axis_size("grp")
    feature = tokens.shape[-1]
    micro_count, slots, tok_count, _ = tokens.shape
    masks = token_mask(window_place)
    gathered = lax.all_gather(master.astype(jnp.bfloat16), "grp", axis=0, tiled=True)
    weights = unpack(gathered, feature)
    wins = micro_count * slots
    extra = -tok_count % 16

    def padded(values):
        values = values.reshape((wins,) + values.shape[2:])
        return jnp.pad(values, ((0, 0), (0, extra)) + ((0, 0),) * (values.ndim - 2))

    block_part, input_part, factors, tail = window_pass(
        padded(tokens), padded(cotangent), padded(masks), weights
    )
    filled = sum(math.prod(dims_of) for dims_of in layout(feature)[:8]) // 128
    tail = jnp.concatenate([member.reshape(-1) for member in tail])
    tail_rows = part_rows * group_size - filled
    tail = jnp.pad(tail, (0, tail_rows * 128 - tail.shape[0])).reshape(tail_rows, 128)
    packed, share_rows = pack_shares(factors, tail, part_rows, group_size, wide_size)
    owned = lax.psum_scatter(packed, ("grp", "wide"), scatter_dimension=0, tiled=True)
    totals = lax.all_gather(owned, "wide", axis=0, tiled=True).astype(jnp.float32)
    factor = 1.0 / (micro_count * wide_size * group_size)
    grads = totals[:part_rows] * factor
    proj_bias_grad = totals[part_rows : part_rows + feature // 128].reshape(-1) * factor
    moment_next = BETA_ONE * first_moment + (1.0 - BETA_ONE) * grads
    second_next = BETA_TWO * second_moment + (1.0 - BETA_TWO) * grads * grads
    fix_one = 1.0 - BETA_ONE**ADAM_STEP
    fix_two = 1.0 - BETA_TWO**ADAM_STEP
    update = (
        moment_next / fix_one / (jnp.sqrt(second_next / fix_two) + ADAM_EPS) + DECAY_RATE * master
    )
    master_next = master - LEARN_RATE * update
    weights_next = lax.all_gather(master_next.astype(jnp.bfloat16), "grp", axis=0, tiled=True)
    block_out = block_part[:, :tok_count].reshape(tokens.shape)
    input_grad = input_part[:, :tok_count].reshape(tokens.shape)
    return (
        block_out,
        input_grad,
        grads,
        master_next,
        moment_next,
        second_next,
        weights_next,
        proj_bias_grad,
    )


def solution(mesh):
    return jax.shard_map(
        body,
        mesh=mesh,
        in_specs=(
            P(None, ("wide", "grp"), None, None),
            P(None, ("wide", "grp"), None, None),
            P(None, ("wide", "grp")),
            P("grp", None),
            P("grp", None),
            P("grp", None),
        ),
        out_specs=(
            P(None, ("wide", "grp"), None, None),
            P(None, ("wide", "grp"), None, None),
            P("grp", None),
            P("grp", None),
            P("grp", None),
            P("grp", None),
            P(),
            P(),
        ),
        check_vma=False,
    )
```

```python
import functools
import math

import jax
import jax.numpy as jnp
from jax import lax
from jax.experimental import pallas as pl
from jax.experimental.pallas import tpu as pltpu
from jax.sharding import PartitionSpec as P

FF = 3072
HD = 64
WS = 14
GRID = 64
ADAM_STEP = 10


EPS_NORM = 1e-06
BETA_ONE = 0.9
BETA_TWO = 0.95
ADAM_EPS = 1e-08
LEARN_RATE = 0.02
DECAY_RATE = 0.1


def layout(feature):
    rel_span = 2 * WS - 1
    return [
        (feature, 3 * feature),
        (2 * feature,),
        (feature, feature),
        (feature,),
        (feature, FF),
        (FF,),
        (FF, feature),
        (feature,),
        (feature,),
        (feature,),
        (feature,),
        (feature,),
        (rel_span, HD),
        (rel_span, HD),
    ]


def unpack(rows, feature):
    members = []
    row = 0
    dims = layout(feature)
    for dims_of in dims[:8]:
        length = math.prod(dims_of) // 128
        members.append(rows[row : row + length].reshape(dims_of))
        row = row + length
    tail_size = sum(math.prod(dims_of) for dims_of in dims[8:])
    tail = rows[row : row - (-tail_size // 128)].reshape(-1)
    offset = 0
    for dims_of in dims[8:]:
        length = math.prod(dims_of)
        members.append(tail[offset : offset + length].reshape(dims_of))
        offset = offset + length
    return tuple(members)


def token_mask(window_place):
    cells = jnp.arange(WS * WS, dtype=jnp.int32)
    inner_row = cells // WS
    inner_col = cells % WS
    places = window_place[..., None]
    live_slot = places < 25
    row_real = WS * (places // 5) + inner_row < GRID
    col_real = WS * (places % 5) + inner_col < GRID
    return jnp.where(live_slot & row_real & col_real, 1.0, 0.0).astype(jnp.float32)


def normalize(inputs):
    row_mean = jnp.mean(inputs, -1, keepdims=True)
    centred = inputs - row_mean
    inv_scale = lax.rsqrt(jnp.mean(centred * centred, -1, keepdims=True) + EPS_NORM)
    return (centred * inv_scale, inv_scale)


def norm_back(grad_hat, normed_hat, inv_scale):
    first_mean = jnp.mean(grad_hat, -1, keepdims=True)
    second_mean = jnp.mean(grad_hat * normed_hat, -1, keepdims=True)
    return inv_scale * (grad_hat - first_mean - normed_hat * second_mean)


def attend_kernel(q_ref, k_ref, v_ref, table_ref, shift_ref, key_ref, probs_ref, out_ref):
    shift = shift_ref[...]
    key_cells = key_ref[...]
    row_count = shift.shape[0]
    real_key = lax.broadcasted_iota(jnp.int32, (row_count, row_count), 1) < WS * WS
    for part in range(2):
        cut = slice(part * HD, (part + 1) * HD)
        queries = q_ref[:, cut]
        along = jnp.dot(queries, table_ref[...], preferred_element_type=jnp.float32)
        for bit in (1, 2, 4, 8):
            along = jnp.where((shift & bit) != 0, pltpu.roll(along, 128 - bit, 1), along)
        high = along.astype(jnp.bfloat16)
        low = (along - high.astype(jnp.float32)).astype(jnp.bfloat16)
        scores = dot_last(queries, k_ref[:, cut]) * (1.0 / math.sqrt(HD))
        scores = scores + dot_last(high, key_cells) + dot_last(low, key_cells)
        scores = jnp.where(real_key, scores, -1e30)
        powers = jnp.exp(scores - jnp.max(scores, -1, keepdims=True))
        probs = (powers / jnp.sum(powers, -1, keepdims=True)).astype(jnp.bfloat16)
        probs_ref[0, part] = probs
        out_ref[:, cut] = jnp.dot(
            probs, v_ref[:, cut], preferred_element_type=jnp.float32
        ).astype(jnp.bfloat16)


def attend_back_kernel(
    q_ref, k_ref, v_ref, probs_ref, grad_ref, table_ref, shift_ref, key_ref,
    dq_ref, dk_ref, dv_ref, dtable_ref,
):
    shift = shift_ref[...]
    key_cells = key_ref[...]
    scale = 1.0 / math.sqrt(HD)

    @pl.when((pl.program_id(0) == 0) & (pl.program_id(1) == 0))
    def _():
        dtable_ref[...] = jnp.zeros(dtable_ref.shape, jnp.float32)

    for part in range(2):
        cut = slice(part * HD, (part + 1) * HD)
        queries = q_ref[:, cut]
        grad = grad_ref[:, cut]
        probs = probs_ref[0, part]
        dv_ref[:, cut] = dot_first(probs, grad).astype(jnp.bfloat16)
        grad_probs = dot_last(grad, v_ref[:, cut])
        wide_probs = probs.astype(jnp.float32)
        inner = jnp.sum(wide_probs * grad_probs, -1, keepdims=True)
        grad_scores = (wide_probs * (grad_probs - inner)).astype(jnp.bfloat16)
        dk_ref[:, cut] = (dot_first(grad_scores, queries) * scale).astype(jnp.bfloat16)
        along = jnp.dot(grad_scores, key_cells, preferred_element_type=jnp.float32)
        for bit in (1, 2, 4, 8):
            along = jnp.where((shift & bit) != 0, pltpu.roll(along, bit, 1), along)
        high = along.astype(jnp.bfloat16)
        low = (along - high.astype(jnp.float32)).astype(jnp.bfloat16)
        grad_query = jnp.dot(grad_scores, k_ref[:, cut], preferred_element_type=jnp.float32) * scale
        grad_query = grad_query + dot_last(high, table_ref[...]) + dot_last(low, table_ref[...])
        dq_ref[:, cut] = grad_query.astype(jnp.bfloat16)
        dtable_ref[...] += dot_first(queries, high) + dot_first(queries, low)


def window_constants(row_count):
    cells = jnp.arange(row_count, dtype=jnp.int32)[:, None]
    lanes = jnp.arange(128, dtype=jnp.int32)[None, :]
    first = lanes < 64
    shift = jnp.where(first, WS - 1 - cells // WS, WS - 1 - cells % WS)
    live = cells < WS * WS
    shift = jnp.where(live, shift, 0)
    offset = jnp.where(first, lanes, lanes - 64)
    place = jnp.where(first, cells // WS, cells % WS)
    key_cells = jnp.where(live & (offset == place), 1.0, 0.0).astype(jnp.bfloat16)
    return shift, key_cells


def wide_table(table_h, table_w):
    pad = jnp.zeros((HD, 64 - table_h.shape[0]), table_h.dtype)
    return jnp.concatenate([table_h[::-1].T, pad, table_w[::-1].T, pad], 1)


def attend(mixed, table, shift, key_cells, feature):
    rows, pairs = shift.shape[0], feature // 128
    wins = mixed.shape[0] // rows
    whole = lambda shape: pl.BlockSpec(shape, lambda w, h: (0,) * len(shape))
    column = lambda base: pl.BlockSpec((rows, 128), lambda w, h: (w, base * pairs + h))
    return pl.pallas_call(
        attend_kernel,
        grid=(wins, pairs),
        in_specs=[column(0), column(1), column(2), whole((HD, 128)), whole((rows, 128)), whole((rows, 128))],
        out_specs=[
            pl.BlockSpec((1, 2, rows, rows), lambda w, h: (w, h, 0, 0)),
            pl.BlockSpec((rows, 128), lambda w, h: (w, h)),
        ],
        out_shape=[
            jax.ShapeDtypeStruct((wins, 2 * pairs, rows, rows), jnp.bfloat16),
            jax.ShapeDtypeStruct((wins * rows, feature), jnp.bfloat16),
        ],
        name="attend",
    )(mixed, mixed, mixed, table, shift, key_cells)


def attend_back(mixed, probs, grad_att, table, shift, key_cells, feature):
    rows, pairs = shift.shape[0], feature // 128
    wins = mixed.shape[0] // rows
    whole = lambda shape: pl.BlockSpec(shape, lambda w, h: (0,) * len(shape))
    column = lambda base: pl.BlockSpec((rows, 128), lambda w, h: (w, base * pairs + h))
    flat = jax.ShapeDtypeStruct((wins * rows, feature), jnp.bfloat16)
    return pl.pallas_call(
        attend_back_kernel,
        grid=(wins, pairs),
        in_specs=[
            column(0), column(1), column(2),
            pl.BlockSpec((1, 2, rows, rows), lambda w, h: (w, h, 0, 0)),
            column(0),
            whole((HD, 128)), whole((rows, 128)), whole((rows, 128)),
        ],
        out_specs=[column(0), column(0), column(0), whole((HD, 128))],
        out_shape=[flat, flat, flat, jax.ShapeDtypeStruct((HD, 128), jnp.float32)],
        name="attend_back",
    )(mixed, mixed, mixed, probs, grad_att, table, shift, key_cells)


def dot_last(left, right):
    return lax.dot_general(left, right, (((1,), (1,)), ((), ())), preferred_element_type=jnp.float32)


def dot_first(left, right):
    return lax.dot_general(left, right, (((0,), (0,)), ((), ())), preferred_element_type=jnp.float32)


def pack_kernel(
    n1_ref, dq_ref, dk_ref, dv_ref, att_ref, dproj_ref, n2_ref, dpre_ref, act_ref, dout_ref, tail_ref,
    out_ref, rows_ref, stage_ref, bias_ref, stage_sems, bias_sems,
    *, part_rows, share_rows, group_size,
):
    count = n1_ref.shape[0]
    ones = jnp.ones((16, count), jnp.bfloat16)

    def weight(base, left_ref, right_refs):
        width = sum(ref.shape[1] for ref in right_refs) // 128

        def block(f, carry):
            left = left_ref[:, pl.ds(pl.multiple_of(f * 128, 128), 128)]
            column = 0
            for ref in right_refs:
                product = dot_first(left, ref[...])
                for j in range(ref.shape[1] // 128):
                    rows_ref[pl.ds(base + f * 128 * width + column, 128, stride=width), :] = product[
                        :, j * 128 : (j + 1) * 128
                    ]
                    column += 1
            return carry

        lax.fori_loop(0, left_ref.shape[1] // 128, block, 0)
        return base + left_ref.shape[1] * width

    def bias(base, ref):
        total = jnp.dot(ones, ref[...], preferred_element_type=jnp.float32)
        for j in range(ref.shape[1] // 128):
            rows_ref[base + j : base + j + 1, :] = total[0:1, j * 128 : (j + 1) * 128]
        return base + ref.shape[1] // 128

    limit = stage_ref.shape[1]
    chunks = []
    for owner in range(group_size):
        low = 0
        while low < part_rows:
            size = min(limit, part_rows - low)
            chunks.append((owner * part_rows + low, owner * share_rows + low, size))
            low += size
    flying = {}
    sent = 0

    def emit(upto):
        nonlocal sent
        while sent < len(chunks) and chunks[sent][0] + chunks[sent][2] <= upto:
            source, target, size = chunks[sent]
            slot = sent % 2
            if slot in flying:
                flying.pop(slot).wait()
            step = next(s for s in (128, 64, 32, 16) if size % s == 0)

            def convert(i, carry, source=source, slot=slot, step=step):
                at = pl.multiple_of(i * step, step)
                stage_ref[slot, pl.ds(at, step), :] = rows_ref[
                    pl.ds(pl.multiple_of(source + at, 16), step), :
                ].astype(jnp.bfloat16)
                return carry

            lax.fori_loop(0, size // step, convert, 0)
            copy = pltpu.make_async_copy(
                stage_ref.at[slot, pl.ds(0, size), :],
                out_ref.at[pl.ds(target, size), :],
                stage_sems.at[slot],
            )
            copy.start()
            flying[slot] = copy
            sent += 1

    row = weight(0, n1_ref, [dq_ref, dk_ref, dv_ref])
    row = bias(row, dq_ref)
    row = bias(row, dv_ref)
    emit(row)
    row = weight(row, att_ref, [dproj_ref])
    proj_bias = row
    row = bias(row, dproj_ref)
    emit(row)
    bias_size = dproj_ref.shape[1] // 128
    spare = share_rows - part_rows
    bias_ref[...] = jnp.concatenate(
        [
            rows_ref[proj_bias : proj_bias + bias_size, :],
            jnp.zeros((spare - bias_size, 128), jnp.float32),
        ],
        0,
    ).astype(jnp.bfloat16)
    bias_copies = [
        pltpu.make_async_copy(
            bias_ref, out_ref.at[pl.ds(owner * share_rows + part_rows, spare), :], bias_sems.at[owner]
        )
        for owner in range(group_size)
    ]
    for copy in bias_copies:
        copy.start()
    row = weight(row, n2_ref, [dpre_ref])
    row = bias(row, dpre_ref)
    emit(row)
    row = weight(row, act_ref, [dout_ref])
    row = bias(row, dout_ref)
    emit(row)
    rows_ref[row : row + tail_ref.shape[0], :] = tail_ref[...]
    emit(group_size * part_rows)
    for slot in list(flying):
        flying.pop(slot).wait()
    for copy in bias_copies:
        copy.wait()


def pack_shares(factors, tail, part_rows, group_size, wide_size):
    feature = factors[0].shape[1]
    grain = 16 * wide_size
    share_rows = -(-(part_rows + feature // 128) // grain) * grain
    spare = share_rows - part_rows
    whole = pl.BlockSpec(memory_space=pltpu.VMEM)
    packed = pl.pallas_call(
        functools.partial(
            pack_kernel, part_rows=part_rows, share_rows=share_rows, group_size=group_size
        ),
        in_specs=[whole] * (len(factors) + 1),
        out_specs=pl.BlockSpec(memory_space=pl.ANY),
        out_shape=jax.ShapeDtypeStruct((group_size * share_rows, 128), jnp.bfloat16),
        scratch_shapes=[
            pltpu.VMEM((group_size * part_rows, 128), jnp.float32),
            pltpu.VMEM((2, 2048, 128), jnp.bfloat16),
            pltpu.VMEM((spare, 128), jnp.bfloat16),
            pltpu.SemaphoreType.DMA((2,)),
            pltpu.SemaphoreType.DMA((group_size,)),
        ],
        compiler_params=pltpu.CompilerParams(vmem_limit_bytes=60 * 1024 * 1024),
        name="pack_grads",
    )(*factors, tail)
    return packed, share_rows


def gelu_slope(pre_act):
    normal_cdf = 0.5 * (1.0 + jax.scipy.special.erf(pre_act / math.sqrt(2.0)))
    return normal_cdf + pre_act * jnp.exp(-0.5 * pre_act * pre_act) / math.sqrt(2.0 * math.pi)


def window_pass(tokens, cotangent, keep_mask, weights):
    (
        qkv_w,
        qv_b,
        proj_w,
        proj_b,
        fc1_w,
        fc1_b,
        fc2_w,
        fc2_b,
        ln1_g,
        ln1_b,
        ln2_g,
        ln2_b,
        table_h,
        table_w,
    ) = weights
    win_count, tok_count, feature = tokens.shape
    row_count = win_count * tok_count
    inputs = tokens.reshape(row_count, feature).astype(jnp.float32)
    keep_rows = keep_mask.reshape(row_count, 1)
    hat_one, scale_one = normalize(inputs)
    normed_one = (
        (hat_one * ln1_g.astype(jnp.float32) + ln1_b.astype(jnp.float32)) * keep_rows
    ).astype(jnp.bfloat16)
    bias_full = jnp.concatenate(
        [qv_b[:feature], jnp.zeros((feature,), jnp.bfloat16), qv_b[feature:]]
    ).astype(jnp.float32)
    mixed = (jnp.dot(normed_one, qkv_w, preferred_element_type=jnp.float32) + bias_full).astype(
        jnp.bfloat16
    )
    shift, key_cells = window_constants(tok_count)
    table = wide_table(table_h, table_w)
    probs, attended = attend(mixed, table, shift, key_cells, feature)
    resid = keep_rows * (
        inputs
        + jnp.dot(attended, proj_w, preferred_element_type=jnp.float32)
        + proj_b.astype(jnp.float32)
    )
    hat_two, scale_two = normalize(resid)
    normed_two = (hat_two * ln2_g.astype(jnp.float32) + ln2_b.astype(jnp.float32)).astype(
        jnp.bfloat16
    )
    pre_act = jnp.dot(normed_two, fc1_w, preferred_element_type=jnp.float32) + fc1_b.astype(
        jnp.float32
    )
    activation = jax.nn.gelu(pre_act, approximate=False).astype(jnp.bfloat16)
    result = keep_rows * (
        resid
        + jnp.dot(activation, fc2_w, preferred_element_type=jnp.float32)
        + fc2_b.astype(jnp.float32)
    )
    cot_rows = cotangent.reshape(row_count, feature).astype(jnp.float32) * keep_rows
    grad_out = cot_rows.astype(jnp.bfloat16)
    grad_act = jnp.einsum("nd,fd->nf", grad_out, fc2_w, preferred_element_type=jnp.float32)
    grad_pre = (grad_act * gelu_slope(pre_act)).astype(jnp.bfloat16)
    grad_norm_two = jnp.einsum("nf,df->nd", grad_pre, fc1_w, preferred_element_type=jnp.float32)
    grad_ln2_g = jnp.sum(grad_norm_two * hat_two, 0)
    grad_ln2_b = jnp.sum(grad_norm_two, 0)
    grad_resid = cot_rows + norm_back(grad_norm_two * ln2_g.astype(jnp.float32), hat_two, scale_two)
    grad_branch = keep_rows * grad_resid
    grad_proj = grad_branch.astype(jnp.bfloat16)
    grad_att = jnp.einsum(
        "ne,de->nd", grad_proj, proj_w, preferred_element_type=jnp.float32
    ).astype(jnp.bfloat16)
    grad_query, grad_keys, grad_values, grad_table = attend_back(
        mixed, probs, grad_att, table, shift, key_cells, feature
    )
    rel_span = table_h.shape[0]
    grad_table_h = grad_table[:, :rel_span].T[::-1]
    grad_table_w = grad_table[:, 64 : 64 + rel_span].T[::-1]
    grad_mixed = jnp.concatenate([grad_query, grad_keys, grad_values], -1)
    grad_norm_one = keep_rows * jnp.einsum(
        "nf,df->nd", grad_mixed, qkv_w, preferred_element_type=jnp.float32
    )
    grad_ln1_g = jnp.sum(grad_norm_one * hat_one, 0)
    grad_ln1_b = jnp.sum(grad_norm_one, 0)
    grad_input = grad_branch + norm_back(
        grad_norm_one * ln1_g.astype(jnp.float32), hat_one, scale_one
    )
    factors = (
        normed_one,
        grad_query,
        grad_keys,
        grad_values,
        attended,
        grad_proj,
        normed_two,
        grad_pre,
        activation,
        grad_out,
    )
    tail = (grad_ln1_g, grad_ln1_b, grad_ln2_g, grad_ln2_b, grad_table_h, grad_table_w)
    block_part = result.reshape(win_count, tok_count, feature).astype(jnp.bfloat16)
    input_part = grad_input.reshape(win_count, tok_count, feature).astype(jnp.bfloat16)
    return (block_part, input_part, factors, tail)


def swap(values, axis, bit):
    return lax.ppermute(values, axis, [(i, i ^ bit) for i in range(lax.axis_size(axis))])


def wide_bits(count):
    place = lax.axis_index("wide")
    return [(place >> bit) & 1 for bit in range(count)]


def splits(part_rows):
    return lax.axis_size("grp") == 2 and lax.axis_size("wide") % 8 == 0 and part_rows % 64 == 0


def eighth_index(core, cross, deep):
    return (core * 2 + cross) * 2 + deep


def gather_groups(mine, diagonal, own):
    core, cross, deep = wide_bits(3)
    first = swap(mine, "grp", 1)
    last = swap(diagonal, "grp", 1)
    side = swap(first, "wide", 2)
    back = swap(first, "wide", 4)
    near = (first, side, back, last)
    far = [swap(part, "wide", 1) for part in near]
    group = lax.axis_index("grp")
    out = jnp.zeros((2, 8) + mine.shape, mine.dtype)
    out = lax.dynamic_update_slice(out, own.reshape((1, 8) + mine.shape), (group, 0, 0, 0))
    for parts, which in ((near, core), (far, 1 - core)):
        for part, flip_cross, flip_deep in zip(parts, (0, 1, 0, 1), (0, 0, 1, 1)):
            at = eighth_index(which, cross ^ flip_cross, deep ^ flip_deep)
            out = lax.dynamic_update_slice(out, part[None, None], (1 - group, at, 0, 0))
    return out.reshape(2 * own.shape[0], 128)


def own_eighths(rows):
    core, cross, deep = wide_bits(3)
    parts = rows.reshape(8, -1, 128)
    spots = (eighth_index(core, cross, deep), eighth_index(core, 1 - cross, 1 - deep))
    return [lax.dynamic_index_in_dim(parts, spot, keepdims=False) for spot in spots]


def adam(grads, master, first_moment, second_moment):
    moment_next = BETA_ONE * first_moment + (1.0 - BETA_ONE) * grads
    second_next = BETA_TWO * second_moment + (1.0 - BETA_TWO) * grads * grads
    fix_one = 1.0 - BETA_ONE**ADAM_STEP
    fix_two = 1.0 - BETA_TWO**ADAM_STEP
    update = (
        moment_next / fix_one / (jnp.sqrt(second_next / fix_two) + ADAM_EPS) + DECAY_RATE * master
    )
    return (master - LEARN_RATE * update, moment_next, second_next)


def body(tokens, cotangent, window_place, master, first_moment, second_moment):
    part_rows = master.shape[0]
    wide_size = lax.axis_size("wide")
    group_size = lax.axis_size("grp")
    feature = tokens.shape[-1]
    micro_count, slots, tok_count, _ = tokens.shape
    masks = token_mask(window_place)
    if splits(part_rows):
        mine, diagonal = (part.astype(jnp.bfloat16) for part in own_eighths(master))
        gathered = gather_groups(mine, diagonal, master.astype(jnp.bfloat16))
    else:
        gathered = lax.all_gather(master.astype(jnp.bfloat16), "grp", axis=0, tiled=True)
    weights = unpack(gathered, feature)
    wins = micro_count * slots
    extra = -tok_count % 16

    def padded(values):
        values = values.reshape((wins,) + values.shape[2:])
        return jnp.pad(values, ((0, 0), (0, extra)) + ((0, 0),) * (values.ndim - 2))

    block_part, input_part, factors, tail = window_pass(
        padded(tokens), padded(cotangent), padded(masks), weights
    )
    filled = sum(math.prod(dims_of) for dims_of in layout(feature)[:8]) // 128
    tail = jnp.concatenate([member.reshape(-1) for member in tail])
    tail_rows = part_rows * group_size - filled
    tail = jnp.pad(tail, (0, tail_rows * 128 - tail.shape[0])).reshape(tail_rows, 128)
    packed, share_rows = pack_shares(factors, tail, part_rows, group_size, wide_size)
    owned = lax.psum_scatter(packed, ("grp", "wide"), scatter_dimension=0, tiled=True)
    totals = lax.all_gather(owned, "wide", axis=0, tiled=True)
    factor = 1.0 / (micro_count * wide_size * group_size)
    bias_total = totals[part_rows : part_rows + feature // 128]
    proj_bias_grad = bias_total.astype(jnp.float32).reshape(-1) * factor
    totals = totals[:part_rows]

    def step(total_rows, *state):
        grads = total_rows.astype(jnp.float32) * factor
        return (grads,) + adam(grads, *state)

    state = (master, first_moment, second_moment)
    grads, master_next, moment_next, second_next = step(totals, *state)
    own_weights = master_next.astype(jnp.bfloat16)
    if splits(part_rows):
        pieces = zip(*(own_eighths(rows) for rows in (totals,) + state))
        mine, diagonal = (step(*piece)[1].astype(jnp.bfloat16) for piece in pieces)
        weights_next = gather_groups(mine, diagonal, own_weights)
    else:
        weights_next = lax.all_gather(own_weights, "grp", axis=0, tiled=True)
    block_out = block_part[:, :tok_count].reshape(tokens.shape)
    input_grad = input_part[:, :tok_count].reshape(tokens.shape)
    return (
        block_out,
        input_grad,
        grads,
        master_next,
        moment_next,
        second_next,
        weights_next,
        proj_bias_grad,
    )


def solution(mesh):
    return jax.shard_map(
        body,
        mesh=mesh,
        in_specs=(
            P(None, ("wide", "grp"), None, None),
            P(None, ("wide", "grp"), None, None),
            P(None, ("wide", "grp")),
            P("grp", None),
            P("grp", None),
            P("grp", None),
        ),
        out_specs=(
            P(None, ("wide", "grp"), None, None),
            P(None, ("wide", "grp"), None, None),
            P("grp", None),
            P("grp", None),
            P("grp", None),
            P("grp", None),
            P(),
            P(),
        ),
        check_vma=False,
    )
```

```python
import functools
import math

import jax
import jax.numpy as jnp
from jax import lax
from jax.experimental import pallas as pl
from jax.experimental.pallas import tpu as pltpu
from jax.sharding import PartitionSpec as P

FF = 3072
HD = 64
WS = 14
GRID = 64
ADAM_STEP = 10


EPS_NORM = 1e-06
BETA_ONE = 0.9
BETA_TWO = 0.95
ADAM_EPS = 1e-08
LEARN_RATE = 0.02
DECAY_RATE = 0.1


def layout(feature):
    rel_span = 2 * WS - 1
    return [
        (feature, 3 * feature),
        (2 * feature,),
        (feature, feature),
        (feature,),
        (feature, FF),
        (FF,),
        (FF, feature),
        (feature,),
        (feature,),
        (feature,),
        (feature,),
        (feature,),
        (rel_span, HD),
        (rel_span, HD),
    ]


def unpack(rows, feature):
    members = []
    row = 0
    dims = layout(feature)
    for dims_of in dims[:8]:
        length = math.prod(dims_of) // 128
        members.append(rows[row : row + length].reshape(dims_of))
        row = row + length
    tail_size = sum(math.prod(dims_of) for dims_of in dims[8:])
    tail = rows[row : row - (-tail_size // 128)].reshape(-1)
    offset = 0
    for dims_of in dims[8:]:
        length = math.prod(dims_of)
        members.append(tail[offset : offset + length].reshape(dims_of))
        offset = offset + length
    return tuple(members)


def token_mask(window_place):
    cells = jnp.arange(WS * WS, dtype=jnp.int32)
    inner_row = cells // WS
    inner_col = cells % WS
    places = window_place[..., None]
    live_slot = places < 25
    row_real = WS * (places // 5) + inner_row < GRID
    col_real = WS * (places % 5) + inner_col < GRID
    return jnp.where(live_slot & row_real & col_real, 1.0, 0.0).astype(jnp.float32)


def normalize(inputs):
    row_mean = jnp.mean(inputs, -1, keepdims=True)
    centred = inputs - row_mean
    inv_scale = lax.rsqrt(jnp.mean(centred * centred, -1, keepdims=True) + EPS_NORM)
    return (centred * inv_scale, inv_scale)


def norm_back(grad_hat, normed_hat, inv_scale):
    first_mean = jnp.mean(grad_hat, -1, keepdims=True)
    second_mean = jnp.mean(grad_hat * normed_hat, -1, keepdims=True)
    return inv_scale * (grad_hat - first_mean - normed_hat * second_mean)


def attend_kernel(q_ref, k_ref, v_ref, table_ref, shift_ref, key_ref, probs_ref, out_ref):
    shift = shift_ref[...]
    key_cells = key_ref[...]
    row_count = shift.shape[0]
    real_key = lax.broadcasted_iota(jnp.int32, (row_count, row_count), 1) < WS * WS
    for part in range(2):
        cut = slice(part * HD, (part + 1) * HD)
        queries = q_ref[:, cut]
        along = jnp.dot(queries, table_ref[...], preferred_element_type=jnp.float32)
        for bit in (1, 2, 4, 8):
            along = jnp.where((shift & bit) != 0, pltpu.roll(along, 128 - bit, 1), along)
        high = along.astype(jnp.bfloat16)
        low = (along - high.astype(jnp.float32)).astype(jnp.bfloat16)
        scores = dot_last(queries, k_ref[:, cut]) * (1.0 / math.sqrt(HD))
        scores = scores + dot_last(high, key_cells) + dot_last(low, key_cells)
        scores = jnp.where(real_key, scores, -1e30)
        powers = jnp.exp(scores - jnp.max(scores, -1, keepdims=True))
        probs = (powers / jnp.sum(powers, -1, keepdims=True)).astype(jnp.bfloat16)
        probs_ref[0, part] = probs
        out_ref[:, cut] = jnp.dot(
            probs, v_ref[:, cut], preferred_element_type=jnp.float32
        ).astype(jnp.bfloat16)


def attend_back_kernel(
    q_ref, k_ref, v_ref, probs_ref, grad_ref, table_ref, shift_ref, key_ref,
    dq_ref, dk_ref, dv_ref, dtable_ref,
):
    shift = shift_ref[...]
    key_cells = key_ref[...]
    scale = 1.0 / math.sqrt(HD)

    @pl.when((pl.program_id(0) == 0) & (pl.program_id(1) == 0))
    def _():
        dtable_ref[...] = jnp.zeros(dtable_ref.shape, jnp.float32)

    for part in range(2):
        cut = slice(part * HD, (part + 1) * HD)
        queries = q_ref[:, cut]
        grad = grad_ref[:, cut]
        probs = probs_ref[0, part]
        dv_ref[:, cut] = dot_first(probs, grad).astype(jnp.bfloat16)
        grad_probs = dot_last(grad, v_ref[:, cut])
        wide_probs = probs.astype(jnp.float32)
        inner = jnp.sum(wide_probs * grad_probs, -1, keepdims=True)
        grad_scores = (wide_probs * (grad_probs - inner)).astype(jnp.bfloat16)
        dk_ref[:, cut] = (dot_first(grad_scores, queries) * scale).astype(jnp.bfloat16)
        along = jnp.dot(grad_scores, key_cells, preferred_element_type=jnp.float32)
        for bit in (1, 2, 4, 8):
            along = jnp.where((shift & bit) != 0, pltpu.roll(along, bit, 1), along)
        high = along.astype(jnp.bfloat16)
        low = (along - high.astype(jnp.float32)).astype(jnp.bfloat16)
        grad_query = jnp.dot(grad_scores, k_ref[:, cut], preferred_element_type=jnp.float32) * scale
        grad_query = grad_query + dot_last(high, table_ref[...]) + dot_last(low, table_ref[...])
        dq_ref[:, cut] = grad_query.astype(jnp.bfloat16)
        dtable_ref[...] += dot_first(queries, high) + dot_first(queries, low)


def window_constants(row_count):
    cells = jnp.arange(row_count, dtype=jnp.int32)[:, None]
    lanes = jnp.arange(128, dtype=jnp.int32)[None, :]
    first = lanes < 64
    shift = jnp.where(first, WS - 1 - cells // WS, WS - 1 - cells % WS)
    live = cells < WS * WS
    shift = jnp.where(live, shift, 0)
    offset = jnp.where(first, lanes, lanes - 64)
    place = jnp.where(first, cells // WS, cells % WS)
    key_cells = jnp.where(live & (offset == place), 1.0, 0.0).astype(jnp.bfloat16)
    return shift, key_cells


def wide_table(table_h, table_w):
    pad = jnp.zeros((HD, 64 - table_h.shape[0]), table_h.dtype)
    return jnp.concatenate([table_h[::-1].T, pad, table_w[::-1].T, pad], 1)


def attend(mixed, table, shift, key_cells, feature):
    rows, pairs = shift.shape[0], feature // 128
    wins = mixed.shape[0] // rows
    whole = lambda shape: pl.BlockSpec(shape, lambda w, h: (0,) * len(shape))
    column = lambda base: pl.BlockSpec((rows, 128), lambda w, h: (w, base * pairs + h))
    return pl.pallas_call(
        attend_kernel,
        grid=(wins, pairs),
        in_specs=[column(0), column(1), column(2), whole((HD, 128)), whole((rows, 128)), whole((rows, 128))],
        out_specs=[
            pl.BlockSpec((1, 2, rows, rows), lambda w, h: (w, h, 0, 0)),
            pl.BlockSpec((rows, 128), lambda w, h: (w, h)),
        ],
        out_shape=[
            jax.ShapeDtypeStruct((wins, 2 * pairs, rows, rows), jnp.bfloat16),
            jax.ShapeDtypeStruct((wins * rows, feature), jnp.bfloat16),
        ],
        name="attend",
    )(mixed, mixed, mixed, table, shift, key_cells)


def attend_back(mixed, probs, grad_att, table, shift, key_cells, feature):
    rows, pairs = shift.shape[0], feature // 128
    wins = mixed.shape[0] // rows
    whole = lambda shape: pl.BlockSpec(shape, lambda w, h: (0,) * len(shape))
    column = lambda base: pl.BlockSpec((rows, 128), lambda w, h: (w, base * pairs + h))
    flat = jax.ShapeDtypeStruct((wins * rows, feature), jnp.bfloat16)
    return pl.pallas_call(
        attend_back_kernel,
        grid=(wins, pairs),
        in_specs=[
            column(0), column(1), column(2),
            pl.BlockSpec((1, 2, rows, rows), lambda w, h: (w, h, 0, 0)),
            column(0),
            whole((HD, 128)), whole((rows, 128)), whole((rows, 128)),
        ],
        out_specs=[column(0), column(0), column(0), whole((HD, 128))],
        out_shape=[flat, flat, flat, jax.ShapeDtypeStruct((HD, 128), jnp.float32)],
        name="attend_back",
    )(mixed, mixed, mixed, probs, grad_att, table, shift, key_cells)


def dot_last(left, right):
    return lax.dot_general(left, right, (((1,), (1,)), ((), ())), preferred_element_type=jnp.float32)


def dot_first(left, right):
    return lax.dot_general(left, right, (((0,), (0,)), ((), ())), preferred_element_type=jnp.float32)


def pack_kernel(
    n1_ref, dq_ref, dk_ref, dv_ref, att_ref, dproj_ref, n2_ref, dpre_ref, act_ref, dout_ref, tail_ref,
    out_ref, rows_ref, stage_ref, bias_ref, stage_sems, bias_sems,
    *, part_rows, share_rows, group_size,
):
    count = n1_ref.shape[0]
    ones = jnp.ones((16, count), jnp.bfloat16)

    def weight(base, left_ref, right_refs):
        width = sum(ref.shape[1] for ref in right_refs) // 128

        def block(f, carry):
            left = left_ref[:, pl.ds(pl.multiple_of(f * 128, 128), 128)]
            column = 0
            for ref in right_refs:
                product = dot_first(left, ref[...])
                for j in range(ref.shape[1] // 128):
                    rows_ref[pl.ds(base + f * 128 * width + column, 128, stride=width), :] = product[
                        :, j * 128 : (j + 1) * 128
                    ]
                    column += 1
            return carry

        lax.fori_loop(0, left_ref.shape[1] // 128, block, 0)
        return base + left_ref.shape[1] * width

    def bias(base, ref):
        total = jnp.dot(ones, ref[...], preferred_element_type=jnp.float32)
        for j in range(ref.shape[1] // 128):
            rows_ref[base + j : base + j + 1, :] = total[0:1, j * 128 : (j + 1) * 128]
        return base + ref.shape[1] // 128

    limit = stage_ref.shape[1]
    chunks = []
    for owner in range(group_size):
        low = 0
        while low < part_rows:
            size = min(limit, part_rows - low)
            chunks.append((owner * part_rows + low, owner * share_rows + low, size))
            low += size
    flying = {}
    sent = 0

    def emit(upto):
        nonlocal sent
        while sent < len(chunks) and chunks[sent][0] + chunks[sent][2] <= upto:
            source, target, size = chunks[sent]
            slot = sent % 2
            if slot in flying:
                flying.pop(slot).wait()
            step = next(s for s in (128, 64, 32, 16) if size % s == 0)

            def convert(i, carry, source=source, slot=slot, step=step):
                at = pl.multiple_of(i * step, step)
                stage_ref[slot, pl.ds(at, step), :] = rows_ref[
                    pl.ds(pl.multiple_of(source + at, 16), step), :
                ].astype(jnp.bfloat16)
                return carry

            lax.fori_loop(0, size // step, convert, 0)
            copy = pltpu.make_async_copy(
                stage_ref.at[slot, pl.ds(0, size), :],
                out_ref.at[pl.ds(target, size), :],
                stage_sems.at[slot],
            )
            copy.start()
            flying[slot] = copy
            sent += 1

    row = weight(0, n1_ref, [dq_ref, dk_ref, dv_ref])
    row = bias(row, dq_ref)
    row = bias(row, dv_ref)
    emit(row)
    row = weight(row, att_ref, [dproj_ref])
    proj_bias = row
    row = bias(row, dproj_ref)
    emit(row)
    bias_size = dproj_ref.shape[1] // 128
    spare = share_rows - part_rows
    bias_ref[...] = jnp.concatenate(
        [
            rows_ref[proj_bias : proj_bias + bias_size, :],
            jnp.zeros((spare - bias_size, 128), jnp.float32),
        ],
        0,
    ).astype(jnp.bfloat16)
    bias_copies = [
        pltpu.make_async_copy(
            bias_ref, out_ref.at[pl.ds(owner * share_rows + part_rows, spare), :], bias_sems.at[owner]
        )
        for owner in range(group_size)
    ]
    for copy in bias_copies:
        copy.start()
    row = weight(row, n2_ref, [dpre_ref])
    row = bias(row, dpre_ref)
    emit(row)
    row = weight(row, act_ref, [dout_ref])
    row = bias(row, dout_ref)
    emit(row)
    rows_ref[row : row + tail_ref.shape[0], :] = tail_ref[...]
    emit(group_size * part_rows)
    for slot in list(flying):
        flying.pop(slot).wait()
    for copy in bias_copies:
        copy.wait()


def pack_shares(factors, tail, part_rows, group_size, wide_size):
    feature = factors[0].shape[1]
    grain = 16 * wide_size
    share_rows = -(-(part_rows + feature // 128) // grain) * grain
    spare = share_rows - part_rows
    whole = pl.BlockSpec(memory_space=pltpu.VMEM)
    packed = pl.pallas_call(
        functools.partial(
            pack_kernel, part_rows=part_rows, share_rows=share_rows, group_size=group_size
        ),
        in_specs=[whole] * (len(factors) + 1),
        out_specs=pl.BlockSpec(memory_space=pl.ANY),
        out_shape=jax.ShapeDtypeStruct((group_size * share_rows, 128), jnp.bfloat16),
        scratch_shapes=[
            pltpu.VMEM((group_size * part_rows, 128), jnp.float32),
            pltpu.VMEM((2, 2048, 128), jnp.bfloat16),
            pltpu.VMEM((spare, 128), jnp.bfloat16),
            pltpu.SemaphoreType.DMA((2,)),
            pltpu.SemaphoreType.DMA((group_size,)),
        ],
        compiler_params=pltpu.CompilerParams(vmem_limit_bytes=60 * 1024 * 1024),
        name="pack_grads",
    )(*factors, tail)
    return packed, share_rows


def gelu_slope(pre_act):
    normal_cdf = 0.5 * (1.0 + jax.scipy.special.erf(pre_act / math.sqrt(2.0)))
    return normal_cdf + pre_act * jnp.exp(-0.5 * pre_act * pre_act) / math.sqrt(2.0 * math.pi)


def window_pass(tokens, cotangent, keep_mask, weights):
    (
        qkv_w,
        qv_b,
        proj_w,
        proj_b,
        fc1_w,
        fc1_b,
        fc2_w,
        fc2_b,
        ln1_g,
        ln1_b,
        ln2_g,
        ln2_b,
        table_h,
        table_w,
    ) = weights
    win_count, tok_count, feature = tokens.shape
    row_count = win_count * tok_count
    inputs = tokens.reshape(row_count, feature).astype(jnp.float32)
    keep_rows = keep_mask.reshape(row_count, 1)
    hat_one, scale_one = normalize(inputs)
    normed_one = (
        (hat_one * ln1_g.astype(jnp.float32) + ln1_b.astype(jnp.float32)) * keep_rows
    ).astype(jnp.bfloat16)
    bias_full = jnp.concatenate(
        [qv_b[:feature], jnp.zeros((feature,), jnp.bfloat16), qv_b[feature:]]
    ).astype(jnp.float32)
    mixed = (jnp.dot(normed_one, qkv_w, preferred_element_type=jnp.float32) + bias_full).astype(
        jnp.bfloat16
    )
    shift, key_cells = window_constants(tok_count)
    table = wide_table(table_h, table_w)
    probs, attended = attend(mixed, table, shift, key_cells, feature)
    resid = keep_rows * (
        inputs
        + jnp.dot(attended, proj_w, preferred_element_type=jnp.float32)
        + proj_b.astype(jnp.float32)
    )
    hat_two, scale_two = normalize(resid)
    normed_two = (hat_two * ln2_g.astype(jnp.float32) + ln2_b.astype(jnp.float32)).astype(
        jnp.bfloat16
    )
    pre_act = jnp.dot(normed_two, fc1_w, preferred_element_type=jnp.float32) + fc1_b.astype(
        jnp.float32
    )
    activation = jax.nn.gelu(pre_act, approximate=False).astype(jnp.bfloat16)
    result = keep_rows * (
        resid
        + jnp.dot(activation, fc2_w, preferred_element_type=jnp.float32)
        + fc2_b.astype(jnp.float32)
    )
    cot_rows = cotangent.reshape(row_count, feature).astype(jnp.float32) * keep_rows
    grad_out = cot_rows.astype(jnp.bfloat16)
    grad_act = jnp.einsum("nd,fd->nf", grad_out, fc2_w, preferred_element_type=jnp.float32)
    grad_pre = (grad_act * gelu_slope(pre_act)).astype(jnp.bfloat16)
    grad_norm_two = jnp.einsum("nf,df->nd", grad_pre, fc1_w, preferred_element_type=jnp.float32)
    grad_ln2_g = jnp.sum(grad_norm_two * hat_two, 0)
    grad_ln2_b = jnp.sum(grad_norm_two, 0)
    grad_resid = cot_rows + norm_back(grad_norm_two * ln2_g.astype(jnp.float32), hat_two, scale_two)
    grad_branch = keep_rows * grad_resid
    grad_proj = grad_branch.astype(jnp.bfloat16)
    grad_att = jnp.einsum(
        "ne,de->nd", grad_proj, proj_w, preferred_element_type=jnp.float32
    ).astype(jnp.bfloat16)
    grad_query, grad_keys, grad_values, grad_table = attend_back(
        mixed, probs, grad_att, table, shift, key_cells, feature
    )
    rel_span = table_h.shape[0]
    grad_table_h = grad_table[:, :rel_span].T[::-1]
    grad_table_w = grad_table[:, 64 : 64 + rel_span].T[::-1]
    grad_mixed = jnp.concatenate([grad_query, grad_keys, grad_values], -1)
    grad_norm_one = keep_rows * jnp.einsum(
        "nf,df->nd", grad_mixed, qkv_w, preferred_element_type=jnp.float32
    )
    grad_ln1_g = jnp.sum(grad_norm_one * hat_one, 0)
    grad_ln1_b = jnp.sum(grad_norm_one, 0)
    grad_input = grad_branch + norm_back(
        grad_norm_one * ln1_g.astype(jnp.float32), hat_one, scale_one
    )
    factors = (
        normed_one,
        grad_query,
        grad_keys,
        grad_values,
        attended,
        grad_proj,
        normed_two,
        grad_pre,
        activation,
        grad_out,
    )
    tail = (grad_ln1_g, grad_ln1_b, grad_ln2_g, grad_ln2_b, grad_table_h, grad_table_w)
    block_part = result.reshape(win_count, tok_count, feature).astype(jnp.bfloat16)
    input_part = grad_input.reshape(win_count, tok_count, feature).astype(jnp.bfloat16)
    return (block_part, input_part, factors, tail)


def swap(values, axis, bit):
    return lax.ppermute(values, axis, [(i, i ^ bit) for i in range(lax.axis_size(axis))])


def wide_bits(count):
    place = lax.axis_index("wide")
    return [(place >> bit) & 1 for bit in range(count)]


def splits(part_rows):
    return lax.axis_size("grp") == 2 and lax.axis_size("wide") % 8 == 0 and part_rows % 64 == 0


def eighth_index(core, cross, deep):
    return (core * 2 + cross) * 2 + deep


def gather_groups(mine, diagonal, finish, base):
    core, cross, deep = wide_bits(3)
    first = swap(mine, "grp", 1)
    last = swap(diagonal, "grp", 1)
    side = swap(first, "wide", 2)
    back = swap(first, "wide", 4)
    near = (first, side, back, last)
    far = [swap(part, "wide", 1) for part in near]
    group = lax.axis_index("grp")
    own = finish(first)
    out = base.reshape((2, 8) + mine.shape)
    out = lax.dynamic_update_slice(out, own.reshape((1, 8) + mine.shape), (group, 0, 0, 0))
    for parts, which in ((near, core), (far, 1 - core)):
        for part, flip_cross, flip_deep in zip(parts, (0, 1, 0, 1), (0, 0, 1, 1)):
            at = eighth_index(which, cross ^ flip_cross, deep ^ flip_deep)
            out = lax.dynamic_update_slice(out, part[None, None], (1 - group, at, 0, 0))
    return out.reshape(2 * own.shape[0], 128)


def own_eighths(rows):
    core, cross, deep = wide_bits(3)
    parts = rows.reshape(8, -1, 128)
    spots = (eighth_index(core, cross, deep), eighth_index(core, 1 - cross, 1 - deep))
    return [lax.dynamic_index_in_dim(parts, spot, keepdims=False) for spot in spots]


def first_step(grads, first_moment):
    return BETA_ONE * first_moment + (1.0 - BETA_ONE) * grads


def second_step(grads, master, moment_next, second_moment):
    second_next = BETA_TWO * second_moment + (1.0 - BETA_TWO) * grads * grads
    fix_one = 1.0 - BETA_ONE**ADAM_STEP
    fix_two = 1.0 - BETA_TWO**ADAM_STEP
    update = (
        moment_next / fix_one / (jnp.sqrt(second_next / fix_two) + ADAM_EPS) + DECAY_RATE * master
    )
    return (master - LEARN_RATE * update, second_next)


def body(tokens, cotangent, window_place, master, first_moment, second_moment):
    part_rows = master.shape[0]
    wide_size = lax.axis_size("wide")
    group_size = lax.axis_size("grp")
    feature = tokens.shape[-1]
    micro_count, slots, tok_count, _ = tokens.shape
    masks = token_mask(window_place)
    if splits(part_rows):
        mine, diagonal = (part.astype(jnp.bfloat16) for part in own_eighths(master))
        gathered = gather_groups(
            mine,
            diagonal,
            lambda first: master.astype(jnp.bfloat16),
            jnp.zeros((part_rows * group_size, 128), jnp.bfloat16),
        )
    else:
        gathered = lax.all_gather(master.astype(jnp.bfloat16), "grp", axis=0, tiled=True)
    weights = unpack(gathered, feature)
    wins = micro_count * slots
    extra = -tok_count % 16

    def padded(values):
        values = values.reshape((wins,) + values.shape[2:])
        return jnp.pad(values, ((0, 0), (0, extra)) + ((0, 0),) * (values.ndim - 2))

    block_part, input_part, factors, tail = window_pass(
        padded(tokens), padded(cotangent), padded(masks), weights
    )
    filled = sum(math.prod(dims_of) for dims_of in layout(feature)[:8]) // 128
    tail = jnp.concatenate([member.reshape(-1) for member in tail])
    tail_rows = part_rows * group_size - filled
    tail = jnp.pad(tail, (0, tail_rows * 128 - tail.shape[0])).reshape(tail_rows, 128)
    packed, share_rows = pack_shares(factors, tail, part_rows, group_size, wide_size)
    owned = lax.psum_scatter(packed, ("grp", "wide"), scatter_dimension=0, tiled=True)
    totals = lax.all_gather(owned, "wide", axis=0, tiled=True)
    factor = 1.0 / (micro_count * wide_size * group_size)
    bias_total = totals[part_rows : part_rows + feature // 128]
    proj_bias_grad = bias_total.astype(jnp.float32).reshape(-1) * factor
    totals = totals[:part_rows]

    def scaled(total_rows):
        return total_rows.astype(jnp.float32) * factor

    grads = scaled(totals)
    moment_next = first_step(grads, first_moment)
    later = []

    def finish(arrived):
        held, moment, _ = lax.optimization_barrier((totals, first_moment, arrived))
        held = scaled(held)
        later.extend(second_step(held, master, first_step(held, moment), second_moment))
        return later[0].astype(jnp.bfloat16)

    if splits(part_rows):
        mine, diagonal = (
            second_step(scaled(total), old, first_step(scaled(total), moment), second)[0].astype(
                jnp.bfloat16
            )
            for total, old, moment, second in zip(
                *(own_eighths(rows) for rows in (totals, master, first_moment, second_moment))
            )
        )
        weights_next = gather_groups(mine, diagonal, finish, gathered)
    else:
        weights_next = lax.all_gather(finish(totals), "grp", axis=0, tiled=True)
    master_next, second_next = later
    block_out = block_part[:, :tok_count].reshape(tokens.shape)
    input_grad = input_part[:, :tok_count].reshape(tokens.shape)
    return (
        block_out,
        input_grad,
        grads,
        master_next,
        moment_next,
        second_next,
        weights_next,
        proj_bias_grad,
    )


def solution(mesh):
    return jax.shard_map(
        body,
        mesh=mesh,
        in_specs=(
            P(None, ("wide", "grp"), None, None),
            P(None, ("wide", "grp"), None, None),
            P(None, ("wide", "grp")),
            P("grp", None),
            P("grp", None),
            P("grp", None),
        ),
        out_specs=(
            P(None, ("wide", "grp"), None, None),
            P(None, ("wide", "grp"), None, None),
            P("grp", None),
            P("grp", None),
            P("grp", None),
            P("grp", None),
            P(),
            P(),
        ),
        check_vma=False,
    )
```

```python
import functools
import math

import jax
import jax.numpy as jnp
from jax import lax
from jax.experimental import pallas as pl
from jax.experimental.pallas import tpu as pltpu
from jax.sharding import PartitionSpec as P

FF = 3072
HD = 64
WS = 14
GRID = 64
ADAM_STEP = 10


EPS_NORM = 1e-06
BETA_ONE = 0.9
BETA_TWO = 0.95
ADAM_EPS = 1e-08
LEARN_RATE = 0.02
DECAY_RATE = 0.1


def layout(feature):
    rel_span = 2 * WS - 1
    return [
        (feature, 3 * feature),
        (2 * feature,),
        (feature, feature),
        (feature,),
        (feature, FF),
        (FF,),
        (FF, feature),
        (feature,),
        (feature,),
        (feature,),
        (feature,),
        (feature,),
        (rel_span, HD),
        (rel_span, HD),
    ]


def unpack(rows, feature):
    members = []
    row = 0
    dims = layout(feature)
    for dims_of in dims[:8]:
        length = math.prod(dims_of) // 128
        members.append(rows[row : row + length].reshape(dims_of))
        row = row + length
    tail_size = sum(math.prod(dims_of) for dims_of in dims[8:])
    tail = rows[row : row - (-tail_size // 128)].reshape(-1)
    offset = 0
    for dims_of in dims[8:]:
        length = math.prod(dims_of)
        members.append(tail[offset : offset + length].reshape(dims_of))
        offset = offset + length
    return tuple(members)


def token_mask(window_place):
    cells = jnp.arange(WS * WS, dtype=jnp.int32)
    inner_row = cells // WS
    inner_col = cells % WS
    places = window_place[..., None]
    live_slot = places < 25
    row_real = WS * (places // 5) + inner_row < GRID
    col_real = WS * (places % 5) + inner_col < GRID
    return jnp.where(live_slot & row_real & col_real, 1.0, 0.0).astype(jnp.float32)


def normalize(inputs):
    row_mean = jnp.mean(inputs, -1, keepdims=True)
    centred = inputs - row_mean
    inv_scale = lax.rsqrt(jnp.mean(centred * centred, -1, keepdims=True) + EPS_NORM)
    return (centred * inv_scale, inv_scale)


def norm_back(grad_hat, normed_hat, inv_scale):
    first_mean = jnp.mean(grad_hat, -1, keepdims=True)
    second_mean = jnp.mean(grad_hat * normed_hat, -1, keepdims=True)
    return inv_scale * (grad_hat - first_mean - normed_hat * second_mean)


def attend_kernel(q_ref, k_ref, v_ref, table_ref, shift_ref, key_ref, probs_ref, out_ref):
    shift = shift_ref[...]
    key_cells = key_ref[...]
    row_count = shift.shape[0]
    real_key = lax.broadcasted_iota(jnp.int32, (row_count, row_count), 1) < WS * WS
    for part in range(2):
        cut = slice(part * HD, (part + 1) * HD)
        queries = q_ref[:, cut]
        along = jnp.dot(queries, table_ref[...], preferred_element_type=jnp.float32)
        for bit in (1, 2, 4, 8):
            along = jnp.where((shift & bit) != 0, pltpu.roll(along, 128 - bit, 1), along)
        high = along.astype(jnp.bfloat16)
        low = (along - high.astype(jnp.float32)).astype(jnp.bfloat16)
        scores = dot_last(queries, k_ref[:, cut]) * (1.0 / math.sqrt(HD))
        scores = scores + dot_last(high, key_cells) + dot_last(low, key_cells)
        scores = jnp.where(real_key, scores, -1e30)
        powers = jnp.exp(scores - jnp.max(scores, -1, keepdims=True))
        probs = (powers / jnp.sum(powers, -1, keepdims=True)).astype(jnp.bfloat16)
        probs_ref[0, part] = probs
        out_ref[:, cut] = jnp.dot(
            probs, v_ref[:, cut], preferred_element_type=jnp.float32
        ).astype(jnp.bfloat16)


def attend_back_kernel(
    q_ref, k_ref, v_ref, probs_ref, grad_ref, table_ref, shift_ref, key_ref,
    dq_ref, dk_ref, dv_ref, dtable_ref,
):
    shift = shift_ref[...]
    key_cells = key_ref[...]
    scale = 1.0 / math.sqrt(HD)

    @pl.when((pl.program_id(0) == 0) & (pl.program_id(1) == 0))
    def _():
        dtable_ref[...] = jnp.zeros(dtable_ref.shape, jnp.float32)

    for part in range(2):
        cut = slice(part * HD, (part + 1) * HD)
        queries = q_ref[:, cut]
        grad = grad_ref[:, cut]
        probs = probs_ref[0, part]
        dv_ref[:, cut] = dot_first(probs, grad).astype(jnp.bfloat16)
        grad_probs = dot_last(grad, v_ref[:, cut])
        wide_probs = probs.astype(jnp.float32)
        inner = jnp.sum(wide_probs * grad_probs, -1, keepdims=True)
        grad_scores = (wide_probs * (grad_probs - inner)).astype(jnp.bfloat16)
        dk_ref[:, cut] = (dot_first(grad_scores, queries) * scale).astype(jnp.bfloat16)
        along = jnp.dot(grad_scores, key_cells, preferred_element_type=jnp.float32)
        for bit in (1, 2, 4, 8):
            along = jnp.where((shift & bit) != 0, pltpu.roll(along, bit, 1), along)
        high = along.astype(jnp.bfloat16)
        low = (along - high.astype(jnp.float32)).astype(jnp.bfloat16)
        grad_query = jnp.dot(grad_scores, k_ref[:, cut], preferred_element_type=jnp.float32) * scale
        grad_query = grad_query + dot_last(high, table_ref[...]) + dot_last(low, table_ref[...])
        dq_ref[:, cut] = grad_query.astype(jnp.bfloat16)
        dtable_ref[...] += dot_first(queries, high) + dot_first(queries, low)


def window_constants(row_count):
    cells = jnp.arange(row_count, dtype=jnp.int32)[:, None]
    lanes = jnp.arange(128, dtype=jnp.int32)[None, :]
    first = lanes < 64
    shift = jnp.where(first, WS - 1 - cells // WS, WS - 1 - cells % WS)
    live = cells < WS * WS
    shift = jnp.where(live, shift, 0)
    offset = jnp.where(first, lanes, lanes - 64)
    place = jnp.where(first, cells // WS, cells % WS)
    key_cells = jnp.where(live & (offset == place), 1.0, 0.0).astype(jnp.bfloat16)
    return shift, key_cells


def wide_table(table_h, table_w):
    pad = jnp.zeros((HD, 64 - table_h.shape[0]), table_h.dtype)
    return jnp.concatenate([table_h[::-1].T, pad, table_w[::-1].T, pad], 1)


def attend(mixed, table, shift, key_cells, feature):
    rows, pairs = shift.shape[0], feature // 128
    wins = mixed.shape[0] // rows
    whole = lambda shape: pl.BlockSpec(shape, lambda w, h: (0,) * len(shape))
    column = lambda base: pl.BlockSpec((rows, 128), lambda w, h: (w, base * pairs + h))
    return pl.pallas_call(
        attend_kernel,
        grid=(wins, pairs),
        in_specs=[column(0), column(1), column(2), whole((HD, 128)), whole((rows, 128)), whole((rows, 128))],
        out_specs=[
            pl.BlockSpec((1, 2, rows, rows), lambda w, h: (w, h, 0, 0)),
            pl.BlockSpec((rows, 128), lambda w, h: (w, h)),
        ],
        out_shape=[
            jax.ShapeDtypeStruct((wins, 2 * pairs, rows, rows), jnp.bfloat16),
            jax.ShapeDtypeStruct((wins * rows, feature), jnp.bfloat16),
        ],
        name="attend",
    )(mixed, mixed, mixed, table, shift, key_cells)


def attend_back(mixed, probs, grad_att, table, shift, key_cells, feature):
    rows, pairs = shift.shape[0], feature // 128
    wins = mixed.shape[0] // rows
    whole = lambda shape: pl.BlockSpec(shape, lambda w, h: (0,) * len(shape))
    column = lambda base: pl.BlockSpec((rows, 128), lambda w, h: (w, base * pairs + h))
    flat = jax.ShapeDtypeStruct((wins * rows, feature), jnp.bfloat16)
    return pl.pallas_call(
        attend_back_kernel,
        grid=(wins, pairs),
        in_specs=[
            column(0), column(1), column(2),
            pl.BlockSpec((1, 2, rows, rows), lambda w, h: (w, h, 0, 0)),
            column(0),
            whole((HD, 128)), whole((rows, 128)), whole((rows, 128)),
        ],
        out_specs=[column(0), column(0), column(0), whole((HD, 128))],
        out_shape=[flat, flat, flat, jax.ShapeDtypeStruct((HD, 128), jnp.float32)],
        name="attend_back",
    )(mixed, mixed, mixed, probs, grad_att, table, shift, key_cells)


def dot_last(left, right):
    return lax.dot_general(left, right, (((1,), (1,)), ((), ())), preferred_element_type=jnp.float32)


def dot_first(left, right):
    return lax.dot_general(left, right, (((0,), (0,)), ((), ())), preferred_element_type=jnp.float32)


def pack_kernel(
    n1_ref, dq_ref, dk_ref, dv_ref, att_ref, dproj_ref, n2_ref, dpre_ref, act_ref, dout_ref, tail_ref,
    out_ref, rows_ref, stage_ref, bias_ref, stage_sems, bias_sems,
    *, part_rows, share_rows, group_size,
):
    count = n1_ref.shape[0]
    ones = jnp.ones((16, count), jnp.bfloat16)

    def weight(base, left_ref, right_refs):
        width = sum(ref.shape[1] for ref in right_refs) // 128

        def block(f, carry):
            left = left_ref[:, pl.ds(pl.multiple_of(f * 128, 128), 128)]
            column = 0
            for ref in right_refs:
                product = dot_first(left, ref[...])
                for j in range(ref.shape[1] // 128):
                    rows_ref[pl.ds(base + f * 128 * width + column, 128, stride=width), :] = product[
                        :, j * 128 : (j + 1) * 128
                    ]
                    column += 1
            return carry

        lax.fori_loop(0, left_ref.shape[1] // 128, block, 0)
        return base + left_ref.shape[1] * width

    def bias(base, ref):
        total = jnp.dot(ones, ref[...], preferred_element_type=jnp.float32)
        for j in range(ref.shape[1] // 128):
            rows_ref[base + j : base + j + 1, :] = total[0:1, j * 128 : (j + 1) * 128]
        return base + ref.shape[1] // 128

    limit = stage_ref.shape[1]
    chunks = []
    for owner in range(group_size):
        low = 0
        while low < part_rows:
            size = min(limit, part_rows - low)
            chunks.append((owner * part_rows + low, owner * share_rows + low, size))
            low += size
    flying = {}
    sent = 0

    def emit(upto):
        nonlocal sent
        while sent < len(chunks) and chunks[sent][0] + chunks[sent][2] <= upto:
            source, target, size = chunks[sent]
            slot = sent % 2
            if slot in flying:
                flying.pop(slot).wait()
            step = next(s for s in (128, 64, 32, 16) if size % s == 0)

            def convert(i, carry, source=source, slot=slot, step=step):
                at = pl.multiple_of(i * step, step)
                stage_ref[slot, pl.ds(at, step), :] = rows_ref[
                    pl.ds(pl.multiple_of(source + at, 16), step), :
                ].astype(jnp.bfloat16)
                return carry

            lax.fori_loop(0, size // step, convert, 0)
            copy = pltpu.make_async_copy(
                stage_ref.at[slot, pl.ds(0, size), :],
                out_ref.at[pl.ds(target, size), :],
                stage_sems.at[slot],
            )
            copy.start()
            flying[slot] = copy
            sent += 1

    row = weight(0, n1_ref, [dq_ref, dk_ref, dv_ref])
    row = bias(row, dq_ref)
    row = bias(row, dv_ref)
    emit(row)
    row = weight(row, att_ref, [dproj_ref])
    proj_bias = row
    row = bias(row, dproj_ref)
    emit(row)
    bias_size = dproj_ref.shape[1] // 128
    spare = share_rows - part_rows
    bias_ref[...] = jnp.concatenate(
        [
            rows_ref[proj_bias : proj_bias + bias_size, :],
            jnp.zeros((spare - bias_size, 128), jnp.float32),
        ],
        0,
    ).astype(jnp.bfloat16)
    bias_copies = [
        pltpu.make_async_copy(
            bias_ref, out_ref.at[pl.ds(owner * share_rows + part_rows, spare), :], bias_sems.at[owner]
        )
        for owner in range(group_size)
    ]
    for copy in bias_copies:
        copy.start()
    row = weight(row, n2_ref, [dpre_ref])
    row = bias(row, dpre_ref)
    emit(row)
    row = weight(row, act_ref, [dout_ref])
    row = bias(row, dout_ref)
    emit(row)
    rows_ref[row : row + tail_ref.shape[0], :] = tail_ref[...]
    emit(group_size * part_rows)
    for slot in list(flying):
        flying.pop(slot).wait()
    for copy in bias_copies:
        copy.wait()


def pack_shares(factors, tail, part_rows, group_size, wide_size):
    feature = factors[0].shape[1]
    grain = 16 * wide_size
    share_rows = -(-(part_rows + feature // 128) // grain) * grain
    spare = share_rows - part_rows
    whole = pl.BlockSpec(memory_space=pltpu.VMEM)
    packed = pl.pallas_call(
        functools.partial(
            pack_kernel, part_rows=part_rows, share_rows=share_rows, group_size=group_size
        ),
        in_specs=[whole] * (len(factors) + 1),
        out_specs=pl.BlockSpec(memory_space=pl.ANY),
        out_shape=jax.ShapeDtypeStruct((group_size * share_rows, 128), jnp.bfloat16),
        scratch_shapes=[
            pltpu.VMEM((group_size * part_rows, 128), jnp.float32),
            pltpu.VMEM((2, 2048, 128), jnp.bfloat16),
            pltpu.VMEM((spare, 128), jnp.bfloat16),
            pltpu.SemaphoreType.DMA((2,)),
            pltpu.SemaphoreType.DMA((group_size,)),
        ],
        compiler_params=pltpu.CompilerParams(vmem_limit_bytes=60 * 1024 * 1024),
        name="pack_grads",
    )(*factors, tail)
    return packed, share_rows


def gelu_slope(pre_act):
    normal_cdf = 0.5 * (1.0 + jax.scipy.special.erf(pre_act / math.sqrt(2.0)))
    return normal_cdf + pre_act * jnp.exp(-0.5 * pre_act * pre_act) / math.sqrt(2.0 * math.pi)


def window_pass(tokens, cotangent, keep_mask, weights):
    (
        qkv_w,
        qv_b,
        proj_w,
        proj_b,
        fc1_w,
        fc1_b,
        fc2_w,
        fc2_b,
        ln1_g,
        ln1_b,
        ln2_g,
        ln2_b,
        table_h,
        table_w,
    ) = weights
    win_count, tok_count, feature = tokens.shape
    row_count = win_count * tok_count
    inputs = tokens.reshape(row_count, feature).astype(jnp.float32)
    keep_rows = keep_mask.reshape(row_count, 1)
    hat_one, scale_one = normalize(inputs)
    normed_one = (
        (hat_one * ln1_g.astype(jnp.float32) + ln1_b.astype(jnp.float32)) * keep_rows
    ).astype(jnp.bfloat16)
    bias_full = jnp.concatenate(
        [qv_b[:feature], jnp.zeros((feature,), jnp.bfloat16), qv_b[feature:]]
    ).astype(jnp.float32)
    mixed = (jnp.dot(normed_one, qkv_w, preferred_element_type=jnp.float32) + bias_full).astype(
        jnp.bfloat16
    )
    shift, key_cells = window_constants(tok_count)
    table = wide_table(table_h, table_w)
    probs, attended = attend(mixed, table, shift, key_cells, feature)
    resid = keep_rows * (
        inputs
        + jnp.dot(attended, proj_w, preferred_element_type=jnp.float32)
        + proj_b.astype(jnp.float32)
    )
    hat_two, scale_two = normalize(resid)
    normed_two = (hat_two * ln2_g.astype(jnp.float32) + ln2_b.astype(jnp.float32)).astype(
        jnp.bfloat16
    )
    pre_act = jnp.dot(normed_two, fc1_w, preferred_element_type=jnp.float32) + fc1_b.astype(
        jnp.float32
    )
    activation = jax.nn.gelu(pre_act, approximate=False).astype(jnp.bfloat16)
    result = keep_rows * (
        resid
        + jnp.dot(activation, fc2_w, preferred_element_type=jnp.float32)
        + fc2_b.astype(jnp.float32)
    )
    cot_rows = cotangent.reshape(row_count, feature).astype(jnp.float32) * keep_rows
    grad_out = cot_rows.astype(jnp.bfloat16)
    grad_act = jnp.einsum("nd,fd->nf", grad_out, fc2_w, preferred_element_type=jnp.float32)
    grad_pre = (grad_act * gelu_slope(pre_act)).astype(jnp.bfloat16)
    grad_norm_two = jnp.einsum("nf,df->nd", grad_pre, fc1_w, preferred_element_type=jnp.float32)
    grad_ln2_g = jnp.sum(grad_norm_two * hat_two, 0)
    grad_ln2_b = jnp.sum(grad_norm_two, 0)
    grad_resid = cot_rows + norm_back(grad_norm_two * ln2_g.astype(jnp.float32), hat_two, scale_two)
    grad_branch = keep_rows * grad_resid
    grad_proj = grad_branch.astype(jnp.bfloat16)
    grad_att = jnp.einsum(
        "ne,de->nd", grad_proj, proj_w, preferred_element_type=jnp.float32
    ).astype(jnp.bfloat16)
    grad_query, grad_keys, grad_values, grad_table = attend_back(
        mixed, probs, grad_att, table, shift, key_cells, feature
    )
    rel_span = table_h.shape[0]
    grad_table_h = grad_table[:, :rel_span].T[::-1]
    grad_table_w = grad_table[:, 64 : 64 + rel_span].T[::-1]
    grad_mixed = jnp.concatenate([grad_query, grad_keys, grad_values], -1)
    grad_norm_one = keep_rows * jnp.einsum(
        "nf,df->nd", grad_mixed, qkv_w, preferred_element_type=jnp.float32
    )
    grad_ln1_g = jnp.sum(grad_norm_one * hat_one, 0)
    grad_ln1_b = jnp.sum(grad_norm_one, 0)
    grad_input = grad_branch + norm_back(
        grad_norm_one * ln1_g.astype(jnp.float32), hat_one, scale_one
    )
    factors = (
        normed_one,
        grad_query,
        grad_keys,
        grad_values,
        attended,
        grad_proj,
        normed_two,
        grad_pre,
        activation,
        grad_out,
    )
    tail = (grad_ln1_g, grad_ln1_b, grad_ln2_g, grad_ln2_b, grad_table_h, grad_table_w)
    block_part = result.reshape(win_count, tok_count, feature).astype(jnp.bfloat16)
    input_part = grad_input.reshape(win_count, tok_count, feature).astype(jnp.bfloat16)
    return (block_part, input_part, factors, tail)


def swap(values, axis, bit):
    return lax.ppermute(values, axis, [(i, i ^ bit) for i in range(lax.axis_size(axis))])


def wide_bits(count):
    place = lax.axis_index("wide")
    return [(place >> bit) & 1 for bit in range(count)]


def splits(part_rows):
    return lax.axis_size("grp") == 2 and lax.axis_size("wide") % 8 == 0 and part_rows % 64 == 0


def eighth_index(core, cross, deep):
    return (core * 2 + cross) * 2 + deep


def gather_groups(mine, diagonal, finish, base):
    core, cross, deep = wide_bits(3)
    first = swap(mine, "grp", 1)
    last = swap(diagonal, "grp", 1)
    side = swap(first, "wide", 2)
    back = swap(first, "wide", 4)
    near = (first, side, back, last)
    far = [swap(part, "wide", 1) for part in near]
    group = lax.axis_index("grp")
    own = finish(first)
    out = base.reshape((2, 8) + mine.shape)
    out = lax.dynamic_update_slice(out, own.reshape((1, 8) + mine.shape), (group, 0, 0, 0))
    for parts, which in ((near, core), (far, 1 - core)):
        for part, flip_cross, flip_deep in zip(parts, (0, 1, 0, 1), (0, 0, 1, 1)):
            at = eighth_index(which, cross ^ flip_cross, deep ^ flip_deep)
            out = lax.dynamic_update_slice(out, part[None, None], (1 - group, at, 0, 0))
    return out.reshape(2 * own.shape[0], 128)


def halve(values, names, name, exchange, bit):
    axis = names.index(name)
    sent = exchange(lax.dynamic_index_in_dim(values, 1 - bit, axis, keepdims=False))
    kept = lax.dynamic_index_in_dim(values, bit, axis, keepdims=False)
    total = (kept.astype(jnp.float32) + sent.astype(jnp.float32)).astype(values.dtype)
    return total, [other for other in names if other != name]


def reduce_shares(packed):
    wide_size = lax.axis_size("wide")
    group_size = lax.axis_size("grp")
    if (wide_size, group_size) != (16, 2):
        return lax.psum_scatter(packed, ("grp", "wide"), scatter_dimension=0, tiled=True)
    share = packed.shape[0] // 32
    core, cross, deep, far = wide_bits(4)
    moves = {
        "core": (lambda v: swap(v, "wide", 1), core),
        "x": (lambda v: swap(v, "wide", 2), cross),
        "near": (lambda v: swap(v, "wide", 4), deep),
        "far": (lambda v: swap(v, "wide", 8), far),
        "y": (lambda v: swap(v, "grp", 1), lax.axis_index("grp")),
    }
    blocks = packed.reshape(2, 2, 2, 2, 2, share, 128)
    units = share // 16
    cuts = [0, (units + 2) // 3 * 16, ((units + 2) // 3 + (units + 1) // 3) * 16, share]
    orders = (("y", "x", "near"), ("x", "near", "y"), ("near", "y", "x"))
    done = []
    for low, high, order in zip(cuts, cuts[1:], orders):
        part = blocks[..., low:high, :]
        names = ["y", "far", "near", "x", "core"]
        for name in ("core",) + order + ("far",):
            part, names = halve(part, names, name, *moves[name])
        done.append(part)
    return jnp.concatenate(done, 0)


def own_eighths(rows):
    core, cross, deep = wide_bits(3)
    parts = rows.reshape(8, -1, 128)
    spots = (eighth_index(core, cross, deep), eighth_index(core, 1 - cross, 1 - deep))
    return [lax.dynamic_index_in_dim(parts, spot, keepdims=False) for spot in spots]


def first_step(grads, first_moment):
    return BETA_ONE * first_moment + (1.0 - BETA_ONE) * grads


def second_step(grads, master, moment_next, second_moment):
    second_next = BETA_TWO * second_moment + (1.0 - BETA_TWO) * grads * grads
    fix_one = 1.0 - BETA_ONE**ADAM_STEP
    fix_two = 1.0 - BETA_TWO**ADAM_STEP
    update = (
        moment_next / fix_one / (jnp.sqrt(second_next / fix_two) + ADAM_EPS) + DECAY_RATE * master
    )
    return (master - LEARN_RATE * update, second_next)


def body(tokens, cotangent, window_place, master, first_moment, second_moment):
    part_rows = master.shape[0]
    wide_size = lax.axis_size("wide")
    group_size = lax.axis_size("grp")
    feature = tokens.shape[-1]
    micro_count, slots, tok_count, _ = tokens.shape
    masks = token_mask(window_place)
    if splits(part_rows):
        mine, diagonal = (part.astype(jnp.bfloat16) for part in own_eighths(master))
        gathered = gather_groups(
            mine,
            diagonal,
            lambda first: master.astype(jnp.bfloat16),
            jnp.zeros((part_rows * group_size, 128), jnp.bfloat16),
        )
    else:
        gathered = lax.all_gather(master.astype(jnp.bfloat16), "grp", axis=0, tiled=True)
    weights = unpack(gathered, feature)
    wins = micro_count * slots
    extra = -tok_count % 16

    def padded(values):
        values = values.reshape((wins,) + values.shape[2:])
        return jnp.pad(values, ((0, 0), (0, extra)) + ((0, 0),) * (values.ndim - 2))

    block_part, input_part, factors, tail = window_pass(
        padded(tokens), padded(cotangent), padded(masks), weights
    )
    filled = sum(math.prod(dims_of) for dims_of in layout(feature)[:8]) // 128
    tail = jnp.concatenate([member.reshape(-1) for member in tail])
    tail_rows = part_rows * group_size - filled
    tail = jnp.pad(tail, (0, tail_rows * 128 - tail.shape[0])).reshape(tail_rows, 128)
    packed, _ = pack_shares(factors, tail, part_rows, group_size, wide_size)
    owned = reduce_shares(packed)
    totals = lax.all_gather(owned, "wide", axis=0, tiled=True)
    factor = 1.0 / (micro_count * wide_size * group_size)
    bias_total = totals[part_rows : part_rows + feature // 128]
    proj_bias_grad = bias_total.astype(jnp.float32).reshape(-1) * factor
    totals = totals[:part_rows]

    def scaled(total_rows):
        return total_rows.astype(jnp.float32) * factor

    grads = scaled(totals)
    moment_next = first_step(grads, first_moment)
    later = []

    def finish(arrived):
        held, moment, _ = lax.optimization_barrier((totals, first_moment, arrived))
        held = scaled(held)
        later.extend(second_step(held, master, first_step(held, moment), second_moment))
        return later[0].astype(jnp.bfloat16)

    if splits(part_rows):
        mine, diagonal = (
            second_step(scaled(total), old, first_step(scaled(total), moment), second)[0].astype(
                jnp.bfloat16
            )
            for total, old, moment, second in zip(
                *(own_eighths(rows) for rows in (totals, master, first_moment, second_moment))
            )
        )
        weights_next = gather_groups(mine, diagonal, finish, gathered)
    else:
        weights_next = lax.all_gather(finish(totals), "grp", axis=0, tiled=True)
    master_next, second_next = later
    block_out = block_part[:, :tok_count].reshape(tokens.shape)
    input_grad = input_part[:, :tok_count].reshape(tokens.shape)
    return (
        block_out,
        input_grad,
        grads,
        master_next,
        moment_next,
        second_next,
        weights_next,
        proj_bias_grad,
    )


def solution(mesh):
    return jax.shard_map(
        body,
        mesh=mesh,
        in_specs=(
            P(None, ("wide", "grp"), None, None),
            P(None, ("wide", "grp"), None, None),
            P(None, ("wide", "grp")),
            P("grp", None),
            P("grp", None),
            P("grp", None),
        ),
        out_specs=(
            P(None, ("wide", "grp"), None, None),
            P(None, ("wide", "grp"), None, None),
            P("grp", None),
            P("grp", None),
            P("grp", None),
            P("grp", None),
            P(),
            P(),
        ),
        check_vma=False,
    )
```

```python
import functools
import math

import jax
import jax.numpy as jnp
from jax import lax
from jax.experimental import pallas as pl
from jax.experimental.pallas import tpu as pltpu
from jax.sharding import PartitionSpec as P

FF = 3072
HD = 64
WS = 14
GRID = 64
ADAM_STEP = 10


EPS_NORM = 1e-06
BETA_ONE = 0.9
BETA_TWO = 0.95
ADAM_EPS = 1e-08
LEARN_RATE = 0.02
DECAY_RATE = 0.1


def layout(feature):
    rel_span = 2 * WS - 1
    return [
        (feature, 3 * feature),
        (2 * feature,),
        (feature, feature),
        (feature,),
        (feature, FF),
        (FF,),
        (FF, feature),
        (feature,),
        (feature,),
        (feature,),
        (feature,),
        (feature,),
        (rel_span, HD),
        (rel_span, HD),
    ]


def unpack(rows, feature):
    members = []
    row = 0
    dims = layout(feature)
    for dims_of in dims[:8]:
        length = math.prod(dims_of) // 128
        members.append(rows[row : row + length].reshape(dims_of))
        row = row + length
    tail_size = sum(math.prod(dims_of) for dims_of in dims[8:])
    tail = rows[row : row - (-tail_size // 128)].reshape(-1)
    offset = 0
    for dims_of in dims[8:]:
        length = math.prod(dims_of)
        members.append(tail[offset : offset + length].reshape(dims_of))
        offset = offset + length
    return tuple(members)


def token_mask(window_place):
    cells = jnp.arange(WS * WS, dtype=jnp.int32)
    inner_row = cells // WS
    inner_col = cells % WS
    places = window_place[..., None]
    live_slot = places < 25
    row_real = WS * (places // 5) + inner_row < GRID
    col_real = WS * (places % 5) + inner_col < GRID
    return jnp.where(live_slot & row_real & col_real, 1.0, 0.0).astype(jnp.float32)


def normalize(inputs):
    row_mean = jnp.mean(inputs, -1, keepdims=True)
    centred = inputs - row_mean
    inv_scale = lax.rsqrt(jnp.mean(centred * centred, -1, keepdims=True) + EPS_NORM)
    return (centred * inv_scale, inv_scale)


def norm_back(grad_hat, normed_hat, inv_scale):
    first_mean = jnp.mean(grad_hat, -1, keepdims=True)
    second_mean = jnp.mean(grad_hat * normed_hat, -1, keepdims=True)
    return inv_scale * (grad_hat - first_mean - normed_hat * second_mean)


def attend_kernel(q_ref, k_ref, v_ref, table_ref, shift_ref, key_ref, probs_ref, out_ref):
    shift = shift_ref[...]
    key_cells = key_ref[...]
    row_count = shift.shape[0]
    real_key = lax.broadcasted_iota(jnp.int32, (row_count, row_count), 1) < WS * WS
    for part in range(2):
        cut = slice(part * HD, (part + 1) * HD)
        queries = q_ref[:, cut]
        along = jnp.dot(queries, table_ref[...], preferred_element_type=jnp.float32)
        for bit in (1, 2, 4, 8):
            along = jnp.where((shift & bit) != 0, pltpu.roll(along, 128 - bit, 1), along)
        high = along.astype(jnp.bfloat16)
        low = (along - high.astype(jnp.float32)).astype(jnp.bfloat16)
        scores = dot_last(queries, k_ref[:, cut]) * (1.0 / math.sqrt(HD))
        scores = scores + dot_last(high, key_cells) + dot_last(low, key_cells)
        scores = jnp.where(real_key, scores, -1e30)
        powers = jnp.exp(scores - jnp.max(scores, -1, keepdims=True))
        probs = (powers / jnp.sum(powers, -1, keepdims=True)).astype(jnp.bfloat16)
        probs_ref[0, part] = probs
        out_ref[:, cut] = jnp.dot(
            probs, v_ref[:, cut], preferred_element_type=jnp.float32
        ).astype(jnp.bfloat16)


def attend_back_kernel(
    q_ref, k_ref, v_ref, probs_ref, grad_ref, table_ref, shift_ref, key_ref,
    dq_ref, dk_ref, dv_ref, dtable_ref,
):
    shift = shift_ref[...]
    key_cells = key_ref[...]
    scale = 1.0 / math.sqrt(HD)

    @pl.when((pl.program_id(0) == 0) & (pl.program_id(1) == 0))
    def _():
        dtable_ref[...] = jnp.zeros(dtable_ref.shape, jnp.float32)

    for part in range(2):
        cut = slice(part * HD, (part + 1) * HD)
        queries = q_ref[:, cut]
        grad = grad_ref[:, cut]
        probs = probs_ref[0, part]
        dv_ref[:, cut] = dot_first(probs, grad).astype(jnp.bfloat16)
        grad_probs = dot_last(grad, v_ref[:, cut])
        wide_probs = probs.astype(jnp.float32)
        inner = jnp.sum(wide_probs * grad_probs, -1, keepdims=True)
        grad_scores = (wide_probs * (grad_probs - inner)).astype(jnp.bfloat16)
        dk_ref[:, cut] = (dot_first(grad_scores, queries) * scale).astype(jnp.bfloat16)
        along = jnp.dot(grad_scores, key_cells, preferred_element_type=jnp.float32)
        for bit in (1, 2, 4, 8):
            along = jnp.where((shift & bit) != 0, pltpu.roll(along, bit, 1), along)
        high = along.astype(jnp.bfloat16)
        low = (along - high.astype(jnp.float32)).astype(jnp.bfloat16)
        grad_query = jnp.dot(grad_scores, k_ref[:, cut], preferred_element_type=jnp.float32) * scale
        grad_query = grad_query + dot_last(high, table_ref[...]) + dot_last(low, table_ref[...])
        dq_ref[:, cut] = grad_query.astype(jnp.bfloat16)
        dtable_ref[...] += dot_first(queries, high) + dot_first(queries, low)


def window_constants(row_count):
    cells = jnp.arange(row_count, dtype=jnp.int32)[:, None]
    lanes = jnp.arange(128, dtype=jnp.int32)[None, :]
    first = lanes < 64
    shift = jnp.where(first, WS - 1 - cells // WS, WS - 1 - cells % WS)
    live = cells < WS * WS
    shift = jnp.where(live, shift, 0)
    offset = jnp.where(first, lanes, lanes - 64)
    place = jnp.where(first, cells // WS, cells % WS)
    key_cells = jnp.where(live & (offset == place), 1.0, 0.0).astype(jnp.bfloat16)
    return shift, key_cells


def wide_table(table_h, table_w):
    pad = jnp.zeros((HD, 64 - table_h.shape[0]), table_h.dtype)
    return jnp.concatenate([table_h[::-1].T, pad, table_w[::-1].T, pad], 1)


def attend(mixed, table, shift, key_cells, feature):
    rows, pairs = shift.shape[0], feature // 128
    wins = mixed.shape[0] // rows
    whole = lambda shape: pl.BlockSpec(shape, lambda w, h: (0,) * len(shape))
    column = lambda base: pl.BlockSpec((rows, 128), lambda w, h: (w, base * pairs + h))
    return pl.pallas_call(
        attend_kernel,
        grid=(wins, pairs),
        in_specs=[column(0), column(1), column(2), whole((HD, 128)), whole((rows, 128)), whole((rows, 128))],
        out_specs=[
            pl.BlockSpec((1, 2, rows, rows), lambda w, h: (w, h, 0, 0)),
            pl.BlockSpec((rows, 128), lambda w, h: (w, h)),
        ],
        out_shape=[
            jax.ShapeDtypeStruct((wins, 2 * pairs, rows, rows), jnp.bfloat16),
            jax.ShapeDtypeStruct((wins * rows, feature), jnp.bfloat16),
        ],
        name="attend",
    )(mixed, mixed, mixed, table, shift, key_cells)


def attend_back(mixed, probs, grad_att, table, shift, key_cells, feature):
    rows, pairs = shift.shape[0], feature // 128
    wins = mixed.shape[0] // rows
    whole = lambda shape: pl.BlockSpec(shape, lambda w, h: (0,) * len(shape))
    column = lambda base: pl.BlockSpec((rows, 128), lambda w, h: (w, base * pairs + h))
    flat = jax.ShapeDtypeStruct((wins * rows, feature), jnp.bfloat16)
    return pl.pallas_call(
        attend_back_kernel,
        grid=(wins, pairs),
        in_specs=[
            column(0), column(1), column(2),
            pl.BlockSpec((1, 2, rows, rows), lambda w, h: (w, h, 0, 0)),
            column(0),
            whole((HD, 128)), whole((rows, 128)), whole((rows, 128)),
        ],
        out_specs=[column(0), column(0), column(0), whole((HD, 128))],
        out_shape=[flat, flat, flat, jax.ShapeDtypeStruct((HD, 128), jnp.float32)],
        name="attend_back",
    )(mixed, mixed, mixed, probs, grad_att, table, shift, key_cells)


def dot_last(left, right):
    return lax.dot_general(left, right, (((1,), (1,)), ((), ())), preferred_element_type=jnp.float32)


def dot_first(left, right):
    return lax.dot_general(left, right, (((0,), (0,)), ((), ())), preferred_element_type=jnp.float32)


ORDERS = (("y", "x", "near"), ("x", "near", "y"), ("near", "y", "x"))


def halves(wide_size, group_size):
    return (wide_size, group_size) == (16, 2)


def pack_kernel(
    n1_ref, dq_ref, dk_ref, dv_ref, att_ref, dproj_ref, n2_ref, dpre_ref, act_ref, dout_ref, tail_ref,
    *refs, part_rows, share_rows, group_size, wide_size, cuts, relative,
):
    *out_refs, rows_ref, stage_ref, bias_ref, stage_sems = refs
    kept_refs, sent_refs = out_refs[: len(cuts)], out_refs[len(cuts) :]
    count = n1_ref.shape[0]
    ones = jnp.ones((16, count), jnp.bfloat16)

    def weight(base, left_ref, right_refs):
        width = sum(ref.shape[1] for ref in right_refs) // 128

        def block(f, carry):
            left = left_ref[:, pl.ds(pl.multiple_of(f * 128, 128), 128)]
            column = 0
            for ref in right_refs:
                product = dot_first(left, ref[...])
                for j in range(ref.shape[1] // 128):
                    rows_ref[pl.ds(base + f * 128 * width + column, 128, stride=width), :] = product[
                        :, j * 128 : (j + 1) * 128
                    ]
                    column += 1
            return carry

        lax.fori_loop(0, left_ref.shape[1] // 128, block, 0)
        return base + left_ref.shape[1] * width

    def bias(base, ref):
        total = jnp.dot(ones, ref[...], preferred_element_type=jnp.float32)
        for j in range(ref.shape[1] // 128):
            rows_ref[base + j : base + j + 1, :] = total[0:1, j * 128 : (j + 1) * 128]
        return base + ref.shape[1] // 128

    share = share_rows // wide_size
    own_wide = lax.axis_index("wide")
    own_group = lax.axis_index("grp")
    chunks = []
    for owner in range(group_size):
        for place in range(wide_size):
            low = place * share
            size = max(0, min(share, part_rows - low))
            chunks.append((owner, place, owner * part_rows + low, size))
    flying = {}
    sent = 0
    bias_known = False

    def pieces(slot, owner, place):
        if not relative:
            return [(stage_ref.at[slot], kept_refs[0].at[owner, place], None)]
        flips = place ^ own_wide
        flip = {
            "y": owner ^ own_group,
            "x": (flips >> 1) & 1,
            "near": (flips >> 2) & 1,
            "far": (flips >> 3) & 1,
        }
        found = []
        for (low, high), order, kept_ref, sent_ref in zip(cuts, ORDERS, kept_refs, sent_refs):
            spot = tuple(flip[name] for name in order + ("far",))
            source = stage_ref.at[slot, pl.ds(low, high - low), :]
            found.append((source, kept_ref.at[spot], sent_ref.at[spot]))
        return found

    def launch(slot, owner, place):
        for source, kept, other in pieces(slot, owner, place):

            def start(target, source=source):
                pltpu.make_async_copy(source, target, stage_sems.at[slot]).start()

            if other is None:
                start(kept)
            else:
                other_core = ((place ^ own_wide) & 1) == 1
                pl.when(other_core)(functools.partial(start, other))
                pl.when(jnp.logical_not(other_core))(functools.partial(start, kept))

    def finish(slot):
        if slot in flying:
            for source, kept, _ in pieces(slot, *flying.pop(slot)):
                pltpu.make_async_copy(source, kept, stage_sems.at[slot]).wait()

    def emit(upto):
        nonlocal sent
        while sent < len(chunks) and chunks[sent][2] + chunks[sent][3] <= upto:
            if chunks[sent][3] < share and not bias_known:
                break
            owner, place, source, size = chunks[sent]
            slot = sent % 2
            finish(slot)
            step = next(s for s in (128, 64, 32, 16) if size % s == 0)

            def convert(i, carry, source=source, slot=slot, step=step):
                at = pl.multiple_of(i * step, step)
                stage_ref[slot, pl.ds(at, step), :] = rows_ref[
                    pl.ds(pl.multiple_of(source + at, 16), step), :
                ].astype(jnp.bfloat16)
                return carry

            lax.fori_loop(0, size // step, convert, 0)
            if size < share:
                bias_place = part_rows - place * share
                first = max(0, -bias_place)
                stage_ref[slot, size:share, :] = bias_ref[first : first + share - size, :]
            launch(slot, owner, place)
            flying[slot] = (owner, place)
            sent += 1

    row = weight(0, n1_ref, [dq_ref, dk_ref, dv_ref])
    row = bias(row, dq_ref)
    row = bias(row, dv_ref)
    emit(row)
    row = weight(row, att_ref, [dproj_ref])
    proj_bias = row
    row = bias(row, dproj_ref)
    bias_size = dproj_ref.shape[1] // 128
    spare = share_rows - part_rows
    bias_ref[...] = jnp.concatenate(
        [
            rows_ref[proj_bias : proj_bias + bias_size, :],
            jnp.zeros((spare - bias_size, 128), jnp.float32),
        ],
        0,
    ).astype(jnp.bfloat16)
    bias_known = True
    emit(row)
    row = weight(row, n2_ref, [dpre_ref])
    row = bias(row, dpre_ref)
    emit(row)
    row = weight(row, act_ref, [dout_ref])
    row = bias(row, dout_ref)
    emit(row)
    rows_ref[row : row + tail_ref.shape[0], :] = tail_ref[...]
    emit(group_size * part_rows)
    for slot in range(2):
        finish(slot)


def pack_shares(factors, tail, part_rows, group_size, wide_size):
    feature = factors[0].shape[1]
    grain = 16 * wide_size
    share_rows = -(-(part_rows + feature // 128) // grain) * grain
    spare = share_rows - part_rows
    share = share_rows // wide_size
    relative = halves(wide_size, group_size)
    whole = pl.BlockSpec(memory_space=pltpu.VMEM)
    if relative:
        units = share // 16
        ends = [0, (units + 2) // 3 * 16, ((units + 2) // 3 + (units + 1) // 3) * 16, share]
        cuts = tuple(zip(ends, ends[1:]))
        shapes = [(2, 2, 2, 2, high - low, 128) for low, high in cuts] * 2
    else:
        cuts = ((0, share),)
        shapes = [(group_size, wide_size, share, 128)]
    return pl.pallas_call(
        functools.partial(
            pack_kernel,
            part_rows=part_rows,
            share_rows=share_rows,
            group_size=group_size,
            wide_size=wide_size,
            cuts=cuts,
            relative=relative,
        ),
        in_specs=[whole] * (len(factors) + 1),
        out_specs=[pl.BlockSpec(memory_space=pl.ANY)] * len(shapes),
        out_shape=[jax.ShapeDtypeStruct(shape, jnp.bfloat16) for shape in shapes],
        scratch_shapes=[
            pltpu.VMEM((group_size * part_rows, 128), jnp.float32),
            pltpu.VMEM((2, share, 128), jnp.bfloat16),
            pltpu.VMEM((spare, 128), jnp.bfloat16),
            pltpu.SemaphoreType.DMA((2,)),
        ],
        compiler_params=pltpu.CompilerParams(vmem_limit_bytes=60 * 1024 * 1024),
        name="pack_grads",
    )(*factors, tail)


def gelu_slope(pre_act):
    normal_cdf = 0.5 * (1.0 + jax.scipy.special.erf(pre_act / math.sqrt(2.0)))
    return normal_cdf + pre_act * jnp.exp(-0.5 * pre_act * pre_act) / math.sqrt(2.0 * math.pi)


def window_pass(tokens, cotangent, keep_mask, weights):
    (
        qkv_w,
        qv_b,
        proj_w,
        proj_b,
        fc1_w,
        fc1_b,
        fc2_w,
        fc2_b,
        ln1_g,
        ln1_b,
        ln2_g,
        ln2_b,
        table_h,
        table_w,
    ) = weights
    win_count, tok_count, feature = tokens.shape
    row_count = win_count * tok_count
    inputs = tokens.reshape(row_count, feature).astype(jnp.float32)
    keep_rows = keep_mask.reshape(row_count, 1)
    hat_one, scale_one = normalize(inputs)
    normed_one = (
        (hat_one * ln1_g.astype(jnp.float32) + ln1_b.astype(jnp.float32)) * keep_rows
    ).astype(jnp.bfloat16)
    bias_full = jnp.concatenate(
        [qv_b[:feature], jnp.zeros((feature,), jnp.bfloat16), qv_b[feature:]]
    ).astype(jnp.float32)
    mixed = (jnp.dot(normed_one, qkv_w, preferred_element_type=jnp.float32) + bias_full).astype(
        jnp.bfloat16
    )
    shift, key_cells = window_constants(tok_count)
    table = wide_table(table_h, table_w)
    probs, attended = attend(mixed, table, shift, key_cells, feature)
    resid = keep_rows * (
        inputs
        + jnp.dot(attended, proj_w, preferred_element_type=jnp.float32)
        + proj_b.astype(jnp.float32)
    )
    hat_two, scale_two = normalize(resid)
    normed_two = (hat_two * ln2_g.astype(jnp.float32) + ln2_b.astype(jnp.float32)).astype(
        jnp.bfloat16
    )
    pre_act = jnp.dot(normed_two, fc1_w, preferred_element_type=jnp.float32) + fc1_b.astype(
        jnp.float32
    )
    activation = jax.nn.gelu(pre_act, approximate=False).astype(jnp.bfloat16)
    result = keep_rows * (
        resid
        + jnp.dot(activation, fc2_w, preferred_element_type=jnp.float32)
        + fc2_b.astype(jnp.float32)
    )
    cot_rows = cotangent.reshape(row_count, feature).astype(jnp.float32) * keep_rows
    grad_out = cot_rows.astype(jnp.bfloat16)
    grad_act = jnp.einsum("nd,fd->nf", grad_out, fc2_w, preferred_element_type=jnp.float32)
    grad_pre = (grad_act * gelu_slope(pre_act)).astype(jnp.bfloat16)
    grad_norm_two = jnp.einsum("nf,df->nd", grad_pre, fc1_w, preferred_element_type=jnp.float32)
    grad_ln2_g = jnp.sum(grad_norm_two * hat_two, 0)
    grad_ln2_b = jnp.sum(grad_norm_two, 0)
    grad_resid = cot_rows + norm_back(grad_norm_two * ln2_g.astype(jnp.float32), hat_two, scale_two)
    grad_branch = keep_rows * grad_resid
    grad_proj = grad_branch.astype(jnp.bfloat16)
    grad_att = jnp.einsum(
        "ne,de->nd", grad_proj, proj_w, preferred_element_type=jnp.float32
    ).astype(jnp.bfloat16)
    grad_query, grad_keys, grad_values, grad_table = attend_back(
        mixed, probs, grad_att, table, shift, key_cells, feature
    )
    rel_span = table_h.shape[0]
    grad_table_h = grad_table[:, :rel_span].T[::-1]
    grad_table_w = grad_table[:, 64 : 64 + rel_span].T[::-1]
    grad_mixed = jnp.concatenate([grad_query, grad_keys, grad_values], -1)
    grad_norm_one = keep_rows * jnp.einsum(
        "nf,df->nd", grad_mixed, qkv_w, preferred_element_type=jnp.float32
    )
    grad_ln1_g = jnp.sum(grad_norm_one * hat_one, 0)
    grad_ln1_b = jnp.sum(grad_norm_one, 0)
    grad_input = grad_branch + norm_back(
        grad_norm_one * ln1_g.astype(jnp.float32), hat_one, scale_one
    )
    factors = (
        normed_one,
        grad_query,
        grad_keys,
        grad_values,
        attended,
        grad_proj,
        normed_two,
        grad_pre,
        activation,
        grad_out,
    )
    tail = (grad_ln1_g, grad_ln1_b, grad_ln2_g, grad_ln2_b, grad_table_h, grad_table_w)
    block_part = result.reshape(win_count, tok_count, feature).astype(jnp.bfloat16)
    input_part = grad_input.reshape(win_count, tok_count, feature).astype(jnp.bfloat16)
    return (block_part, input_part, factors, tail)


def swap(values, axis, bit):
    return lax.ppermute(values, axis, [(i, i ^ bit) for i in range(lax.axis_size(axis))])


def wide_bits(count):
    place = lax.axis_index("wide")
    return [(place >> bit) & 1 for bit in range(count)]


def splits(part_rows):
    return lax.axis_size("grp") == 2 and lax.axis_size("wide") % 8 == 0 and part_rows % 64 == 0


def eighth_index(core, cross, deep):
    return (core * 2 + cross) * 2 + deep


def gather_groups(mine, diagonal, finish, base):
    core, cross, deep = wide_bits(3)
    first = swap(mine, "grp", 1)
    diagonal, first = lax.optimization_barrier((diagonal, first))
    last = swap(diagonal, "grp", 1)
    side = swap(first, "wide", 2)
    back = swap(first, "wide", 4)
    near = (first, side, back, last)
    far = [swap(part, "wide", 1) for part in near]
    group = lax.axis_index("grp")
    own = finish(first)
    out = base.reshape((2, 8) + mine.shape)
    out = lax.dynamic_update_slice(out, own.reshape((1, 8) + mine.shape), (group, 0, 0, 0))
    for parts, which in ((near, core), (far, 1 - core)):
        for part, flip_cross, flip_deep in zip(parts, (0, 1, 0, 1), (0, 0, 1, 1)):
            at = eighth_index(which, cross ^ flip_cross, deep ^ flip_deep)
            out = lax.dynamic_update_slice(out, part[None, None], (1 - group, at, 0, 0))
    return out.reshape(2 * own.shape[0], 128)


def joined(kept, sent):
    return (kept.astype(jnp.float32) + sent.astype(jnp.float32)).astype(kept.dtype)


def reduce_shares(packed):
    if len(packed) == 1:
        rows = packed[0].reshape(-1, 128)
        return lax.psum_scatter(rows, ("grp", "wide"), scatter_dimension=0, tiled=True)
    moves = {
        "x": lambda v: swap(v, "wide", 2),
        "near": lambda v: swap(v, "wide", 4),
        "far": lambda v: swap(v, "wide", 8),
        "y": lambda v: swap(v, "grp", 1),
    }
    done = []
    for kept, sent, order in zip(packed[:3], packed[3:], ORDERS):
        arrived = swap(sent, "wide", 1)
        for name in order + ("far",):
            leaving = joined(kept[1], arrived[1])
            kept = joined(kept[0], arrived[0])
            arrived = moves[name](leaving)
        done.append(joined(kept, arrived))
    return jnp.concatenate(done, 0)


def own_eighths(rows):
    core, cross, deep = wide_bits(3)
    parts = rows.reshape(8, -1, 128)
    spots = (eighth_index(core, cross, deep), eighth_index(core, 1 - cross, 1 - deep))
    return [lax.dynamic_index_in_dim(parts, spot, keepdims=False) for spot in spots]


def first_step(grads, first_moment):
    return BETA_ONE * first_moment + (1.0 - BETA_ONE) * grads


def second_step(grads, master, moment_next, second_moment):
    second_next = BETA_TWO * second_moment + (1.0 - BETA_TWO) * grads * grads
    fix_one = 1.0 - BETA_ONE**ADAM_STEP
    fix_two = 1.0 - BETA_TWO**ADAM_STEP
    update = (
        moment_next / fix_one / (jnp.sqrt(second_next / fix_two) + ADAM_EPS) + DECAY_RATE * master
    )
    return (master - LEARN_RATE * update, second_next)


def body(tokens, cotangent, window_place, master, first_moment, second_moment):
    part_rows = master.shape[0]
    wide_size = lax.axis_size("wide")
    group_size = lax.axis_size("grp")
    feature = tokens.shape[-1]
    micro_count, slots, tok_count, _ = tokens.shape
    masks = token_mask(window_place)
    if splits(part_rows):
        mine, diagonal = (part.astype(jnp.bfloat16) for part in own_eighths(master))
        gathered = gather_groups(
            mine,
            diagonal,
            lambda first: master.astype(jnp.bfloat16),
            jnp.zeros((part_rows * group_size, 128), jnp.bfloat16),
        )
    else:
        gathered = lax.all_gather(master.astype(jnp.bfloat16), "grp", axis=0, tiled=True)
    weights = unpack(gathered, feature)
    wins = micro_count * slots
    extra = -tok_count % 16

    def padded(values):
        values = values.reshape((wins,) + values.shape[2:])
        return jnp.pad(values, ((0, 0), (0, extra)) + ((0, 0),) * (values.ndim - 2))

    block_part, input_part, factors, tail = window_pass(
        padded(tokens), padded(cotangent), padded(masks), weights
    )
    filled = sum(math.prod(dims_of) for dims_of in layout(feature)[:8]) // 128
    tail = jnp.concatenate([member.reshape(-1) for member in tail])
    tail_rows = part_rows * group_size - filled
    tail = jnp.pad(tail, (0, tail_rows * 128 - tail.shape[0])).reshape(tail_rows, 128)
    packed = pack_shares(factors, tail, part_rows, group_size, wide_size)
    owned = reduce_shares(packed)
    totals = lax.all_gather(owned, "wide", axis=0, tiled=True)
    factor = 1.0 / (micro_count * wide_size * group_size)
    bias_total = totals[part_rows : part_rows + feature // 128]
    proj_bias_grad = bias_total.astype(jnp.float32).reshape(-1) * factor
    totals = totals[:part_rows]

    def scaled(total_rows):
        return total_rows.astype(jnp.float32) * factor

    grads = scaled(totals)
    moment_next = first_step(grads, first_moment)
    later = []

    def finish(arrived):
        held, moment, _ = lax.optimization_barrier((totals, first_moment, arrived))
        held = scaled(held)
        later.extend(second_step(held, master, first_step(held, moment), second_moment))
        return later[0].astype(jnp.bfloat16)

    if splits(part_rows):
        mine, diagonal = (
            second_step(scaled(total), old, first_step(scaled(total), moment), second)[0].astype(
                jnp.bfloat16
            )
            for total, old, moment, second in zip(
                *(own_eighths(rows) for rows in (totals, master, first_moment, second_moment))
            )
        )
        weights_next = gather_groups(mine, diagonal, finish, gathered)
    else:
        weights_next = lax.all_gather(finish(totals), "grp", axis=0, tiled=True)
    master_next, second_next = later
    block_out = block_part[:, :tok_count].reshape(tokens.shape)
    input_grad = input_part[:, :tok_count].reshape(tokens.shape)
    return (
        block_out,
        input_grad,
        grads,
        master_next,
        moment_next,
        second_next,
        weights_next,
        proj_bias_grad,
    )


def solution(mesh):
    return jax.shard_map(
        body,
        mesh=mesh,
        in_specs=(
            P(None, ("wide", "grp"), None, None),
            P(None, ("wide", "grp"), None, None),
            P(None, ("wide", "grp")),
            P("grp", None),
            P("grp", None),
            P("grp", None),
        ),
        out_specs=(
            P(None, ("wide", "grp"), None, None),
            P(None, ("wide", "grp"), None, None),
            P("grp", None),
            P("grp", None),
            P("grp", None),
            P("grp", None),
            P(),
            P(),
        ),
        check_vma=False,
    )
```

```python
import functools
import math

import jax
import jax.numpy as jnp
from jax import lax
from jax.experimental import pallas as pl
from jax.experimental.pallas import tpu as pltpu
from jax.sharding import PartitionSpec as P

FF = 3072
HD = 64
WS = 14
GRID = 64
ADAM_STEP = 10


EPS_NORM = 1e-06
BETA_ONE = 0.9
BETA_TWO = 0.95
ADAM_EPS = 1e-08
LEARN_RATE = 0.02
DECAY_RATE = 0.1


def layout(feature):
    rel_span = 2 * WS - 1
    return [
        (feature, 3 * feature),
        (2 * feature,),
        (feature, feature),
        (feature,),
        (feature, FF),
        (FF,),
        (FF, feature),
        (feature,),
        (feature,),
        (feature,),
        (feature,),
        (feature,),
        (rel_span, HD),
        (rel_span, HD),
    ]


def unpack(rows, feature):
    members = []
    row = 0
    dims = layout(feature)
    for dims_of in dims[:8]:
        length = math.prod(dims_of) // 128
        members.append(rows[row : row + length].reshape(dims_of))
        row = row + length
    tail_size = sum(math.prod(dims_of) for dims_of in dims[8:])
    tail = rows[row : row - (-tail_size // 128)].reshape(-1)
    offset = 0
    for dims_of in dims[8:]:
        length = math.prod(dims_of)
        members.append(tail[offset : offset + length].reshape(dims_of))
        offset = offset + length
    return tuple(members)


def token_mask(window_place):
    cells = jnp.arange(WS * WS, dtype=jnp.int32)
    inner_row = cells // WS
    inner_col = cells % WS
    places = window_place[..., None]
    live_slot = places < 25
    row_real = WS * (places // 5) + inner_row < GRID
    col_real = WS * (places % 5) + inner_col < GRID
    return jnp.where(live_slot & row_real & col_real, 1.0, 0.0).astype(jnp.float32)


def normalize(inputs):
    row_mean = jnp.mean(inputs, -1, keepdims=True)
    centred = inputs - row_mean
    inv_scale = lax.rsqrt(jnp.mean(centred * centred, -1, keepdims=True) + EPS_NORM)
    return (centred * inv_scale, inv_scale)


def norm_back(grad_hat, normed_hat, inv_scale):
    first_mean = jnp.mean(grad_hat, -1, keepdims=True)
    second_mean = jnp.mean(grad_hat * normed_hat, -1, keepdims=True)
    return inv_scale * (grad_hat - first_mean - normed_hat * second_mean)


def attend_kernel(q_ref, k_ref, v_ref, table_ref, shift_ref, key_ref, probs_ref, out_ref):
    shift = shift_ref[...]
    key_cells = key_ref[...]
    row_count = shift.shape[0]
    real_key = lax.broadcasted_iota(jnp.int32, (row_count, row_count), 1) < WS * WS
    for part in range(2):
        cut = slice(part * HD, (part + 1) * HD)
        queries = q_ref[:, cut]
        along = jnp.dot(queries, table_ref[...], preferred_element_type=jnp.float32)
        for bit in (1, 2, 4, 8):
            along = jnp.where((shift & bit) != 0, pltpu.roll(along, 128 - bit, 1), along)
        high = along.astype(jnp.bfloat16)
        low = (along - high.astype(jnp.float32)).astype(jnp.bfloat16)
        scores = dot_last(queries, k_ref[:, cut]) * (1.0 / math.sqrt(HD))
        scores = scores + dot_last(high, key_cells) + dot_last(low, key_cells)
        scores = jnp.where(real_key, scores, -1e30)
        powers = jnp.exp(scores - jnp.max(scores, -1, keepdims=True))
        probs = (powers / jnp.sum(powers, -1, keepdims=True)).astype(jnp.bfloat16)
        probs_ref[0, part] = probs
        out_ref[:, cut] = jnp.dot(
            probs, v_ref[:, cut], preferred_element_type=jnp.float32
        ).astype(jnp.bfloat16)


def attend_back_kernel(
    q_ref, k_ref, v_ref, probs_ref, grad_ref, table_ref, shift_ref, key_ref,
    dq_ref, dk_ref, dv_ref, dtable_ref,
):
    shift = shift_ref[...]
    key_cells = key_ref[...]
    scale = 1.0 / math.sqrt(HD)

    @pl.when((pl.program_id(0) == 0) & (pl.program_id(1) == 0))
    def _():
        dtable_ref[...] = jnp.zeros(dtable_ref.shape, jnp.float32)

    for part in range(2):
        cut = slice(part * HD, (part + 1) * HD)
        queries = q_ref[:, cut]
        grad = grad_ref[:, cut]
        probs = probs_ref[0, part]
        dv_ref[:, cut] = dot_first(probs, grad).astype(jnp.bfloat16)
        grad_probs = dot_last(grad, v_ref[:, cut])
        wide_probs = probs.astype(jnp.float32)
        inner = jnp.sum(wide_probs * grad_probs, -1, keepdims=True)
        grad_scores = (wide_probs * (grad_probs - inner)).astype(jnp.bfloat16)
        dk_ref[:, cut] = (dot_first(grad_scores, queries) * scale).astype(jnp.bfloat16)
        along = jnp.dot(grad_scores, key_cells, preferred_element_type=jnp.float32)
        for bit in (1, 2, 4, 8):
            along = jnp.where((shift & bit) != 0, pltpu.roll(along, bit, 1), along)
        high = along.astype(jnp.bfloat16)
        low = (along - high.astype(jnp.float32)).astype(jnp.bfloat16)
        grad_query = jnp.dot(grad_scores, k_ref[:, cut], preferred_element_type=jnp.float32) * scale
        grad_query = grad_query + dot_last(high, table_ref[...]) + dot_last(low, table_ref[...])
        dq_ref[:, cut] = grad_query.astype(jnp.bfloat16)
        dtable_ref[...] += dot_first(queries, high) + dot_first(queries, low)


def window_constants(row_count):
    cells = jnp.arange(row_count, dtype=jnp.int32)[:, None]
    lanes = jnp.arange(128, dtype=jnp.int32)[None, :]
    first = lanes < 64
    shift = jnp.where(first, WS - 1 - cells // WS, WS - 1 - cells % WS)
    live = cells < WS * WS
    shift = jnp.where(live, shift, 0)
    offset = jnp.where(first, lanes, lanes - 64)
    place = jnp.where(first, cells // WS, cells % WS)
    key_cells = jnp.where(live & (offset == place), 1.0, 0.0).astype(jnp.bfloat16)
    return shift, key_cells


def wide_table(table_h, table_w):
    pad = jnp.zeros((HD, 64 - table_h.shape[0]), table_h.dtype)
    return jnp.concatenate([table_h[::-1].T, pad, table_w[::-1].T, pad], 1)


def attend(mixed, table, shift, key_cells, feature):
    rows, pairs = shift.shape[0], feature // 128
    wins = mixed.shape[0] // rows
    whole = lambda shape: pl.BlockSpec(shape, lambda w, h: (0,) * len(shape))
    column = lambda base: pl.BlockSpec((rows, 128), lambda w, h: (w, base * pairs + h))
    return pl.pallas_call(
        attend_kernel,
        grid=(wins, pairs),
        in_specs=[column(0), column(1), column(2), whole((HD, 128)), whole((rows, 128)), whole((rows, 128))],
        out_specs=[
            pl.BlockSpec((1, 2, rows, rows), lambda w, h: (w, h, 0, 0)),
            pl.BlockSpec((rows, 128), lambda w, h: (w, h)),
        ],
        out_shape=[
            jax.ShapeDtypeStruct((wins, 2 * pairs, rows, rows), jnp.bfloat16),
            jax.ShapeDtypeStruct((wins * rows, feature), jnp.bfloat16),
        ],
        name="attend",
    )(mixed, mixed, mixed, table, shift, key_cells)


def attend_back(mixed, probs, grad_att, table, shift, key_cells, feature):
    rows, pairs = shift.shape[0], feature // 128
    wins = mixed.shape[0] // rows
    whole = lambda shape: pl.BlockSpec(shape, lambda w, h: (0,) * len(shape))
    column = lambda base: pl.BlockSpec((rows, 128), lambda w, h: (w, base * pairs + h))
    flat = jax.ShapeDtypeStruct((wins * rows, feature), jnp.bfloat16)
    return pl.pallas_call(
        attend_back_kernel,
        grid=(wins, pairs),
        in_specs=[
            column(0), column(1), column(2),
            pl.BlockSpec((1, 2, rows, rows), lambda w, h: (w, h, 0, 0)),
            column(0),
            whole((HD, 128)), whole((rows, 128)), whole((rows, 128)),
        ],
        out_specs=[column(0), column(0), column(0), whole((HD, 128))],
        out_shape=[flat, flat, flat, jax.ShapeDtypeStruct((HD, 128), jnp.float32)],
        name="attend_back",
    )(mixed, mixed, mixed, probs, grad_att, table, shift, key_cells)


def dot_last(left, right):
    return lax.dot_general(left, right, (((1,), (1,)), ((), ())), preferred_element_type=jnp.float32)


def dot_first(left, right):
    return lax.dot_general(left, right, (((0,), (0,)), ((), ())), preferred_element_type=jnp.float32)


ORDERS = (("y", "x", "near"), ("x", "near", "y"), ("near", "y", "x"))


def halves(wide_size, group_size):
    return (wide_size, group_size) == (16, 2)


def pack_kernel(
    n1_ref, dq_ref, dk_ref, dv_ref, att_ref, dproj_ref, n2_ref, dpre_ref, act_ref, dout_ref, tail_ref,
    *refs, part_rows, share_rows, group_size, wide_size, cuts, relative,
):
    *out_refs, rows_ref, stage_ref, bias_ref, stage_sems = refs
    kept_refs, sent_refs = out_refs[: len(cuts)], out_refs[len(cuts) :]
    count = n1_ref.shape[0]
    ones = jnp.ones((16, count), jnp.bfloat16)

    def weight(base, left_ref, right_refs):
        width = sum(ref.shape[1] for ref in right_refs) // 128

        def block(f, carry):
            left = left_ref[:, pl.ds(pl.multiple_of(f * 128, 128), 128)]
            column = 0
            for ref in right_refs:
                product = dot_first(left, ref[...])
                for j in range(ref.shape[1] // 128):
                    rows_ref[pl.ds(base + f * 128 * width + column, 128, stride=width), :] = product[
                        :, j * 128 : (j + 1) * 128
                    ]
                    column += 1
            return carry

        lax.fori_loop(0, left_ref.shape[1] // 128, block, 0)
        return base + left_ref.shape[1] * width

    def bias(base, ref):
        total = jnp.dot(ones, ref[...], preferred_element_type=jnp.float32)
        for j in range(ref.shape[1] // 128):
            rows_ref[base + j : base + j + 1, :] = total[0:1, j * 128 : (j + 1) * 128]
        return base + ref.shape[1] // 128

    share = share_rows // wide_size
    own_wide = lax.axis_index("wide")
    own_group = lax.axis_index("grp")
    chunks = []
    for owner in range(group_size):
        for place in range(wide_size):
            low = place * share
            size = max(0, min(share, part_rows - low))
            chunks.append((owner, place, owner * part_rows + low, size))
    flying = {}
    sent = 0
    bias_known = False

    def pieces(slot, owner, place):
        if not relative:
            return [(stage_ref.at[slot], kept_refs[0].at[owner, place], None)]
        flips = place ^ own_wide
        flip = {
            "y": owner ^ own_group,
            "x": (flips >> 1) & 1,
            "near": (flips >> 2) & 1,
            "far": (flips >> 3) & 1,
        }
        found = []
        for (low, high), order, kept_ref, sent_ref in zip(cuts, ORDERS, kept_refs, sent_refs):
            spot = tuple(flip[name] for name in order + ("far",))
            source = stage_ref.at[slot, pl.ds(low, high - low), :]
            found.append((source, kept_ref.at[spot], sent_ref.at[spot]))
        return found

    def launch(slot, owner, place):
        for source, kept, other in pieces(slot, owner, place):

            def start(target, source=source):
                pltpu.make_async_copy(source, target, stage_sems.at[slot]).start()

            if other is None:
                start(kept)
            else:
                other_core = ((place ^ own_wide) & 1) == 1
                pl.when(other_core)(functools.partial(start, other))
                pl.when(jnp.logical_not(other_core))(functools.partial(start, kept))

    def finish(slot):
        if slot in flying:
            for source, kept, _ in pieces(slot, *flying.pop(slot)):
                pltpu.make_async_copy(source, kept, stage_sems.at[slot]).wait()

    def emit(upto):
        nonlocal sent
        while sent < len(chunks) and chunks[sent][2] + chunks[sent][3] <= upto:
            if chunks[sent][3] < share and not bias_known:
                break
            owner, place, source, size = chunks[sent]
            slot = sent % 2
            finish(slot)

            def convert(at, count, source=source, slot=slot):
                stage_ref[slot, pl.ds(at, count), :] = rows_ref[
                    pl.ds(pl.multiple_of(source + at, 16), count), :
                ].astype(jnp.bfloat16)

            def convert_block(i, carry, convert=convert):
                convert(pl.multiple_of(i * 128, 128), 128)
                return carry

            lax.fori_loop(0, size // 128, convert_block, 0)
            if size % 128:
                convert(size - size % 128, size % 128)
            if size < share:
                bias_place = part_rows - place * share
                first = max(0, -bias_place)
                stage_ref[slot, size:share, :] = bias_ref[first : first + share - size, :]
            launch(slot, owner, place)
            flying[slot] = (owner, place)
            sent += 1

    row = weight(0, n1_ref, [dq_ref, dk_ref, dv_ref])
    row = bias(row, dq_ref)
    row = bias(row, dv_ref)
    emit(row)
    row = weight(row, att_ref, [dproj_ref])
    proj_bias = row
    row = bias(row, dproj_ref)
    bias_size = dproj_ref.shape[1] // 128
    spare = share_rows - part_rows
    bias_ref[...] = jnp.concatenate(
        [
            rows_ref[proj_bias : proj_bias + bias_size, :],
            jnp.zeros((spare - bias_size, 128), jnp.float32),
        ],
        0,
    ).astype(jnp.bfloat16)
    bias_known = True
    emit(row)
    row = weight(row, n2_ref, [dpre_ref])
    row = bias(row, dpre_ref)
    emit(row)
    row = weight(row, act_ref, [dout_ref])
    row = bias(row, dout_ref)
    emit(row)
    rows_ref[row : row + tail_ref.shape[0], :] = tail_ref[...]
    emit(group_size * part_rows)
    for slot in range(2):
        finish(slot)


def pack_shares(factors, tail, part_rows, group_size, wide_size):
    feature = factors[0].shape[1]
    grain = 16 * wide_size
    share_rows = -(-(part_rows + feature // 128) // grain) * grain
    spare = share_rows - part_rows
    share = share_rows // wide_size
    relative = halves(wide_size, group_size)
    whole = pl.BlockSpec(memory_space=pltpu.VMEM)
    if relative:
        units = share // 16
        ends = [0, (units + 2) // 3 * 16, ((units + 2) // 3 + (units + 1) // 3) * 16, share]
        cuts = tuple(zip(ends, ends[1:]))
        shapes = [(2, 2, 2, 2, high - low, 128) for low, high in cuts] * 2
    else:
        cuts = ((0, share),)
        shapes = [(group_size, wide_size, share, 128)]
    return pl.pallas_call(
        functools.partial(
            pack_kernel,
            part_rows=part_rows,
            share_rows=share_rows,
            group_size=group_size,
            wide_size=wide_size,
            cuts=cuts,
            relative=relative,
        ),
        in_specs=[whole] * (len(factors) + 1),
        out_specs=[pl.BlockSpec(memory_space=pl.ANY)] * len(shapes),
        out_shape=[jax.ShapeDtypeStruct(shape, jnp.bfloat16) for shape in shapes],
        scratch_shapes=[
            pltpu.VMEM((group_size * part_rows, 128), jnp.float32),
            pltpu.VMEM((2, share, 128), jnp.bfloat16),
            pltpu.VMEM((spare, 128), jnp.bfloat16),
            pltpu.SemaphoreType.DMA((2,)),
        ],
        compiler_params=pltpu.CompilerParams(vmem_limit_bytes=60 * 1024 * 1024),
        name="pack_grads",
    )(*factors, tail)


def gelu_slope(pre_act):
    normal_cdf = 0.5 * (1.0 + jax.scipy.special.erf(pre_act / math.sqrt(2.0)))
    return normal_cdf + pre_act * jnp.exp(-0.5 * pre_act * pre_act) / math.sqrt(2.0 * math.pi)


def window_pass(tokens, cotangent, keep_mask, weights):
    (
        qkv_w,
        qv_b,
        proj_w,
        proj_b,
        fc1_w,
        fc1_b,
        fc2_w,
        fc2_b,
        ln1_g,
        ln1_b,
        ln2_g,
        ln2_b,
        table_h,
        table_w,
    ) = weights
    win_count, tok_count, feature = tokens.shape
    row_count = win_count * tok_count
    inputs = tokens.reshape(row_count, feature).astype(jnp.float32)
    keep_rows = keep_mask.reshape(row_count, 1)
    hat_one, scale_one = normalize(inputs)
    normed_one = (
        (hat_one * ln1_g.astype(jnp.float32) + ln1_b.astype(jnp.float32)) * keep_rows
    ).astype(jnp.bfloat16)
    bias_full = jnp.concatenate(
        [qv_b[:feature], jnp.zeros((feature,), jnp.bfloat16), qv_b[feature:]]
    ).astype(jnp.float32)
    mixed = (jnp.dot(normed_one, qkv_w, preferred_element_type=jnp.float32) + bias_full).astype(
        jnp.bfloat16
    )
    shift, key_cells = window_constants(tok_count)
    table = wide_table(table_h, table_w)
    probs, attended = attend(mixed, table, shift, key_cells, feature)
    resid = keep_rows * (
        inputs
        + jnp.dot(attended, proj_w, preferred_element_type=jnp.float32)
        + proj_b.astype(jnp.float32)
    )
    hat_two, scale_two = normalize(resid)
    normed_two = (hat_two * ln2_g.astype(jnp.float32) + ln2_b.astype(jnp.float32)).astype(
        jnp.bfloat16
    )
    pre_act = jnp.dot(normed_two, fc1_w, preferred_element_type=jnp.float32) + fc1_b.astype(
        jnp.float32
    )
    activation = jax.nn.gelu(pre_act, approximate=False).astype(jnp.bfloat16)
    result = keep_rows * (
        resid
        + jnp.dot(activation, fc2_w, preferred_element_type=jnp.float32)
        + fc2_b.astype(jnp.float32)
    )
    cot_rows = cotangent.reshape(row_count, feature).astype(jnp.float32) * keep_rows
    grad_out = cot_rows.astype(jnp.bfloat16)
    grad_act = jnp.einsum("nd,fd->nf", grad_out, fc2_w, preferred_element_type=jnp.float32)
    grad_pre = (grad_act * gelu_slope(pre_act)).astype(jnp.bfloat16)
    grad_norm_two = jnp.einsum("nf,df->nd", grad_pre, fc1_w, preferred_element_type=jnp.float32)
    grad_ln2_g = jnp.sum(grad_norm_two * hat_two, 0)
    grad_ln2_b = jnp.sum(grad_norm_two, 0)
    grad_resid = cot_rows + norm_back(grad_norm_two * ln2_g.astype(jnp.float32), hat_two, scale_two)
    grad_branch = keep_rows * grad_resid
    grad_proj = grad_branch.astype(jnp.bfloat16)
    grad_att = jnp.einsum(
        "ne,de->nd", grad_proj, proj_w, preferred_element_type=jnp.float32
    ).astype(jnp.bfloat16)
    grad_query, grad_keys, grad_values, grad_table = attend_back(
        mixed, probs, grad_att, table, shift, key_cells, feature
    )
    rel_span = table_h.shape[0]
    grad_table_h = grad_table[:, :rel_span].T[::-1]
    grad_table_w = grad_table[:, 64 : 64 + rel_span].T[::-1]
    grad_mixed = jnp.concatenate([grad_query, grad_keys, grad_values], -1)
    grad_norm_one = keep_rows * jnp.einsum(
        "nf,df->nd", grad_mixed, qkv_w, preferred_element_type=jnp.float32
    )
    grad_ln1_g = jnp.sum(grad_norm_one * hat_one, 0)
    grad_ln1_b = jnp.sum(grad_norm_one, 0)
    grad_input = grad_branch + norm_back(
        grad_norm_one * ln1_g.astype(jnp.float32), hat_one, scale_one
    )
    factors = (
        normed_one,
        grad_query,
        grad_keys,
        grad_values,
        attended,
        grad_proj,
        normed_two,
        grad_pre,
        activation,
        grad_out,
    )
    tail = (grad_ln1_g, grad_ln1_b, grad_ln2_g, grad_ln2_b, grad_table_h, grad_table_w)
    block_part = result.reshape(win_count, tok_count, feature).astype(jnp.bfloat16)
    input_part = grad_input.reshape(win_count, tok_count, feature).astype(jnp.bfloat16)
    return (block_part, input_part, factors, tail)


def swap(values, axis, bit):
    return lax.ppermute(values, axis, [(i, i ^ bit) for i in range(lax.axis_size(axis))])


def wide_bits(count):
    place = lax.axis_index("wide")
    return [(place >> bit) & 1 for bit in range(count)]


def splits(part_rows):
    return lax.axis_size("grp") == 2 and lax.axis_size("wide") % 8 == 0 and part_rows % 64 == 0


def eighth_index(core, cross, deep):
    return (core * 2 + cross) * 2 + deep


def gather_groups(mine, diagonal, finish, base):
    core, cross, deep = wide_bits(3)
    first = swap(mine, "grp", 1)
    diagonal, first = lax.optimization_barrier((diagonal, first))
    last = swap(diagonal, "grp", 1)
    side = swap(first, "wide", 2)
    back = swap(first, "wide", 4)
    near = (first, side, back, last)
    far = [swap(part, "wide", 1) for part in near]
    group = lax.axis_index("grp")
    own = finish(first)
    out = base.reshape((2, 8) + mine.shape)
    out = lax.dynamic_update_slice(out, own.reshape((1, 8) + mine.shape), (group, 0, 0, 0))
    for parts, which in ((near, core), (far, 1 - core)):
        for part, flip_cross, flip_deep in zip(parts, (0, 1, 0, 1), (0, 0, 1, 1)):
            at = eighth_index(which, cross ^ flip_cross, deep ^ flip_deep)
            out = lax.dynamic_update_slice(out, part[None, None], (1 - group, at, 0, 0))
    return out.reshape(2 * own.shape[0], 128)


def joined(kept, sent):
    return (kept.astype(jnp.float32) + sent.astype(jnp.float32)).astype(kept.dtype)


def reduce_shares(packed):
    if len(packed) == 1:
        rows = packed[0].reshape(-1, 128)
        return lax.psum_scatter(rows, ("grp", "wide"), scatter_dimension=0, tiled=True)
    moves = {
        "x": lambda v: swap(v, "wide", 2),
        "near": lambda v: swap(v, "wide", 4),
        "far": lambda v: swap(v, "wide", 8),
        "y": lambda v: swap(v, "grp", 1),
    }
    done = []
    for kept, sent, order in zip(packed[:3], packed[3:], ORDERS):
        arrived = swap(sent, "wide", 1)
        for name in order + ("far",):
            leaving = joined(kept[1], arrived[1])
            kept = joined(kept[0], arrived[0])
            arrived = moves[name](leaving)
        done.append(joined(kept, arrived))
    return jnp.concatenate(done, 0)


def own_eighths(rows):
    core, cross, deep = wide_bits(3)
    parts = rows.reshape(8, -1, 128)
    spots = (eighth_index(core, cross, deep), eighth_index(core, 1 - cross, 1 - deep))
    return [lax.dynamic_index_in_dim(parts, spot, keepdims=False) for spot in spots]


def first_step(grads, first_moment):
    return BETA_ONE * first_moment + (1.0 - BETA_ONE) * grads


def second_step(grads, master, moment_next, second_moment):
    second_next = BETA_TWO * second_moment + (1.0 - BETA_TWO) * grads * grads
    fix_one = 1.0 - BETA_ONE**ADAM_STEP
    fix_two = 1.0 - BETA_TWO**ADAM_STEP
    update = (
        moment_next / fix_one / (jnp.sqrt(second_next / fix_two) + ADAM_EPS) + DECAY_RATE * master
    )
    return (master - LEARN_RATE * update, second_next)


def body(tokens, cotangent, window_place, master, first_moment, second_moment):
    part_rows = master.shape[0]
    wide_size = lax.axis_size("wide")
    group_size = lax.axis_size("grp")
    feature = tokens.shape[-1]
    micro_count, slots, tok_count, _ = tokens.shape
    masks = token_mask(window_place)
    if splits(part_rows):
        mine, diagonal = (part.astype(jnp.bfloat16) for part in own_eighths(master))
        gathered = gather_groups(
            mine,
            diagonal,
            lambda first: master.astype(jnp.bfloat16),
            jnp.zeros((part_rows * group_size, 128), jnp.bfloat16),
        )
    else:
        gathered = lax.all_gather(master.astype(jnp.bfloat16), "grp", axis=0, tiled=True)
    weights = unpack(gathered, feature)
    wins = micro_count * slots
    extra = -tok_count % 16

    def padded(values):
        values = values.reshape((wins,) + values.shape[2:])
        return jnp.pad(values, ((0, 0), (0, extra)) + ((0, 0),) * (values.ndim - 2))

    block_part, input_part, factors, tail = window_pass(
        padded(tokens), padded(cotangent), padded(masks), weights
    )
    filled = sum(math.prod(dims_of) for dims_of in layout(feature)[:8]) // 128
    tail = jnp.concatenate([member.reshape(-1) for member in tail])
    tail_rows = part_rows * group_size - filled
    tail = jnp.pad(tail, (0, tail_rows * 128 - tail.shape[0])).reshape(tail_rows, 128)
    packed = pack_shares(factors, tail, part_rows, group_size, wide_size)
    owned = reduce_shares(packed)
    totals = lax.all_gather(owned, "wide", axis=0, tiled=True)
    factor = 1.0 / (micro_count * wide_size * group_size)
    bias_total = totals[part_rows : part_rows + feature // 128]
    proj_bias_grad = bias_total.astype(jnp.float32).reshape(-1) * factor
    totals = totals[:part_rows]

    def scaled(total_rows):
        return total_rows.astype(jnp.float32) * factor

    grads = scaled(totals)
    moment_next = first_step(grads, first_moment)
    later = []

    def finish(arrived):
        held, moment, _ = lax.optimization_barrier((totals, first_moment, arrived))
        held = scaled(held)
        later.extend(second_step(held, master, first_step(held, moment), second_moment))
        return later[0].astype(jnp.bfloat16)

    if splits(part_rows):
        mine, diagonal = (
            second_step(scaled(total), old, first_step(scaled(total), moment), second)[0].astype(
                jnp.bfloat16
            )
            for total, old, moment, second in zip(
                *(own_eighths(rows) for rows in (totals, master, first_moment, second_moment))
            )
        )
        weights_next = gather_groups(mine, diagonal, finish, gathered)
    else:
        weights_next = lax.all_gather(finish(totals), "grp", axis=0, tiled=True)
    master_next, second_next = later
    block_out = block_part[:, :tok_count].reshape(tokens.shape)
    input_grad = input_part[:, :tok_count].reshape(tokens.shape)
    return (
        block_out,
        input_grad,
        grads,
        master_next,
        moment_next,
        second_next,
        weights_next,
        proj_bias_grad,
    )


def solution(mesh):
    return jax.shard_map(
        body,
        mesh=mesh,
        in_specs=(
            P(None, ("wide", "grp"), None, None),
            P(None, ("wide", "grp"), None, None),
            P(None, ("wide", "grp")),
            P("grp", None),
            P("grp", None),
            P("grp", None),
        ),
        out_specs=(
            P(None, ("wide", "grp"), None, None),
            P(None, ("wide", "grp"), None, None),
            P("grp", None),
            P("grp", None),
            P("grp", None),
            P("grp", None),
            P(),
            P(),
        ),
        check_vma=False,
    )
```

```python
import functools
import math

import jax
import jax.numpy as jnp
from jax import lax
from jax.experimental import pallas as pl
from jax.experimental.pallas import tpu as pltpu
from jax.sharding import PartitionSpec as P

FF = 3072
HD = 64
WS = 14
GRID = 64
ADAM_STEP = 10


EPS_NORM = 1e-06
BETA_ONE = 0.9
BETA_TWO = 0.95
ADAM_EPS = 1e-08
LEARN_RATE = 0.02
DECAY_RATE = 0.1


def layout(feature):
    rel_span = 2 * WS - 1
    return [
        (feature, 3 * feature),
        (2 * feature,),
        (feature, feature),
        (feature,),
        (feature, FF),
        (FF,),
        (FF, feature),
        (feature,),
        (feature,),
        (feature,),
        (feature,),
        (feature,),
        (rel_span, HD),
        (rel_span, HD),
    ]


def unpack(rows, feature):
    members = []
    row = 0
    dims = layout(feature)
    for dims_of in dims[:8]:
        length = math.prod(dims_of) // 128
        members.append(rows[row : row + length].reshape(dims_of))
        row = row + length
    tail_size = sum(math.prod(dims_of) for dims_of in dims[8:])
    tail = rows[row : row - (-tail_size // 128)].reshape(-1)
    offset = 0
    for dims_of in dims[8:]:
        length = math.prod(dims_of)
        members.append(tail[offset : offset + length].reshape(dims_of))
        offset = offset + length
    return tuple(members)


def token_mask(window_place):
    cells = jnp.arange(WS * WS, dtype=jnp.int32)
    inner_row = cells // WS
    inner_col = cells % WS
    places = window_place[..., None]
    live_slot = places < 25
    row_real = WS * (places // 5) + inner_row < GRID
    col_real = WS * (places % 5) + inner_col < GRID
    return jnp.where(live_slot & row_real & col_real, 1.0, 0.0).astype(jnp.float32)


def normalize(inputs):
    row_mean = jnp.mean(inputs, -1, keepdims=True)
    centred = inputs - row_mean
    inv_scale = lax.rsqrt(jnp.mean(centred * centred, -1, keepdims=True) + EPS_NORM)
    return (centred * inv_scale, inv_scale)


def norm_back(grad_hat, normed_hat, inv_scale):
    first_mean = jnp.mean(grad_hat, -1, keepdims=True)
    second_mean = jnp.mean(grad_hat * normed_hat, -1, keepdims=True)
    return inv_scale * (grad_hat - first_mean - normed_hat * second_mean)


def attend_kernel(q_ref, k_ref, v_ref, table_ref, shift_ref, key_ref, probs_ref, out_ref):
    shift = shift_ref[...]
    key_cells = key_ref[...]
    row_count = shift.shape[0]
    real_key = lax.broadcasted_iota(jnp.int32, (row_count, row_count), 1) < WS * WS
    for part in range(2):
        cut = slice(part * HD, (part + 1) * HD)
        queries = q_ref[:, cut]
        along = jnp.dot(queries, table_ref[...], preferred_element_type=jnp.float32)
        for bit in (1, 2, 4, 8):
            along = jnp.where((shift & bit) != 0, pltpu.roll(along, 128 - bit, 1), along)
        high = along.astype(jnp.bfloat16)
        low = (along - high.astype(jnp.float32)).astype(jnp.bfloat16)
        scores = dot_last(queries, k_ref[:, cut]) * (1.0 / math.sqrt(HD))
        scores = scores + dot_last(high, key_cells) + dot_last(low, key_cells)
        scores = jnp.where(real_key, scores, -1e30)
        powers = jnp.exp(scores - jnp.max(scores, -1, keepdims=True))
        probs = (powers / jnp.sum(powers, -1, keepdims=True)).astype(jnp.bfloat16)
        probs_ref[0, part] = probs
        out_ref[:, cut] = jnp.dot(
            probs, v_ref[:, cut], preferred_element_type=jnp.float32
        ).astype(jnp.bfloat16)


def attend_back_kernel(
    q_ref, k_ref, v_ref, probs_ref, grad_ref, table_ref, shift_ref, key_ref,
    dq_ref, dk_ref, dv_ref, dtable_ref,
):
    shift = shift_ref[...]
    key_cells = key_ref[...]
    scale = 1.0 / math.sqrt(HD)

    @pl.when((pl.program_id(0) == 0) & (pl.program_id(1) == 0))
    def _():
        dtable_ref[...] = jnp.zeros(dtable_ref.shape, jnp.float32)

    for part in range(2):
        cut = slice(part * HD, (part + 1) * HD)
        queries = q_ref[:, cut]
        grad = grad_ref[:, cut]
        probs = probs_ref[0, part]
        dv_ref[:, cut] = dot_first(probs, grad).astype(jnp.bfloat16)
        grad_probs = dot_last(grad, v_ref[:, cut])
        wide_probs = probs.astype(jnp.float32)
        inner = jnp.sum(wide_probs * grad_probs, -1, keepdims=True)
        grad_scores = (wide_probs * (grad_probs - inner)).astype(jnp.bfloat16)
        dk_ref[:, cut] = (dot_first(grad_scores, queries) * scale).astype(jnp.bfloat16)
        along = jnp.dot(grad_scores, key_cells, preferred_element_type=jnp.float32)
        for bit in (1, 2, 4, 8):
            along = jnp.where((shift & bit) != 0, pltpu.roll(along, bit, 1), along)
        high = along.astype(jnp.bfloat16)
        low = (along - high.astype(jnp.float32)).astype(jnp.bfloat16)
        grad_query = jnp.dot(grad_scores, k_ref[:, cut], preferred_element_type=jnp.float32) * scale
        grad_query = grad_query + dot_last(high, table_ref[...]) + dot_last(low, table_ref[...])
        dq_ref[:, cut] = grad_query.astype(jnp.bfloat16)
        dtable_ref[...] += dot_first(queries, high) + dot_first(queries, low)


def window_constants(row_count):
    cells = jnp.arange(row_count, dtype=jnp.int32)[:, None]
    lanes = jnp.arange(128, dtype=jnp.int32)[None, :]
    first = lanes < 64
    shift = jnp.where(first, WS - 1 - cells // WS, WS - 1 - cells % WS)
    live = cells < WS * WS
    shift = jnp.where(live, shift, 0)
    offset = jnp.where(first, lanes, lanes - 64)
    place = jnp.where(first, cells // WS, cells % WS)
    key_cells = jnp.where(live & (offset == place), 1.0, 0.0).astype(jnp.bfloat16)
    return shift, key_cells


def wide_table(table_h, table_w):
    pad = jnp.zeros((HD, 64 - table_h.shape[0]), table_h.dtype)
    return jnp.concatenate([table_h[::-1].T, pad, table_w[::-1].T, pad], 1)


def attend(mixed, table, shift, key_cells, feature):
    rows, pairs = shift.shape[0], feature // 128
    wins = mixed.shape[0] // rows
    whole = lambda shape: pl.BlockSpec(shape, lambda w, h: (0,) * len(shape))
    column = lambda base: pl.BlockSpec((rows, 128), lambda w, h: (w, base * pairs + h))
    return pl.pallas_call(
        attend_kernel,
        grid=(wins, pairs),
        in_specs=[column(0), column(1), column(2), whole((HD, 128)), whole((rows, 128)), whole((rows, 128))],
        out_specs=[
            pl.BlockSpec((1, 2, rows, rows), lambda w, h: (w, h, 0, 0)),
            pl.BlockSpec((rows, 128), lambda w, h: (w, h)),
        ],
        out_shape=[
            jax.ShapeDtypeStruct((wins, 2 * pairs, rows, rows), jnp.bfloat16),
            jax.ShapeDtypeStruct((wins * rows, feature), jnp.bfloat16),
        ],
        name="attend",
    )(mixed, mixed, mixed, table, shift, key_cells)


def attend_back(mixed, probs, grad_att, table, shift, key_cells, feature):
    rows, pairs = shift.shape[0], feature // 128
    wins = mixed.shape[0] // rows
    whole = lambda shape: pl.BlockSpec(shape, lambda w, h: (0,) * len(shape))
    column = lambda base: pl.BlockSpec((rows, 128), lambda w, h: (w, base * pairs + h))
    flat = jax.ShapeDtypeStruct((wins * rows, feature), jnp.bfloat16)
    return pl.pallas_call(
        attend_back_kernel,
        grid=(wins, pairs),
        in_specs=[
            column(0), column(1), column(2),
            pl.BlockSpec((1, 2, rows, rows), lambda w, h: (w, h, 0, 0)),
            column(0),
            whole((HD, 128)), whole((rows, 128)), whole((rows, 128)),
        ],
        out_specs=[column(0), column(0), column(0), whole((HD, 128))],
        out_shape=[flat, flat, flat, jax.ShapeDtypeStruct((HD, 128), jnp.float32)],
        name="attend_back",
    )(mixed, mixed, mixed, probs, grad_att, table, shift, key_cells)


def dot_last(left, right):
    return lax.dot_general(left, right, (((1,), (1,)), ((), ())), preferred_element_type=jnp.float32)


def dot_first(left, right):
    return lax.dot_general(left, right, (((0,), (0,)), ((), ())), preferred_element_type=jnp.float32)


ORDERS = (("y", "x", "near"), ("x", "near", "y"), ("near", "y", "x"))


def halves(wide_size, group_size):
    return (wide_size, group_size) == (16, 2)


def pack_kernel(
    n1_ref, dq_ref, dk_ref, dv_ref, att_ref, dproj_ref, n2_ref, dpre_ref, act_ref, dout_ref, tail_ref,
    *refs, part_rows, share_rows, group_size, wide_size, cuts, relative,
):
    *out_refs, rows_ref, stage_ref, bias_ref, stage_sems = refs
    kept_refs, sent_refs = out_refs[: len(cuts)], out_refs[len(cuts) :]
    count = n1_ref.shape[0]
    ones = jnp.ones((16, count), jnp.bfloat16)

    def weight(base, left_ref, right_refs):
        width = sum(ref.shape[1] for ref in right_refs) // 128

        def block(f, carry):
            left = left_ref[:, pl.ds(pl.multiple_of(f * 128, 128), 128)]
            column = 0
            for ref in right_refs:
                product = dot_first(left, ref[...])
                for j in range(ref.shape[1] // 128):
                    rows_ref[pl.ds(base + f * 128 * width + column, 128, stride=width), :] = product[
                        :, j * 128 : (j + 1) * 128
                    ]
                    column += 1
            return carry

        lax.fori_loop(0, left_ref.shape[1] // 128, block, 0)
        return base + left_ref.shape[1] * width

    def bias(base, ref):
        total = jnp.dot(ones, ref[...], preferred_element_type=jnp.float32)
        for j in range(ref.shape[1] // 128):
            rows_ref[base + j : base + j + 1, :] = total[0:1, j * 128 : (j + 1) * 128]
        return base + ref.shape[1] // 128

    share = share_rows // wide_size
    own_wide = lax.axis_index("wide")
    own_group = lax.axis_index("grp")
    chunks = []
    for owner in range(group_size):
        for place in range(wide_size):
            low = place * share
            size = max(0, min(share, part_rows - low))
            chunks.append((owner, place, owner * part_rows + low, size))
    flying = {}
    sent = 0
    bias_known = False

    def pieces(slot, owner, place):
        if not relative:
            return [(stage_ref.at[slot], kept_refs[0].at[owner, place], None)]
        flips = place ^ own_wide
        flip = {
            "y": owner ^ own_group,
            "x": (flips >> 1) & 1,
            "near": (flips >> 2) & 1,
            "far": (flips >> 3) & 1,
        }
        found = []
        for (low, high), order, kept_ref, sent_ref in zip(cuts, ORDERS, kept_refs, sent_refs):
            spot = tuple(flip[name] for name in order + ("far",))
            source = stage_ref.at[slot, pl.ds(low, high - low), :]
            found.append((source, kept_ref.at[spot], sent_ref.at[spot]))
        return found

    def launch(slot, owner, place):
        for source, kept, other in pieces(slot, owner, place):

            def start(target, source=source):
                pltpu.make_async_copy(source, target, stage_sems.at[slot]).start()

            if other is None:
                start(kept)
            else:
                other_core = ((place ^ own_wide) & 1) == 1
                pl.when(other_core)(functools.partial(start, other))
                pl.when(jnp.logical_not(other_core))(functools.partial(start, kept))

    def finish(slot):
        if slot in flying:
            for source, kept, _ in pieces(slot, *flying.pop(slot)):
                pltpu.make_async_copy(source, kept, stage_sems.at[slot]).wait()

    def emit(upto):
        nonlocal sent
        while sent < len(chunks) and chunks[sent][2] + chunks[sent][3] <= upto:
            if chunks[sent][3] < share and not bias_known:
                break
            owner, place, source, size = chunks[sent]
            slot = sent % 2
            finish(slot)

            def convert(at, count, source=source, slot=slot):
                stage_ref[slot, pl.ds(at, count), :] = rows_ref[
                    pl.ds(pl.multiple_of(source + at, 16), count), :
                ].astype(jnp.bfloat16)

            def convert_block(i, carry, convert=convert):
                convert(pl.multiple_of(i * 128, 128), 128)
                return carry

            lax.fori_loop(0, size // 128, convert_block, 0)
            if size % 128:
                convert(size - size % 128, size % 128)
            if size < share:
                bias_place = part_rows - place * share
                first = max(0, -bias_place)
                stage_ref[slot, size:share, :] = bias_ref[first : first + share - size, :]
            launch(slot, owner, place)
            flying[slot] = (owner, place)
            sent += 1

    row = weight(0, n1_ref, [dq_ref, dk_ref, dv_ref])
    row = bias(row, dq_ref)
    row = bias(row, dv_ref)
    emit(row)
    row = weight(row, att_ref, [dproj_ref])
    proj_bias = row
    row = bias(row, dproj_ref)
    bias_size = dproj_ref.shape[1] // 128
    spare = share_rows - part_rows
    bias_ref[...] = jnp.concatenate(
        [
            rows_ref[proj_bias : proj_bias + bias_size, :],
            jnp.zeros((spare - bias_size, 128), jnp.float32),
        ],
        0,
    ).astype(jnp.bfloat16)
    bias_known = True
    emit(row)
    row = weight(row, n2_ref, [dpre_ref])
    row = bias(row, dpre_ref)
    emit(row)
    row = weight(row, act_ref, [dout_ref])
    row = bias(row, dout_ref)
    emit(row)
    rows_ref[row : row + tail_ref.shape[0], :] = tail_ref[...]
    emit(group_size * part_rows)
    for slot in range(2):
        finish(slot)


def pack_shares(factors, tail, part_rows, group_size, wide_size):
    feature = factors[0].shape[1]
    grain = 16 * wide_size
    share_rows = -(-(part_rows + feature // 128) // grain) * grain
    spare = share_rows - part_rows
    share = share_rows // wide_size
    relative = halves(wide_size, group_size)
    whole = pl.BlockSpec(memory_space=pltpu.VMEM)
    if relative:
        units = share // 16
        ends = [0, (units + 2) // 3 * 16, ((units + 2) // 3 + (units + 1) // 3) * 16, share]
        cuts = tuple(zip(ends, ends[1:]))
        shapes = [(2, 2, 2, 2, high - low, 128) for low, high in cuts] * 2
    else:
        cuts = ((0, share),)
        shapes = [(group_size, wide_size, share, 128)]
    return pl.pallas_call(
        functools.partial(
            pack_kernel,
            part_rows=part_rows,
            share_rows=share_rows,
            group_size=group_size,
            wide_size=wide_size,
            cuts=cuts,
            relative=relative,
        ),
        in_specs=[whole] * (len(factors) + 1),
        out_specs=[pl.BlockSpec(memory_space=pl.ANY)] * len(shapes),
        out_shape=[jax.ShapeDtypeStruct(shape, jnp.bfloat16) for shape in shapes],
        scratch_shapes=[
            pltpu.VMEM((group_size * part_rows, 128), jnp.float32),
            pltpu.VMEM((2, share, 128), jnp.bfloat16),
            pltpu.VMEM((spare, 128), jnp.bfloat16),
            pltpu.SemaphoreType.DMA((2,)),
        ],
        compiler_params=pltpu.CompilerParams(vmem_limit_bytes=60 * 1024 * 1024),
        name="pack_grads",
    )(*factors, tail)


def gelu_slope(pre_act):
    normal_cdf = 0.5 * (1.0 + jax.scipy.special.erf(pre_act / math.sqrt(2.0)))
    return normal_cdf + pre_act * jnp.exp(-0.5 * pre_act * pre_act) / math.sqrt(2.0 * math.pi)


def window_pass(tokens, cotangent, keep_mask, weights):
    (
        qkv_w,
        qv_b,
        proj_w,
        proj_b,
        fc1_w,
        fc1_b,
        fc2_w,
        fc2_b,
        ln1_g,
        ln1_b,
        ln2_g,
        ln2_b,
        table_h,
        table_w,
    ) = weights
    win_count, tok_count, feature = tokens.shape
    row_count = win_count * tok_count
    inputs = tokens.reshape(row_count, feature).astype(jnp.float32)
    keep_rows = keep_mask.reshape(row_count, 1)
    hat_one, scale_one = normalize(inputs)
    normed_one = (
        (hat_one * ln1_g.astype(jnp.float32) + ln1_b.astype(jnp.float32)) * keep_rows
    ).astype(jnp.bfloat16)
    bias_full = jnp.concatenate(
        [qv_b[:feature], jnp.zeros((feature,), jnp.bfloat16), qv_b[feature:]]
    ).astype(jnp.float32)
    mixed = (jnp.dot(normed_one, qkv_w, preferred_element_type=jnp.float32) + bias_full).astype(
        jnp.bfloat16
    )
    shift, key_cells = window_constants(tok_count)
    table = wide_table(table_h, table_w)
    probs, attended = attend(mixed, table, shift, key_cells, feature)
    resid = keep_rows * (
        inputs
        + jnp.dot(attended, proj_w, preferred_element_type=jnp.float32)
        + proj_b.astype(jnp.float32)
    )
    hat_two, scale_two = normalize(resid)
    normed_two = (hat_two * ln2_g.astype(jnp.float32) + ln2_b.astype(jnp.float32)).astype(
        jnp.bfloat16
    )
    pre_act = jnp.dot(normed_two, fc1_w, preferred_element_type=jnp.float32) + fc1_b.astype(
        jnp.float32
    )
    activation = jax.nn.gelu(pre_act, approximate=False).astype(jnp.bfloat16)
    result = keep_rows * (
        resid
        + jnp.dot(activation, fc2_w, preferred_element_type=jnp.float32)
        + fc2_b.astype(jnp.float32)
    )
    cot_rows = cotangent.reshape(row_count, feature).astype(jnp.float32) * keep_rows
    grad_out = cot_rows.astype(jnp.bfloat16)
    grad_act = jnp.einsum("nd,fd->nf", grad_out, fc2_w, preferred_element_type=jnp.float32)
    grad_pre = (grad_act * gelu_slope(pre_act)).astype(jnp.bfloat16)
    grad_norm_two = jnp.einsum("nf,df->nd", grad_pre, fc1_w, preferred_element_type=jnp.float32)
    grad_ln2_g = jnp.sum(grad_norm_two * hat_two, 0)
    grad_ln2_b = jnp.sum(grad_norm_two, 0)
    grad_resid = cot_rows + norm_back(grad_norm_two * ln2_g.astype(jnp.float32), hat_two, scale_two)
    grad_branch = keep_rows * grad_resid
    grad_proj = grad_branch.astype(jnp.bfloat16)
    grad_att = jnp.einsum(
        "ne,de->nd", grad_proj, proj_w, preferred_element_type=jnp.float32
    ).astype(jnp.bfloat16)
    grad_query, grad_keys, grad_values, grad_table = attend_back(
        mixed, probs, grad_att, table, shift, key_cells, feature
    )
    rel_span = table_h.shape[0]
    grad_table_h = grad_table[:, :rel_span].T[::-1]
    grad_table_w = grad_table[:, 64 : 64 + rel_span].T[::-1]
    grad_mixed = jnp.concatenate([grad_query, grad_keys, grad_values], -1)
    grad_norm_one = keep_rows * jnp.einsum(
        "nf,df->nd", grad_mixed, qkv_w, preferred_element_type=jnp.float32
    )
    grad_ln1_g = jnp.sum(grad_norm_one * hat_one, 0)
    grad_ln1_b = jnp.sum(grad_norm_one, 0)
    grad_input = grad_branch + norm_back(
        grad_norm_one * ln1_g.astype(jnp.float32), hat_one, scale_one
    )
    factors = (
        normed_one,
        grad_query,
        grad_keys,
        grad_values,
        attended,
        grad_proj,
        normed_two,
        grad_pre,
        activation,
        grad_out,
    )
    tail = (grad_ln1_g, grad_ln1_b, grad_ln2_g, grad_ln2_b, grad_table_h, grad_table_w)
    block_part = result.reshape(win_count, tok_count, feature).astype(jnp.bfloat16)
    input_part = grad_input.reshape(win_count, tok_count, feature).astype(jnp.bfloat16)
    return (block_part, input_part, factors, tail)


def swap(values, axis, bit):
    return lax.ppermute(values, axis, [(i, i ^ bit) for i in range(lax.axis_size(axis))])


def wide_bits(count):
    place = lax.axis_index("wide")
    return [(place >> bit) & 1 for bit in range(count)]


def splits(part_rows):
    return lax.axis_size("grp") == 2 and lax.axis_size("wide") % 8 == 0 and part_rows % 64 == 0


def eighth_index(core, cross, deep):
    return (core * 2 + cross) * 2 + deep


def gather_groups(mine, diagonal, finish):
    core, cross, deep = wide_bits(3)
    first = swap(mine, "grp", 1)
    diagonal, first = lax.optimization_barrier((diagonal, first))
    last = swap(diagonal, "grp", 1)
    side = swap(first, "wide", 2)
    back = swap(first, "wide", 4)
    near = (first, side, back, last)
    far = [swap(part, "wide", 1) for part in near]
    group = lax.axis_index("grp")
    out = finish(first)
    rows = out.shape[0] * out.shape[1]
    out = out.reshape((2, 8) + mine.shape)
    for parts, which in ((near, core), (far, 1 - core)):
        for part, flip_cross, flip_deep in zip(parts, (0, 1, 0, 1), (0, 0, 1, 1)):
            at = eighth_index(which, cross ^ flip_cross, deep ^ flip_deep)
            out = lax.dynamic_update_slice(out, part[None, None], (1 - group, at, 0, 0))
    return out.reshape(rows, 128)


def joined(kept, sent):
    return (kept.astype(jnp.float32) + sent.astype(jnp.float32)).astype(kept.dtype)


def reduce_shares(packed):
    if len(packed) == 1:
        rows = packed[0].reshape(-1, 128)
        return lax.psum_scatter(rows, ("grp", "wide"), scatter_dimension=0, tiled=True)
    moves = {
        "x": lambda v: swap(v, "wide", 2),
        "near": lambda v: swap(v, "wide", 4),
        "far": lambda v: swap(v, "wide", 8),
        "y": lambda v: swap(v, "grp", 1),
    }
    done = []
    for kept, sent, order in zip(packed[:3], packed[3:], ORDERS):
        arrived = swap(sent, "wide", 1)
        for name in order + ("far",):
            leaving = joined(kept[1], arrived[1])
            kept = joined(kept[0], arrived[0])
            arrived = moves[name](leaving)
        done.append(joined(kept, arrived))
    return jnp.concatenate(done, 0)


def own_eighths(rows):
    core, cross, deep = wide_bits(3)
    parts = rows.reshape(8, -1, 128)
    spots = (eighth_index(core, cross, deep), eighth_index(core, 1 - cross, 1 - deep))
    return [lax.dynamic_index_in_dim(parts, spot, keepdims=False) for spot in spots]


def first_step(grads, first_moment):
    return BETA_ONE * first_moment + (1.0 - BETA_ONE) * grads


def second_step(grads, master, moment_next, second_moment):
    second_next = BETA_TWO * second_moment + (1.0 - BETA_TWO) * grads * grads
    fix_one = 1.0 - BETA_ONE**ADAM_STEP
    fix_two = 1.0 - BETA_TWO**ADAM_STEP
    update = (
        moment_next / fix_one / (jnp.sqrt(second_next / fix_two) + ADAM_EPS) + DECAY_RATE * master
    )
    return (master - LEARN_RATE * update, second_next)


BLOCK_ROWS = 1024


def place_kernel(group_ref, master_ref, out_ref):
    out_ref[0] = master_ref[...].astype(jnp.bfloat16)


def place_own(master):
    rows = master.shape[0]
    return pl.pallas_call(
        place_kernel,
        grid_spec=pltpu.PrefetchScalarGridSpec(
            num_scalar_prefetch=1,
            grid=(pl.cdiv(rows, BLOCK_ROWS),),
            in_specs=[pl.BlockSpec((BLOCK_ROWS, 128), lambda i, g: (i, 0))],
            out_specs=pl.BlockSpec((1, BLOCK_ROWS, 128), lambda i, g: (g[0], i, 0)),
        ),
        out_shape=jax.ShapeDtypeStruct((2, rows, 128), jnp.bfloat16),
        name="place_own",
    )(lax.axis_index("grp").reshape(1), master)


def eighth_kernel(spot_ref, total_ref, master_ref, first_ref, second_ref, out_ref, *, factor):
    grads = total_ref[...].astype(jnp.float32) * factor
    moment = first_step(grads, first_ref[...])
    out_ref[0] = second_step(grads, master_ref[...], moment, second_ref[...])[0].astype(jnp.bfloat16)


def eighth_weights(totals, state, factor):
    size = state[0].shape[0] // 8
    core, cross, deep = wide_bits(3)
    spots = (eighth_index(core, cross, deep), eighth_index(core, 1 - cross, 1 - deep))
    both = pl.pallas_call(
        functools.partial(eighth_kernel, factor=factor),
        grid_spec=pltpu.PrefetchScalarGridSpec(
            num_scalar_prefetch=1,
            grid=(2,),
            in_specs=[pl.BlockSpec((size, 128), lambda i, spot: (spot[i], 0))] * 4,
            out_specs=pl.BlockSpec((1, size, 128), lambda i, spot: (i, 0, 0)),
        ),
        out_shape=jax.ShapeDtypeStruct((2, size, 128), jnp.bfloat16),
        name="eighth_weights",
    )(jnp.stack(spots).astype(jnp.int32), totals, *state)
    return both[0], both[1]


def adam_kernel(group_ref, total_ref, master_ref, first_ref, second_ref, *refs, factor):
    grads_ref, master_out, first_out, second_out, weights_ref = refs[-5:]
    grads = total_ref[...].astype(jnp.float32) * factor
    moment = first_step(grads, first_ref[...])
    master_next, second_next = second_step(grads, master_ref[...], moment, second_ref[...])
    grads_ref[...] = grads
    master_out[...] = master_next
    first_out[...] = moment
    second_out[...] = second_next
    weights_ref[0] = master_next.astype(jnp.bfloat16)


def adam_rows(totals, state, factor, first_block, last_block, onto, after):
    rows = state[0].shape[0]
    row_spec = pl.BlockSpec((BLOCK_ROWS, 128), lambda i, g: (first_block + i, 0))
    anywhere = pl.BlockSpec(memory_space=pl.ANY)
    wide = jax.ShapeDtypeStruct((rows, 128), jnp.float32)
    spare = 5 - len(onto)
    return pl.pallas_call(
        functools.partial(adam_kernel, factor=factor),
        grid_spec=pltpu.PrefetchScalarGridSpec(
            num_scalar_prefetch=1,
            grid=(last_block - first_block,),
            in_specs=[row_spec] * 4 + [anywhere] * (len(onto) + len(after)),
            out_specs=[row_spec] * 4
            + [pl.BlockSpec((1, BLOCK_ROWS, 128), lambda i, g: (g[0], first_block + i, 0))],
        ),
        out_shape=[wide] * 4 + [jax.ShapeDtypeStruct((2, rows, 128), jnp.bfloat16)],
        input_output_aliases={5 + i: spare + i for i in range(len(onto))},
        name="adam_rows",
    )(lax.axis_index("grp").reshape(1), totals, *state, *onto, *after)


def body(tokens, cotangent, window_place, master, first_moment, second_moment):
    part_rows = master.shape[0]
    wide_size = lax.axis_size("wide")
    group_size = lax.axis_size("grp")
    feature = tokens.shape[-1]
    micro_count, slots, tok_count, _ = tokens.shape
    masks = token_mask(window_place)
    if splits(part_rows):
        mine, diagonal = (part.astype(jnp.bfloat16) for part in own_eighths(master))
        gathered = gather_groups(mine, diagonal, lambda first: place_own(master))
    else:
        gathered = lax.all_gather(master.astype(jnp.bfloat16), "grp", axis=0, tiled=True)
    weights = unpack(gathered, feature)
    wins = micro_count * slots
    extra = -tok_count % 16

    def padded(values):
        values = values.reshape((wins,) + values.shape[2:])
        return jnp.pad(values, ((0, 0), (0, extra)) + ((0, 0),) * (values.ndim - 2))

    block_part, input_part, factors, tail = window_pass(
        padded(tokens), padded(cotangent), padded(masks), weights
    )
    filled = sum(math.prod(dims_of) for dims_of in layout(feature)[:8]) // 128
    tail = jnp.concatenate([member.reshape(-1) for member in tail])
    tail_rows = part_rows * group_size - filled
    tail = jnp.pad(tail, (0, tail_rows * 128 - tail.shape[0])).reshape(tail_rows, 128)
    packed = pack_shares(factors, tail, part_rows, group_size, wide_size)
    owned = reduce_shares(packed)
    totals = lax.all_gather(owned, "wide", axis=0, tiled=True)
    factor = 1.0 / (micro_count * wide_size * group_size)
    bias_total = totals[part_rows : part_rows + feature // 128]
    proj_bias_grad = bias_total.astype(jnp.float32).reshape(-1) * factor
    state = (master, first_moment, second_moment)
    if splits(part_rows):
        updated = []

        def finish(first):
            blocks = pl.cdiv(part_rows, BLOCK_ROWS)
            half = blocks // 2
            held = gathered.reshape(2, part_rows, 128)
            begun = adam_rows(totals, state, factor, 0, half, (held,), ())
            updated.extend(adam_rows(totals, state, factor, half, blocks, begun, (first,)))
            return updated.pop()

        mine, diagonal = eighth_weights(totals, state, factor)
        weights_next = gather_groups(mine, diagonal, finish)
        grads, master_next, moment_next, second_next = updated
    else:
        grads = totals[:part_rows].astype(jnp.float32) * factor
        moment_next = first_step(grads, first_moment)
        master_next, second_next = second_step(grads, master, moment_next, second_moment)
        own_weights = master_next.astype(jnp.bfloat16)
        weights_next = lax.all_gather(own_weights, "grp", axis=0, tiled=True)
    block_out = block_part[:, :tok_count].reshape(tokens.shape)
    input_grad = input_part[:, :tok_count].reshape(tokens.shape)
    return (
        block_out,
        input_grad,
        grads,
        master_next,
        moment_next,
        second_next,
        weights_next,
        proj_bias_grad,
    )


def solution(mesh):
    return jax.shard_map(
        body,
        mesh=mesh,
        in_specs=(
            P(None, ("wide", "grp"), None, None),
            P(None, ("wide", "grp"), None, None),
            P(None, ("wide", "grp")),
            P("grp", None),
            P("grp", None),
            P("grp", None),
        ),
        out_specs=(
            P(None, ("wide", "grp"), None, None),
            P(None, ("wide", "grp"), None, None),
            P("grp", None),
            P("grp", None),
            P("grp", None),
            P("grp", None),
            P(),
            P(),
        ),
        check_vma=False,
    )
```

```python
import functools
import math

import jax
import jax.numpy as jnp
from jax import lax
from jax.experimental import pallas as pl
from jax.experimental.pallas import tpu as pltpu
from jax.sharding import PartitionSpec as P

FF = 3072
HD = 64
WS = 14
GRID = 64
ADAM_STEP = 10


EPS_NORM = 1e-06
BETA_ONE = 0.9
BETA_TWO = 0.95
ADAM_EPS = 1e-08
LEARN_RATE = 0.02
DECAY_RATE = 0.1


def layout(feature):
    rel_span = 2 * WS - 1
    return [
        (feature, 3 * feature),
        (2 * feature,),
        (feature, feature),
        (feature,),
        (feature, FF),
        (FF,),
        (FF, feature),
        (feature,),
        (feature,),
        (feature,),
        (feature,),
        (feature,),
        (rel_span, HD),
        (rel_span, HD),
    ]


CHUNK = 2304


def unpack_kernel(rows_ref, *refs, plan):
    *out_refs, raw_ref, wide_ref, sems = refs
    step = pl.program_id(0)
    limit = raw_ref.shape[1]
    total = sum(count for _, count, _ in plan)

    def chunk_copy(index, slot):
        start = jnp.int32(0)
        before = 0
        for row, count, _ in plan:
            at = row // 16 * 16 + (index - before) * CHUNK
            start = jnp.where(index >= before, at, start)
            before += count
        return pltpu.make_async_copy(
            rows_ref.at[pl.ds(pl.multiple_of(start, 16), limit), :], raw_ref.at[slot], sems.at[slot]
        )

    slot = lax.rem(step, 2)

    @pl.when(step == 0)
    def _():
        chunk_copy(step, slot).start()

    @pl.when(step + 1 < total)
    def _():
        chunk_copy(step + 1, 1 - slot).start()

    chunk_copy(step, slot).wait()
    part = limit // 5

    def widen(i, carry):
        at = pl.multiple_of(i * part, 16)
        wide_ref[pl.ds(at, part), :] = raw_ref[slot, pl.ds(at, part), :].astype(jnp.float32)
        return carry

    lax.fori_loop(0, 5, widen, 0)
    before = 0
    for (row, count, width), out_ref in zip(plan, out_refs):

        @pl.when((step >= before) & (step < before + count))
        def _(row=row, width=width, out_ref=out_ref):
            for j in range(width):
                picked = wide_ref[pl.ds(row % 16 + j, CHUNK // width, stride=width), :]
                out_ref[:, j * 128 : (j + 1) * 128] = picked.astype(jnp.bfloat16)

        before += count


def unpack_matrices(rows, dims, starts):
    plan = tuple(
        (start, math.prod(dims_of) // 128 // CHUNK, dims_of[1] // 128)
        for start, dims_of in zip(starts, dims)
    )
    specs = []
    before = 0
    for (_, count, width), dims_of in zip(plan, dims):

        def place(i, before=before, count=count):
            return (jnp.clip(i - before, 0, count - 1), 0)

        specs.append(pl.BlockSpec((CHUNK // width, dims_of[1]), place))
        before += count
    return pl.pallas_call(
        functools.partial(unpack_kernel, plan=plan),
        grid=(before,),
        in_specs=[pl.BlockSpec(memory_space=pl.ANY)],
        out_specs=specs,
        out_shape=[jax.ShapeDtypeStruct(dims_of, jnp.bfloat16) for dims_of in dims],
        scratch_shapes=[
            pltpu.VMEM((2, CHUNK + 16, 128), jnp.bfloat16),
            pltpu.VMEM((CHUNK + 16, 128), jnp.float32),
            pltpu.SemaphoreType.DMA((2,)),
        ],
        name="unpack_matrices",
    )(rows)


def unpack(rows, feature):
    dims = layout(feature)
    starts = []
    row = 0
    for dims_of in dims[:8]:
        starts.append(row)
        row = row + math.prod(dims_of) // 128
    matrices = unpack_matrices(rows, dims[:8:2], starts[:8:2])
    members = []
    for index, dims_of in enumerate(dims[:8]):
        if index % 2 == 0:
            members.append(matrices[index // 2])
        else:
            start = starts[index]
            members.append(rows[start : start + dims_of[0] // 128].reshape(dims_of))
    tail_size = sum(math.prod(dims_of) for dims_of in dims[8:])
    tail = rows[row : row - (-tail_size // 128)].reshape(-1)
    offset = 0
    for dims_of in dims[8:]:
        length = math.prod(dims_of)
        members.append(tail[offset : offset + length].reshape(dims_of))
        offset = offset + length
    return tuple(members)


def token_mask(window_place):
    cells = jnp.arange(WS * WS, dtype=jnp.int32)
    inner_row = cells // WS
    inner_col = cells % WS
    places = window_place[..., None]
    live_slot = places < 25
    row_real = WS * (places // 5) + inner_row < GRID
    col_real = WS * (places % 5) + inner_col < GRID
    return jnp.where(live_slot & row_real & col_real, 1.0, 0.0).astype(jnp.float32)


def normalize(inputs):
    row_mean = jnp.mean(inputs, -1, keepdims=True)
    centred = inputs - row_mean
    inv_scale = lax.rsqrt(jnp.mean(centred * centred, -1, keepdims=True) + EPS_NORM)
    return (centred * inv_scale, inv_scale)


def norm_back(grad_hat, normed_hat, inv_scale):
    first_mean = jnp.mean(grad_hat, -1, keepdims=True)
    second_mean = jnp.mean(grad_hat * normed_hat, -1, keepdims=True)
    return inv_scale * (grad_hat - first_mean - normed_hat * second_mean)


def attend_kernel(q_ref, k_ref, v_ref, table_ref, shift_ref, key_ref, probs_ref, out_ref):
    shift = shift_ref[...]
    key_cells = key_ref[...]
    row_count = shift.shape[0]
    real_key = lax.broadcasted_iota(jnp.int32, (row_count, row_count), 1) < WS * WS
    for part in range(2):
        cut = slice(part * HD, (part + 1) * HD)
        queries = q_ref[:, cut]
        along = jnp.dot(queries, table_ref[...], preferred_element_type=jnp.float32)
        for bit in (1, 2, 4, 8):
            along = jnp.where((shift & bit) != 0, pltpu.roll(along, 128 - bit, 1), along)
        high = along.astype(jnp.bfloat16)
        low = (along - high.astype(jnp.float32)).astype(jnp.bfloat16)
        scores = dot_last(queries, k_ref[:, cut]) * (1.0 / math.sqrt(HD))
        scores = scores + dot_last(high, key_cells) + dot_last(low, key_cells)
        scores = jnp.where(real_key, scores, -1e30)
        powers = jnp.exp(scores - jnp.max(scores, -1, keepdims=True))
        probs = (powers / jnp.sum(powers, -1, keepdims=True)).astype(jnp.bfloat16)
        probs_ref[0, part] = probs
        out_ref[:, cut] = jnp.dot(
            probs, v_ref[:, cut], preferred_element_type=jnp.float32
        ).astype(jnp.bfloat16)


def attend_back_kernel(
    q_ref, k_ref, v_ref, probs_ref, grad_ref, table_ref, shift_ref, key_ref,
    dq_ref, dk_ref, dv_ref, dtable_ref,
):
    shift = shift_ref[...]
    key_cells = key_ref[...]
    scale = 1.0 / math.sqrt(HD)

    @pl.when((pl.program_id(0) == 0) & (pl.program_id(1) == 0))
    def _():
        dtable_ref[...] = jnp.zeros(dtable_ref.shape, jnp.float32)

    for part in range(2):
        cut = slice(part * HD, (part + 1) * HD)
        queries = q_ref[:, cut]
        grad = grad_ref[:, cut]
        probs = probs_ref[0, part]
        dv_ref[:, cut] = dot_first(probs, grad).astype(jnp.bfloat16)
        grad_probs = dot_last(grad, v_ref[:, cut])
        wide_probs = probs.astype(jnp.float32)
        inner = jnp.sum(wide_probs * grad_probs, -1, keepdims=True)
        grad_scores = (wide_probs * (grad_probs - inner)).astype(jnp.bfloat16)
        dk_ref[:, cut] = (dot_first(grad_scores, queries) * scale).astype(jnp.bfloat16)
        along = jnp.dot(grad_scores, key_cells, preferred_element_type=jnp.float32)
        for bit in (1, 2, 4, 8):
            along = jnp.where((shift & bit) != 0, pltpu.roll(along, bit, 1), along)
        high = along.astype(jnp.bfloat16)
        low = (along - high.astype(jnp.float32)).astype(jnp.bfloat16)
        grad_query = jnp.dot(grad_scores, k_ref[:, cut], preferred_element_type=jnp.float32) * scale
        grad_query = grad_query + dot_last(high, table_ref[...]) + dot_last(low, table_ref[...])
        dq_ref[:, cut] = grad_query.astype(jnp.bfloat16)
        dtable_ref[...] += dot_first(queries, high) + dot_first(queries, low)


def window_constants(row_count):
    cells = jnp.arange(row_count, dtype=jnp.int32)[:, None]
    lanes = jnp.arange(128, dtype=jnp.int32)[None, :]
    first = lanes < 64
    shift = jnp.where(first, WS - 1 - cells // WS, WS - 1 - cells % WS)
    live = cells < WS * WS
    shift = jnp.where(live, shift, 0)
    offset = jnp.where(first, lanes, lanes - 64)
    place = jnp.where(first, cells // WS, cells % WS)
    key_cells = jnp.where(live & (offset == place), 1.0, 0.0).astype(jnp.bfloat16)
    return shift, key_cells


def wide_table(table_h, table_w):
    pad = jnp.zeros((HD, 64 - table_h.shape[0]), table_h.dtype)
    return jnp.concatenate([table_h[::-1].T, pad, table_w[::-1].T, pad], 1)


def attend(mixed, table, shift, key_cells, feature):
    rows, pairs = shift.shape[0], feature // 128
    wins = mixed.shape[0] // rows
    whole = lambda shape: pl.BlockSpec(shape, lambda w, h: (0,) * len(shape))
    column = lambda base: pl.BlockSpec((rows, 128), lambda w, h: (w, base * pairs + h))
    return pl.pallas_call(
        attend_kernel,
        grid=(wins, pairs),
        in_specs=[column(0), column(1), column(2), whole((HD, 128)), whole((rows, 128)), whole((rows, 128))],
        out_specs=[
            pl.BlockSpec((1, 2, rows, rows), lambda w, h: (w, h, 0, 0)),
            pl.BlockSpec((rows, 128), lambda w, h: (w, h)),
        ],
        out_shape=[
            jax.ShapeDtypeStruct((wins, 2 * pairs, rows, rows), jnp.bfloat16),
            jax.ShapeDtypeStruct((wins * rows, feature), jnp.bfloat16),
        ],
        name="attend",
    )(mixed, mixed, mixed, table, shift, key_cells)


def attend_back(mixed, probs, grad_att, table, shift, key_cells, feature):
    rows, pairs = shift.shape[0], feature // 128
    wins = mixed.shape[0] // rows
    whole = lambda shape: pl.BlockSpec(shape, lambda w, h: (0,) * len(shape))
    column = lambda base: pl.BlockSpec((rows, 128), lambda w, h: (w, base * pairs + h))
    flat = jax.ShapeDtypeStruct((wins * rows, feature), jnp.bfloat16)
    return pl.pallas_call(
        attend_back_kernel,
        grid=(wins, pairs),
        in_specs=[
            column(0), column(1), column(2),
            pl.BlockSpec((1, 2, rows, rows), lambda w, h: (w, h, 0, 0)),
            column(0),
            whole((HD, 128)), whole((rows, 128)), whole((rows, 128)),
        ],
        out_specs=[column(0), column(0), column(0), whole((HD, 128))],
        out_shape=[flat, flat, flat, jax.ShapeDtypeStruct((HD, 128), jnp.float32)],
        name="attend_back",
    )(mixed, mixed, mixed, probs, grad_att, table, shift, key_cells)


def dot_last(left, right):
    return lax.dot_general(left, right, (((1,), (1,)), ((), ())), preferred_element_type=jnp.float32)


def dot_first(left, right):
    return lax.dot_general(left, right, (((0,), (0,)), ((), ())), preferred_element_type=jnp.float32)


ORDERS = (("y", "x", "near"), ("x", "near", "y"), ("near", "y", "x"))


def halves(wide_size, group_size):
    return (wide_size, group_size) == (16, 2)


def pack_kernel(
    n1_ref, dq_ref, dk_ref, dv_ref, att_ref, dproj_ref, n2_ref, dpre_ref, act_ref, dout_ref, tail_ref,
    *refs, part_rows, share_rows, group_size, wide_size, cuts, relative,
):
    *out_refs, rows_ref, stage_ref, bias_ref, stage_sems = refs
    kept_refs, sent_refs = out_refs[: len(cuts)], out_refs[len(cuts) :]
    count = n1_ref.shape[0]
    ones = jnp.ones((16, count), jnp.bfloat16)

    def weight(base, left_ref, right_refs):
        width = sum(ref.shape[1] for ref in right_refs) // 128

        def block(f, carry):
            left = left_ref[:, pl.ds(pl.multiple_of(f * 128, 128), 128)]
            column = 0
            for ref in right_refs:
                product = dot_first(left, ref[...])
                for j in range(ref.shape[1] // 128):
                    rows_ref[pl.ds(base + f * 128 * width + column, 128, stride=width), :] = product[
                        :, j * 128 : (j + 1) * 128
                    ]
                    column += 1
            return carry

        lax.fori_loop(0, left_ref.shape[1] // 128, block, 0)
        return base + left_ref.shape[1] * width

    def bias(base, ref):
        total = jnp.dot(ones, ref[...], preferred_element_type=jnp.float32)
        for j in range(ref.shape[1] // 128):
            rows_ref[base + j : base + j + 1, :] = total[0:1, j * 128 : (j + 1) * 128]
        return base + ref.shape[1] // 128

    share = share_rows // wide_size
    own_wide = lax.axis_index("wide")
    own_group = lax.axis_index("grp")
    chunks = []
    for owner in range(group_size):
        for place in range(wide_size):
            low = place * share
            size = max(0, min(share, part_rows - low))
            chunks.append((owner, place, owner * part_rows + low, size))
    flying = {}
    sent = 0
    bias_known = False

    def pieces(slot, owner, place):
        if not relative:
            return [(stage_ref.at[slot], kept_refs[0].at[owner, place], None)]
        flips = place ^ own_wide
        flip = {
            "y": owner ^ own_group,
            "x": (flips >> 1) & 1,
            "near": (flips >> 2) & 1,
            "far": (flips >> 3) & 1,
        }
        found = []
        for (low, high), order, kept_ref, sent_ref in zip(cuts, ORDERS, kept_refs, sent_refs):
            spot = tuple(flip[name] for name in order + ("far",))
            source = stage_ref.at[slot, pl.ds(low, high - low), :]
            found.append((source, kept_ref.at[spot], sent_ref.at[spot]))
        return found

    def launch(slot, owner, place):
        for source, kept, other in pieces(slot, owner, place):

            def start(target, source=source):
                pltpu.make_async_copy(source, target, stage_sems.at[slot]).start()

            if other is None:
                start(kept)
            else:
                other_core = ((place ^ own_wide) & 1) == 1
                pl.when(other_core)(functools.partial(start, other))
                pl.when(jnp.logical_not(other_core))(functools.partial(start, kept))

    def finish(slot):
        if slot in flying:
            for source, kept, _ in pieces(slot, *flying.pop(slot)):
                pltpu.make_async_copy(source, kept, stage_sems.at[slot]).wait()

    def emit(upto):
        nonlocal sent
        while sent < len(chunks) and chunks[sent][2] + chunks[sent][3] <= upto:
            if chunks[sent][3] < share and not bias_known:
                break
            owner, place, source, size = chunks[sent]
            slot = sent % 2
            finish(slot)

            def convert(at, count, source=source, slot=slot):
                stage_ref[slot, pl.ds(at, count), :] = rows_ref[
                    pl.ds(pl.multiple_of(source + at, 16), count), :
                ].astype(jnp.bfloat16)

            def convert_block(i, carry, convert=convert):
                convert(pl.multiple_of(i * 128, 128), 128)
                return carry

            lax.fori_loop(0, size // 128, convert_block, 0)
            if size % 128:
                convert(size - size % 128, size % 128)
            if size < share:
                bias_place = part_rows - place * share
                first = max(0, -bias_place)
                stage_ref[slot, size:share, :] = bias_ref[first : first + share - size, :]
            launch(slot, owner, place)
            flying[slot] = (owner, place)
            sent += 1

    row = weight(0, n1_ref, [dq_ref, dk_ref, dv_ref])
    row = bias(row, dq_ref)
    row = bias(row, dv_ref)
    emit(row)
    row = weight(row, att_ref, [dproj_ref])
    proj_bias = row
    row = bias(row, dproj_ref)
    bias_size = dproj_ref.shape[1] // 128
    spare = share_rows - part_rows
    bias_ref[...] = jnp.concatenate(
        [
            rows_ref[proj_bias : proj_bias + bias_size, :],
            jnp.zeros((spare - bias_size, 128), jnp.float32),
        ],
        0,
    ).astype(jnp.bfloat16)
    bias_known = True
    emit(row)
    row = weight(row, n2_ref, [dpre_ref])
    row = bias(row, dpre_ref)
    emit(row)
    row = weight(row, act_ref, [dout_ref])
    row = bias(row, dout_ref)
    emit(row)
    rows_ref[row : row + tail_ref.shape[0], :] = tail_ref[...]
    emit(group_size * part_rows)
    for slot in range(2):
        finish(slot)


def pack_shares(factors, tail, part_rows, group_size, wide_size):
    feature = factors[0].shape[1]
    grain = 16 * wide_size
    share_rows = -(-(part_rows + feature // 128) // grain) * grain
    spare = share_rows - part_rows
    share = share_rows // wide_size
    relative = halves(wide_size, group_size)
    whole = pl.BlockSpec(memory_space=pltpu.VMEM)
    if relative:
        units = share // 16
        ends = [0, (units + 2) // 3 * 16, ((units + 2) // 3 + (units + 1) // 3) * 16, share]
        cuts = tuple(zip(ends, ends[1:]))
        shapes = [(2, 2, 2, 2, high - low, 128) for low, high in cuts] * 2
    else:
        cuts = ((0, share),)
        shapes = [(group_size, wide_size, share, 128)]
    return pl.pallas_call(
        functools.partial(
            pack_kernel,
            part_rows=part_rows,
            share_rows=share_rows,
            group_size=group_size,
            wide_size=wide_size,
            cuts=cuts,
            relative=relative,
        ),
        in_specs=[whole] * (len(factors) + 1),
        out_specs=[pl.BlockSpec(memory_space=pl.ANY)] * len(shapes),
        out_shape=[jax.ShapeDtypeStruct(shape, jnp.bfloat16) for shape in shapes],
        scratch_shapes=[
            pltpu.VMEM((group_size * part_rows, 128), jnp.float32),
            pltpu.VMEM((2, share, 128), jnp.bfloat16),
            pltpu.VMEM((spare, 128), jnp.bfloat16),
            pltpu.SemaphoreType.DMA((2,)),
        ],
        compiler_params=pltpu.CompilerParams(vmem_limit_bytes=60 * 1024 * 1024),
        name="pack_grads",
    )(*factors, tail)


def gelu_slope(pre_act):
    normal_cdf = 0.5 * (1.0 + jax.scipy.special.erf(pre_act / math.sqrt(2.0)))
    return normal_cdf + pre_act * jnp.exp(-0.5 * pre_act * pre_act) / math.sqrt(2.0 * math.pi)


def window_pass(tokens, cotangent, keep_mask, weights):
    (
        qkv_w,
        qv_b,
        proj_w,
        proj_b,
        fc1_w,
        fc1_b,
        fc2_w,
        fc2_b,
        ln1_g,
        ln1_b,
        ln2_g,
        ln2_b,
        table_h,
        table_w,
    ) = weights
    win_count, tok_count, feature = tokens.shape
    row_count = win_count * tok_count
    inputs = tokens.reshape(row_count, feature).astype(jnp.float32)
    keep_rows = keep_mask.reshape(row_count, 1)
    hat_one, scale_one = normalize(inputs)
    normed_one = (
        (hat_one * ln1_g.astype(jnp.float32) + ln1_b.astype(jnp.float32)) * keep_rows
    ).astype(jnp.bfloat16)
    bias_full = jnp.concatenate(
        [qv_b[:feature], jnp.zeros((feature,), jnp.bfloat16), qv_b[feature:]]
    ).astype(jnp.float32)
    mixed = (jnp.dot(normed_one, qkv_w, preferred_element_type=jnp.float32) + bias_full).astype(
        jnp.bfloat16
    )
    shift, key_cells = window_constants(tok_count)
    table = wide_table(table_h, table_w)
    probs, attended = attend(mixed, table, shift, key_cells, feature)
    resid = keep_rows * (
        inputs
        + jnp.dot(attended, proj_w, preferred_element_type=jnp.float32)
        + proj_b.astype(jnp.float32)
    )
    hat_two, scale_two = normalize(resid)
    normed_two = (hat_two * ln2_g.astype(jnp.float32) + ln2_b.astype(jnp.float32)).astype(
        jnp.bfloat16
    )
    pre_act = jnp.dot(normed_two, fc1_w, preferred_element_type=jnp.float32) + fc1_b.astype(
        jnp.float32
    )
    activation = jax.nn.gelu(pre_act, approximate=False).astype(jnp.bfloat16)
    result = keep_rows * (
        resid
        + jnp.dot(activation, fc2_w, preferred_element_type=jnp.float32)
        + fc2_b.astype(jnp.float32)
    )
    cot_rows = cotangent.reshape(row_count, feature).astype(jnp.float32) * keep_rows
    grad_out = cot_rows.astype(jnp.bfloat16)
    grad_act = jnp.einsum("nd,fd->nf", grad_out, fc2_w, preferred_element_type=jnp.float32)
    grad_pre = (grad_act * gelu_slope(pre_act)).astype(jnp.bfloat16)
    grad_norm_two = jnp.einsum("nf,df->nd", grad_pre, fc1_w, preferred_element_type=jnp.float32)
    grad_ln2_g = jnp.sum(grad_norm_two * hat_two, 0)
    grad_ln2_b = jnp.sum(grad_norm_two, 0)
    grad_resid = cot_rows + norm_back(grad_norm_two * ln2_g.astype(jnp.float32), hat_two, scale_two)
    grad_branch = keep_rows * grad_resid
    grad_proj = grad_branch.astype(jnp.bfloat16)
    grad_att = jnp.einsum(
        "ne,de->nd", grad_proj, proj_w, preferred_element_type=jnp.float32
    ).astype(jnp.bfloat16)
    grad_query, grad_keys, grad_values, grad_table = attend_back(
        mixed, probs, grad_att, table, shift, key_cells, feature
    )
    rel_span = table_h.shape[0]
    grad_table_h = grad_table[:, :rel_span].T[::-1]
    grad_table_w = grad_table[:, 64 : 64 + rel_span].T[::-1]
    grad_mixed = jnp.concatenate([grad_query, grad_keys, grad_values], -1)
    grad_norm_one = keep_rows * jnp.einsum(
        "nf,df->nd", grad_mixed, qkv_w, preferred_element_type=jnp.float32
    )
    grad_ln1_g = jnp.sum(grad_norm_one * hat_one, 0)
    grad_ln1_b = jnp.sum(grad_norm_one, 0)
    grad_input = grad_branch + norm_back(
        grad_norm_one * ln1_g.astype(jnp.float32), hat_one, scale_one
    )
    factors = (
        normed_one,
        grad_query,
        grad_keys,
        grad_values,
        attended,
        grad_proj,
        normed_two,
        grad_pre,
        activation,
        grad_out,
    )
    tail = (grad_ln1_g, grad_ln1_b, grad_ln2_g, grad_ln2_b, grad_table_h, grad_table_w)
    block_part = result.reshape(win_count, tok_count, feature).astype(jnp.bfloat16)
    input_part = grad_input.reshape(win_count, tok_count, feature).astype(jnp.bfloat16)
    return (block_part, input_part, factors, tail)


def swap(values, axis, bit):
    return lax.ppermute(values, axis, [(i, i ^ bit) for i in range(lax.axis_size(axis))])


def wide_bits(count):
    place = lax.axis_index("wide")
    return [(place >> bit) & 1 for bit in range(count)]


def splits(part_rows):
    return lax.axis_size("grp") == 2 and lax.axis_size("wide") % 8 == 0 and part_rows % 64 == 0


def eighth_index(core, cross, deep):
    return (core * 2 + cross) * 2 + deep


def gather_groups(mine, diagonal, finish):
    core, cross, deep = wide_bits(3)
    first = swap(mine, "grp", 1)
    diagonal, first = lax.optimization_barrier((diagonal, first))
    last = swap(diagonal, "grp", 1)
    side = swap(first, "wide", 2)
    back = swap(first, "wide", 4)
    near = (first, side, back, last)
    far = [swap(part, "wide", 1) for part in near]
    group = lax.axis_index("grp")
    out = finish(first)
    rows = out.shape[0] * out.shape[1]
    out = out.reshape((2, 8) + mine.shape)
    for parts, which in ((near, core), (far, 1 - core)):
        for part, flip_cross, flip_deep in zip(parts, (0, 1, 0, 1), (0, 0, 1, 1)):
            at = eighth_index(which, cross ^ flip_cross, deep ^ flip_deep)
            out = lax.dynamic_update_slice(out, part[None, None], (1 - group, at, 0, 0))
    return out.reshape(rows, 128)


def joined(kept, sent):
    return (kept.astype(jnp.float32) + sent.astype(jnp.float32)).astype(kept.dtype)


def reduce_shares(packed):
    if len(packed) == 1:
        rows = packed[0].reshape(-1, 128)
        return lax.psum_scatter(rows, ("grp", "wide"), scatter_dimension=0, tiled=True)
    moves = {
        "x": lambda v: swap(v, "wide", 2),
        "near": lambda v: swap(v, "wide", 4),
        "far": lambda v: swap(v, "wide", 8),
        "y": lambda v: swap(v, "grp", 1),
    }
    done = []
    for kept, sent, order in zip(packed[:3], packed[3:], ORDERS):
        arrived = swap(sent, "wide", 1)
        for name in order + ("far",):
            leaving = joined(kept[1], arrived[1])
            kept = joined(kept[0], arrived[0])
            arrived = moves[name](leaving)
        done.append(joined(kept, arrived))
    return jnp.concatenate(done, 0)


def own_eighths(rows):
    core, cross, deep = wide_bits(3)
    parts = rows.reshape(8, -1, 128)
    spots = (eighth_index(core, cross, deep), eighth_index(core, 1 - cross, 1 - deep))
    return [lax.dynamic_index_in_dim(parts, spot, keepdims=False) for spot in spots]


def first_step(grads, first_moment):
    return BETA_ONE * first_moment + (1.0 - BETA_ONE) * grads


def second_step(grads, master, moment_next, second_moment):
    second_next = BETA_TWO * second_moment + (1.0 - BETA_TWO) * grads * grads
    fix_one = 1.0 - BETA_ONE**ADAM_STEP
    fix_two = 1.0 - BETA_TWO**ADAM_STEP
    update = (
        moment_next / fix_one / (jnp.sqrt(second_next / fix_two) + ADAM_EPS) + DECAY_RATE * master
    )
    return (master - LEARN_RATE * update, second_next)


BLOCK_ROWS = 2048


def place_kernel(group_ref, master_ref, out_ref):
    out_ref[0] = master_ref[...].astype(jnp.bfloat16)


def place_own(master):
    rows = master.shape[0]
    return pl.pallas_call(
        place_kernel,
        grid_spec=pltpu.PrefetchScalarGridSpec(
            num_scalar_prefetch=1,
            grid=(pl.cdiv(rows, BLOCK_ROWS),),
            in_specs=[pl.BlockSpec((BLOCK_ROWS, 128), lambda i, g: (i, 0))],
            out_specs=pl.BlockSpec((1, BLOCK_ROWS, 128), lambda i, g: (g[0], i, 0)),
        ),
        out_shape=jax.ShapeDtypeStruct((2, rows, 128), jnp.bfloat16),
        name="place_own",
    )(lax.axis_index("grp").reshape(1), master)


def eighth_kernel(spot_ref, total_ref, master_ref, first_ref, second_ref, out_ref, *, factor):
    grads = total_ref[...].astype(jnp.float32) * factor
    moment = first_step(grads, first_ref[...])
    out_ref[0] = second_step(grads, master_ref[...], moment, second_ref[...])[0].astype(jnp.bfloat16)


def eighth_weights(totals, state, factor):
    size = state[0].shape[0] // 8
    core, cross, deep = wide_bits(3)
    spots = (eighth_index(core, cross, deep), eighth_index(core, 1 - cross, 1 - deep))
    both = pl.pallas_call(
        functools.partial(eighth_kernel, factor=factor),
        grid_spec=pltpu.PrefetchScalarGridSpec(
            num_scalar_prefetch=1,
            grid=(2,),
            in_specs=[pl.BlockSpec((size, 128), lambda i, spot: (spot[i], 0))] * 4,
            out_specs=pl.BlockSpec((1, size, 128), lambda i, spot: (i, 0, 0)),
        ),
        out_shape=jax.ShapeDtypeStruct((2, size, 128), jnp.bfloat16),
        name="eighth_weights",
    )(jnp.stack(spots).astype(jnp.int32), totals, *state)
    return both[0], both[1]


def adam_kernel(group_ref, total_ref, master_ref, first_ref, second_ref, *refs, factor):
    grads_ref, master_out, first_out, second_out, weights_ref = refs[-5:]
    grads = total_ref[...].astype(jnp.float32) * factor
    moment = first_step(grads, first_ref[...])
    master_next, second_next = second_step(grads, master_ref[...], moment, second_ref[...])
    grads_ref[...] = grads
    master_out[...] = master_next
    first_out[...] = moment
    second_out[...] = second_next
    weights_ref[0] = master_next.astype(jnp.bfloat16)


def adam_rows(totals, state, factor, first_block, last_block, onto, after):
    rows = state[0].shape[0]
    row_spec = pl.BlockSpec((BLOCK_ROWS, 128), lambda i, g: (first_block + i, 0))
    anywhere = pl.BlockSpec(memory_space=pl.ANY)
    wide = jax.ShapeDtypeStruct((rows, 128), jnp.float32)
    spare = 5 - len(onto)
    return pl.pallas_call(
        functools.partial(adam_kernel, factor=factor),
        grid_spec=pltpu.PrefetchScalarGridSpec(
            num_scalar_prefetch=1,
            grid=(last_block - first_block,),
            in_specs=[row_spec] * 4 + [anywhere] * (len(onto) + len(after)),
            out_specs=[row_spec] * 4
            + [pl.BlockSpec((1, BLOCK_ROWS, 128), lambda i, g: (g[0], first_block + i, 0))],
        ),
        out_shape=[wide] * 4 + [jax.ShapeDtypeStruct((2, rows, 128), jnp.bfloat16)],
        input_output_aliases={5 + i: spare + i for i in range(len(onto))},
        name="adam_rows",
    )(lax.axis_index("grp").reshape(1), totals, *state, *onto, *after)


def body(tokens, cotangent, window_place, master, first_moment, second_moment):
    part_rows = master.shape[0]
    wide_size = lax.axis_size("wide")
    group_size = lax.axis_size("grp")
    feature = tokens.shape[-1]
    micro_count, slots, tok_count, _ = tokens.shape
    masks = token_mask(window_place)
    if splits(part_rows):
        mine, diagonal = (part.astype(jnp.bfloat16) for part in own_eighths(master))
        gathered = gather_groups(mine, diagonal, lambda first: place_own(master))
    else:
        gathered = lax.all_gather(master.astype(jnp.bfloat16), "grp", axis=0, tiled=True)
    weights = unpack(gathered, feature)
    wins = micro_count * slots
    extra = -tok_count % 16

    def padded(values):
        values = values.reshape((wins,) + values.shape[2:])
        return jnp.pad(values, ((0, 0), (0, extra)) + ((0, 0),) * (values.ndim - 2))

    block_part, input_part, factors, tail = window_pass(
        padded(tokens), padded(cotangent), padded(masks), weights
    )
    filled = sum(math.prod(dims_of) for dims_of in layout(feature)[:8]) // 128
    tail = jnp.concatenate([member.reshape(-1) for member in tail])
    tail_rows = part_rows * group_size - filled
    tail = jnp.pad(tail, (0, tail_rows * 128 - tail.shape[0])).reshape(tail_rows, 128)
    packed = pack_shares(factors, tail, part_rows, group_size, wide_size)
    owned = reduce_shares(packed)
    block_out = block_part[:, :tok_count].reshape(tokens.shape)
    input_grad = input_part[:, :tok_count].reshape(tokens.shape)
    owned, block_out, input_grad = lax.optimization_barrier((owned, block_out, input_grad))
    totals = lax.all_gather(owned, "wide", axis=0, tiled=True)
    factor = 1.0 / (micro_count * wide_size * group_size)
    bias_total = totals[part_rows : part_rows + feature // 128]
    proj_bias_grad = bias_total.astype(jnp.float32).reshape(-1) * factor
    state = (master, first_moment, second_moment)
    if splits(part_rows):
        updated = []

        def finish(first):
            blocks = pl.cdiv(part_rows, BLOCK_ROWS)
            half = blocks // 2
            held = gathered.reshape(2, part_rows, 128)
            begun = adam_rows(totals, state, factor, 0, half, (held,), ())
            updated.extend(adam_rows(totals, state, factor, half, blocks, begun, (first,)))
            return updated.pop()

        mine, diagonal = eighth_weights(totals, state, factor)
        weights_next = gather_groups(mine, diagonal, finish)
        grads, master_next, moment_next, second_next = updated
    else:
        grads = totals[:part_rows].astype(jnp.float32) * factor
        moment_next = first_step(grads, first_moment)
        master_next, second_next = second_step(grads, master, moment_next, second_moment)
        own_weights = master_next.astype(jnp.bfloat16)
        weights_next = lax.all_gather(own_weights, "grp", axis=0, tiled=True)
    return (
        block_out,
        input_grad,
        grads,
        master_next,
        moment_next,
        second_next,
        weights_next,
        proj_bias_grad,
    )


def solution(mesh):
    return jax.shard_map(
        body,
        mesh=mesh,
        in_specs=(
            P(None, ("wide", "grp"), None, None),
            P(None, ("wide", "grp"), None, None),
            P(None, ("wide", "grp")),
            P("grp", None),
            P("grp", None),
            P("grp", None),
        ),
        out_specs=(
            P(None, ("wide", "grp"), None, None),
            P(None, ("wide", "grp"), None, None),
            P("grp", None),
            P("grp", None),
            P("grp", None),
            P("grp", None),
            P(),
            P(),
        ),
        check_vma=False,
    )
```

```python
import functools
import math

import jax
import jax.numpy as jnp
from jax import lax
from jax.experimental import pallas as pl
from jax.experimental.pallas import tpu as pltpu
from jax.sharding import PartitionSpec as P

FF = 3072
HD = 64
WS = 14
GRID = 64
ADAM_STEP = 10


EPS_NORM = 1e-06
BETA_ONE = 0.9
BETA_TWO = 0.95
ADAM_EPS = 1e-08
LEARN_RATE = 0.02
DECAY_RATE = 0.1


def layout(feature):
    rel_span = 2 * WS - 1
    return [
        (feature, 3 * feature),
        (2 * feature,),
        (feature, feature),
        (feature,),
        (feature, FF),
        (FF,),
        (FF, feature),
        (feature,),
        (feature,),
        (feature,),
        (feature,),
        (feature,),
        (rel_span, HD),
        (rel_span, HD),
    ]


CHUNK = 2304


def unpack_kernel(rows_ref, *refs, plan):
    *out_refs, raw_ref, wide_ref, sems = refs
    step = pl.program_id(0)
    limit = raw_ref.shape[1]
    total = sum(count for _, count, _ in plan)

    def chunk_copy(index, slot):
        start = jnp.int32(0)
        before = 0
        for row, count, _ in plan:
            at = row // 16 * 16 + (index - before) * CHUNK
            start = jnp.where(index >= before, at, start)
            before += count
        return pltpu.make_async_copy(
            rows_ref.at[pl.ds(pl.multiple_of(start, 16), limit), :], raw_ref.at[slot], sems.at[slot]
        )

    slot = lax.rem(step, 2)

    @pl.when(step == 0)
    def _():
        chunk_copy(step, slot).start()

    @pl.when(step + 1 < total)
    def _():
        chunk_copy(step + 1, 1 - slot).start()

    chunk_copy(step, slot).wait()
    part = limit // 5

    def widen(i, carry):
        at = pl.multiple_of(i * part, 16)
        wide_ref[pl.ds(at, part), :] = raw_ref[slot, pl.ds(at, part), :].astype(jnp.float32)
        return carry

    lax.fori_loop(0, 5, widen, 0)
    before = 0
    for (row, count, width), out_ref in zip(plan, out_refs):

        @pl.when((step >= before) & (step < before + count))
        def _(row=row, width=width, out_ref=out_ref):
            for j in range(width):
                picked = wide_ref[pl.ds(row % 16 + j, CHUNK // width, stride=width), :]
                out_ref[:, j * 128 : (j + 1) * 128] = picked.astype(jnp.bfloat16)

        before += count


def unpack_matrices(rows, dims, starts):
    plan = tuple(
        (start, math.prod(dims_of) // 128 // CHUNK, dims_of[1] // 128)
        for start, dims_of in zip(starts, dims)
    )
    specs = []
    before = 0
    for (_, count, width), dims_of in zip(plan, dims):

        def place(i, before=before, count=count):
            return (jnp.clip(i - before, 0, count - 1), 0)

        specs.append(pl.BlockSpec((CHUNK // width, dims_of[1]), place))
        before += count
    return pl.pallas_call(
        functools.partial(unpack_kernel, plan=plan),
        grid=(before,),
        in_specs=[pl.BlockSpec(memory_space=pl.ANY)],
        out_specs=specs,
        out_shape=[jax.ShapeDtypeStruct(dims_of, jnp.bfloat16) for dims_of in dims],
        scratch_shapes=[
            pltpu.VMEM((2, CHUNK + 16, 128), jnp.bfloat16),
            pltpu.VMEM((CHUNK + 16, 128), jnp.float32),
            pltpu.SemaphoreType.DMA((2,)),
        ],
        name="unpack_matrices",
    )(rows)


def unpack(rows, feature):
    dims = layout(feature)
    starts = []
    row = 0
    for dims_of in dims[:8]:
        starts.append(row)
        row = row + math.prod(dims_of) // 128
    matrices = unpack_matrices(rows, dims[:8:2], starts[:8:2])
    members = []
    for index, dims_of in enumerate(dims[:8]):
        if index % 2 == 0:
            members.append(matrices[index // 2])
        else:
            start = starts[index]
            members.append(rows[start : start + dims_of[0] // 128].reshape(dims_of))
    tail_size = sum(math.prod(dims_of) for dims_of in dims[8:])
    tail = rows[row : row - (-tail_size // 128)].reshape(-1)
    offset = 0
    for dims_of in dims[8:]:
        length = math.prod(dims_of)
        members.append(tail[offset : offset + length].reshape(dims_of))
        offset = offset + length
    return tuple(members)


def token_mask(window_place):
    cells = jnp.arange(WS * WS, dtype=jnp.int32)
    inner_row = cells // WS
    inner_col = cells % WS
    places = window_place[..., None]
    live_slot = places < 25
    row_real = WS * (places // 5) + inner_row < GRID
    col_real = WS * (places % 5) + inner_col < GRID
    return jnp.where(live_slot & row_real & col_real, 1.0, 0.0).astype(jnp.float32)


def normalize(inputs):
    row_mean = jnp.mean(inputs, -1, keepdims=True)
    centred = inputs - row_mean
    inv_scale = lax.rsqrt(jnp.mean(centred * centred, -1, keepdims=True) + EPS_NORM)
    return (centred * inv_scale, inv_scale)


def norm_back(grad_hat, normed_hat, inv_scale):
    first_mean = jnp.mean(grad_hat, -1, keepdims=True)
    second_mean = jnp.mean(grad_hat * normed_hat, -1, keepdims=True)
    return inv_scale * (grad_hat - first_mean - normed_hat * second_mean)


def attend_kernel(q_ref, k_ref, v_ref, table_ref, shift_ref, key_ref, probs_ref, out_ref):
    shift = shift_ref[...]
    key_cells = key_ref[...]
    last_lane = lax.broadcasted_iota(jnp.int32, shift.shape, 1) == 127
    double_cells = jnp.concatenate([key_cells, key_cells], 1)
    for part in range(2):
        cut = slice(part * HD, (part + 1) * HD)
        queries = q_ref[:, cut]
        along = jnp.dot(queries, table_ref[...], preferred_element_type=jnp.float32)
        for bit in (1, 2, 4, 8):
            along = jnp.where((shift & bit) != 0, pltpu.roll(along, 128 - bit, 1), along)
        along = jnp.where(last_lane, 1.0, along)
        scores = dot_last(queries * (1.0 / math.sqrt(HD)), k_ref[:, cut])
        scores = scores + dot_last(high_low(along), double_cells)
        powers = jnp.exp(scores - jnp.max(scores, -1, keepdims=True))
        probs = (powers * (1.0 / jnp.sum(powers, -1, keepdims=True))).astype(jnp.bfloat16)
        probs_ref[0, part] = probs
        out_ref[:, cut] = jnp.dot(
            probs, v_ref[:, cut], preferred_element_type=jnp.float32
        ).astype(jnp.bfloat16)


def attend_back_kernel(
    q_ref, k_ref, v_ref, probs_ref, grad_ref, table_ref, shift_ref, key_ref,
    dq_ref, dk_ref, dv_ref, dtable_ref,
):
    shift = shift_ref[...]
    key_cells = key_ref[...]
    double_table = jnp.concatenate([table_ref[...], table_ref[...]], 1)
    scale = 1.0 / math.sqrt(HD)

    @pl.when((pl.program_id(0) == 0) & (pl.program_id(1) == 0))
    def _():
        dtable_ref[...] = jnp.zeros(dtable_ref.shape, jnp.float32)

    for part in range(2):
        cut = slice(part * HD, (part + 1) * HD)
        queries = q_ref[:, cut]
        grad = grad_ref[:, cut]
        probs = probs_ref[0, part]
        dv_ref[:, cut] = dot_first(probs, grad).astype(jnp.bfloat16)
        grad_probs = dot_last(grad, v_ref[:, cut])
        wide_probs = probs.astype(jnp.float32)
        inner = jnp.sum(wide_probs * grad_probs, -1, keepdims=True)
        grad_scores = (wide_probs * (grad_probs - inner)).astype(jnp.bfloat16)
        dk_ref[:, cut] = (dot_first(grad_scores, queries) * scale).astype(jnp.bfloat16)
        both = jnp.dot(
            grad_scores,
            jnp.concatenate([key_cells, k_ref[:, cut]], 1),
            preferred_element_type=jnp.float32,
        )
        along = both[:, :128]
        for bit in (1, 2, 4, 8):
            along = jnp.where((shift & bit) != 0, pltpu.roll(along, bit, 1), along)
        pair = high_low(along)
        grad_query = both[:, 128:] * scale + dot_last(pair, double_table)
        dq_ref[:, cut] = grad_query.astype(jnp.bfloat16)
        table_pair = dot_first(queries, pair)
        dtable_ref[...] += table_pair[:, :128] + table_pair[:, 128:]


def high_low(values):
    high = values.astype(jnp.bfloat16)
    low = (values - high.astype(jnp.float32)).astype(jnp.bfloat16)
    return jnp.concatenate([high, low], 1)


def window_constants(row_count):
    cells = jnp.arange(row_count, dtype=jnp.int32)[:, None]
    lanes = jnp.arange(128, dtype=jnp.int32)[None, :]
    first = lanes < 64
    shift = jnp.where(first, WS - 1 - cells // WS, WS - 1 - cells % WS)
    live = cells < WS * WS
    shift = jnp.where(live, shift, 0)
    offset = jnp.where(first, lanes, lanes - 64)
    place = jnp.where(first, cells // WS, cells % WS)
    key_cells = jnp.where(live & (offset == place), 1.0, 0.0)
    key_cells = jnp.where((lanes == 127) & ~live, -1e30, key_cells).astype(jnp.bfloat16)
    return shift, key_cells


def wide_table(table_h, table_w):
    pad = jnp.zeros((HD, 64 - table_h.shape[0]), table_h.dtype)
    return jnp.concatenate([table_h[::-1].T, pad, table_w[::-1].T, pad], 1)


def attend(mixed, table, shift, key_cells, feature):
    rows, pairs = shift.shape[0], feature // 128
    wins = mixed.shape[0] // rows
    whole = lambda shape: pl.BlockSpec(shape, lambda w, h: (0,) * len(shape))
    column = lambda base: pl.BlockSpec((rows, 128), lambda w, h: (w, base * pairs + h))
    return pl.pallas_call(
        attend_kernel,
        grid=(wins, pairs),
        in_specs=[column(0), column(1), column(2), whole((HD, 128)), whole((rows, 128)), whole((rows, 128))],
        out_specs=[
            pl.BlockSpec((1, 2, rows, rows), lambda w, h: (w, h, 0, 0)),
            pl.BlockSpec((rows, 128), lambda w, h: (w, h)),
        ],
        out_shape=[
            jax.ShapeDtypeStruct((wins, 2 * pairs, rows, rows), jnp.bfloat16),
            jax.ShapeDtypeStruct((wins * rows, feature), jnp.bfloat16),
        ],
        name="attend",
    )(mixed, mixed, mixed, table, shift, key_cells)


def attend_back(mixed, probs, grad_att, table, shift, key_cells, feature):
    rows, pairs = shift.shape[0], feature // 128
    wins = mixed.shape[0] // rows
    whole = lambda shape: pl.BlockSpec(shape, lambda w, h: (0,) * len(shape))
    column = lambda base: pl.BlockSpec((rows, 128), lambda w, h: (w, base * pairs + h))
    flat = jax.ShapeDtypeStruct((wins * rows, feature), jnp.bfloat16)
    return pl.pallas_call(
        attend_back_kernel,
        grid=(wins, pairs),
        in_specs=[
            column(0), column(1), column(2),
            pl.BlockSpec((1, 2, rows, rows), lambda w, h: (w, h, 0, 0)),
            column(0),
            whole((HD, 128)), whole((rows, 128)), whole((rows, 128)),
        ],
        out_specs=[column(0), column(0), column(0), whole((HD, 128))],
        out_shape=[flat, flat, flat, jax.ShapeDtypeStruct((HD, 128), jnp.float32)],
        name="attend_back",
    )(mixed, mixed, mixed, probs, grad_att, table, shift, key_cells)


def dot_last(left, right):
    return lax.dot_general(left, right, (((1,), (1,)), ((), ())), preferred_element_type=jnp.float32)


def dot_first(left, right):
    return lax.dot_general(left, right, (((0,), (0,)), ((), ())), preferred_element_type=jnp.float32)


ORDERS = (("y", "x", "near"), ("x", "near", "y"), ("near", "y", "x"))


def halves(wide_size, group_size):
    return (wide_size, group_size) == (16, 2)


def pack_kernel(
    n1_ref, dq_ref, dk_ref, dv_ref, att_ref, dproj_ref, n2_ref, dpre_ref, act_ref, dout_ref, tail_ref,
    *refs, part_rows, share_rows, group_size, wide_size, cuts, relative,
):
    *out_refs, rows_ref, stage_ref, bias_ref, stage_sems = refs
    kept_refs, sent_refs = out_refs[: len(cuts)], out_refs[len(cuts) :]
    count = n1_ref.shape[0]
    ones = jnp.ones((16, count), jnp.bfloat16)

    def weight(base, left_ref, right_refs):
        width = sum(ref.shape[1] for ref in right_refs) // 128

        def block(f, carry):
            left = left_ref[:, pl.ds(pl.multiple_of(f * 128, 128), 128)]
            column = 0
            for ref in right_refs:
                product = dot_first(left, ref[...])
                for j in range(ref.shape[1] // 128):
                    rows_ref[pl.ds(base + f * 128 * width + column, 128, stride=width), :] = product[
                        :, j * 128 : (j + 1) * 128
                    ]
                    column += 1
            return carry

        lax.fori_loop(0, left_ref.shape[1] // 128, block, 0)
        return base + left_ref.shape[1] * width

    def bias(base, ref):
        total = jnp.dot(ones, ref[...], preferred_element_type=jnp.float32)
        for j in range(ref.shape[1] // 128):
            rows_ref[base + j : base + j + 1, :] = total[0:1, j * 128 : (j + 1) * 128]
        return base + ref.shape[1] // 128

    share = share_rows // wide_size
    own_wide = lax.axis_index("wide")
    own_group = lax.axis_index("grp")
    chunks = []
    for owner in range(group_size):
        for place in range(wide_size):
            low = place * share
            size = max(0, min(share, part_rows - low))
            chunks.append((owner, place, owner * part_rows + low, size))
    flying = {}
    sent = 0
    bias_known = False

    def pieces(slot, owner, place):
        if not relative:
            return [(stage_ref.at[slot], kept_refs[0].at[owner, place], None)]
        flips = place ^ own_wide
        flip = {
            "y": owner ^ own_group,
            "x": (flips >> 1) & 1,
            "near": (flips >> 2) & 1,
            "far": (flips >> 3) & 1,
        }
        found = []
        for (low, high), order, kept_ref, sent_ref in zip(cuts, ORDERS, kept_refs, sent_refs):
            spot = tuple(flip[name] for name in order + ("far",))
            source = stage_ref.at[slot, pl.ds(low, high - low), :]
            found.append((source, kept_ref.at[spot], sent_ref.at[spot]))
        return found

    def launch(slot, owner, place):
        for source, kept, other in pieces(slot, owner, place):

            def start(target, source=source):
                pltpu.make_async_copy(source, target, stage_sems.at[slot]).start()

            if other is None:
                start(kept)
            else:
                other_core = ((place ^ own_wide) & 1) == 1
                pl.when(other_core)(functools.partial(start, other))
                pl.when(jnp.logical_not(other_core))(functools.partial(start, kept))

    def finish(slot):
        if slot in flying:
            for source, kept, _ in pieces(slot, *flying.pop(slot)):
                pltpu.make_async_copy(source, kept, stage_sems.at[slot]).wait()

    def emit(upto):
        nonlocal sent
        while sent < len(chunks) and chunks[sent][2] + chunks[sent][3] <= upto:
            if chunks[sent][3] < share and not bias_known:
                break
            owner, place, source, size = chunks[sent]
            slot = sent % 2
            finish(slot)

            def convert(at, count, source=source, slot=slot):
                stage_ref[slot, pl.ds(at, count), :] = rows_ref[
                    pl.ds(pl.multiple_of(source + at, 16), count), :
                ].astype(jnp.bfloat16)

            def convert_block(i, carry, convert=convert):
                convert(pl.multiple_of(i * 128, 128), 128)
                return carry

            lax.fori_loop(0, size // 128, convert_block, 0)
            if size % 128:
                convert(size - size % 128, size % 128)
            if size < share:
                bias_place = part_rows - place * share
                first = max(0, -bias_place)
                stage_ref[slot, size:share, :] = bias_ref[first : first + share - size, :]
            launch(slot, owner, place)
            flying[slot] = (owner, place)
            sent += 1

    row = weight(0, n1_ref, [dq_ref, dk_ref, dv_ref])
    row = bias(row, dq_ref)
    row = bias(row, dv_ref)
    emit(row)
    row = weight(row, att_ref, [dproj_ref])
    proj_bias = row
    row = bias(row, dproj_ref)
    bias_size = dproj_ref.shape[1] // 128
    spare = share_rows - part_rows
    bias_ref[...] = jnp.concatenate(
        [
            rows_ref[proj_bias : proj_bias + bias_size, :],
            jnp.zeros((spare - bias_size, 128), jnp.float32),
        ],
        0,
    ).astype(jnp.bfloat16)
    bias_known = True
    emit(row)
    row = weight(row, n2_ref, [dpre_ref])
    row = bias(row, dpre_ref)
    emit(row)
    row = weight(row, act_ref, [dout_ref])
    row = bias(row, dout_ref)
    emit(row)
    rows_ref[row : row + tail_ref.shape[0], :] = tail_ref[...]
    emit(group_size * part_rows)
    for slot in range(2):
        finish(slot)


def pack_shares(factors, tail, part_rows, group_size, wide_size):
    feature = factors[0].shape[1]
    grain = 16 * wide_size
    share_rows = -(-(part_rows + feature // 128) // grain) * grain
    spare = share_rows - part_rows
    share = share_rows // wide_size
    relative = halves(wide_size, group_size)
    whole = pl.BlockSpec(memory_space=pltpu.VMEM)
    if relative:
        units = share // 16
        ends = [0, (units + 2) // 3 * 16, ((units + 2) // 3 + (units + 1) // 3) * 16, share]
        cuts = tuple(zip(ends, ends[1:]))
        shapes = [(2, 2, 2, 2, high - low, 128) for low, high in cuts] * 2
    else:
        cuts = ((0, share),)
        shapes = [(group_size, wide_size, share, 128)]
    return pl.pallas_call(
        functools.partial(
            pack_kernel,
            part_rows=part_rows,
            share_rows=share_rows,
            group_size=group_size,
            wide_size=wide_size,
            cuts=cuts,
            relative=relative,
        ),
        in_specs=[whole] * (len(factors) + 1),
        out_specs=[pl.BlockSpec(memory_space=pl.ANY)] * len(shapes),
        out_shape=[jax.ShapeDtypeStruct(shape, jnp.bfloat16) for shape in shapes],
        scratch_shapes=[
            pltpu.VMEM((group_size * part_rows, 128), jnp.float32),
            pltpu.VMEM((2, share, 128), jnp.bfloat16),
            pltpu.VMEM((spare, 128), jnp.bfloat16),
            pltpu.SemaphoreType.DMA((2,)),
        ],
        compiler_params=pltpu.CompilerParams(vmem_limit_bytes=60 * 1024 * 1024),
        name="pack_grads",
    )(*factors, tail)


def gelu_and_slope(pre_act):
    normal_cdf = 0.5 * (1.0 + jax.scipy.special.erf(pre_act / math.sqrt(2.0)))
    return pre_act * normal_cdf, normal_cdf + pre_act * jnp.exp(-0.5 * pre_act * pre_act) / math.sqrt(2.0 * math.pi)


def window_pass(tokens, cotangent, keep_mask, weights):
    (
        qkv_w,
        qv_b,
        proj_w,
        proj_b,
        fc1_w,
        fc1_b,
        fc2_w,
        fc2_b,
        ln1_g,
        ln1_b,
        ln2_g,
        ln2_b,
        table_h,
        table_w,
    ) = weights
    win_count, tok_count, feature = tokens.shape
    row_count = win_count * tok_count
    inputs = tokens.reshape(row_count, feature).astype(jnp.float32)
    keep_rows = keep_mask.reshape(row_count, 1)
    hat_one, scale_one = normalize(inputs)
    normed_one = (
        (hat_one * ln1_g.astype(jnp.float32) + ln1_b.astype(jnp.float32)) * keep_rows
    ).astype(jnp.bfloat16)
    bias_full = jnp.concatenate(
        [qv_b[:feature], jnp.zeros((feature,), jnp.bfloat16), qv_b[feature:]]
    ).astype(jnp.float32)
    mixed = (jnp.dot(normed_one, qkv_w, preferred_element_type=jnp.float32) + bias_full).astype(
        jnp.bfloat16
    )
    shift, key_cells = window_constants(tok_count)
    table = wide_table(table_h, table_w)
    probs, attended = attend(mixed, table, shift, key_cells, feature)
    resid = keep_rows * (
        inputs
        + jnp.dot(attended, proj_w, preferred_element_type=jnp.float32)
        + proj_b.astype(jnp.float32)
    )
    hat_two, scale_two = normalize(resid)
    normed_two = (hat_two * ln2_g.astype(jnp.float32) + ln2_b.astype(jnp.float32)).astype(
        jnp.bfloat16
    )
    pre_act = jnp.dot(normed_two, fc1_w, preferred_element_type=jnp.float32) + fc1_b.astype(
        jnp.float32
    )
    activation, slope = gelu_and_slope(pre_act)
    activation = activation.astype(jnp.bfloat16)
    result = keep_rows * (
        resid
        + jnp.dot(activation, fc2_w, preferred_element_type=jnp.float32)
        + fc2_b.astype(jnp.float32)
    )
    cot_rows = cotangent.reshape(row_count, feature).astype(jnp.float32) * keep_rows
    grad_out = cot_rows.astype(jnp.bfloat16)
    grad_act = jnp.einsum("nd,fd->nf", grad_out, fc2_w, preferred_element_type=jnp.float32)
    grad_pre = (grad_act * slope).astype(jnp.bfloat16)
    grad_norm_two = jnp.einsum("nf,df->nd", grad_pre, fc1_w, preferred_element_type=jnp.float32)
    grad_ln2_g = jnp.sum(grad_norm_two * hat_two, 0)
    grad_ln2_b = jnp.sum(grad_norm_two, 0)
    grad_resid = cot_rows + norm_back(grad_norm_two * ln2_g.astype(jnp.float32), hat_two, scale_two)
    grad_branch = keep_rows * grad_resid
    grad_proj = grad_branch.astype(jnp.bfloat16)
    grad_att = jnp.einsum(
        "ne,de->nd", grad_proj, proj_w, preferred_element_type=jnp.float32
    ).astype(jnp.bfloat16)
    grad_query, grad_keys, grad_values, grad_table = attend_back(
        mixed, probs, grad_att, table, shift, key_cells, feature
    )
    rel_span = table_h.shape[0]
    grad_table_h = grad_table[:, :rel_span].T[::-1]
    grad_table_w = grad_table[:, 64 : 64 + rel_span].T[::-1]
    grad_mixed = jnp.concatenate([grad_query, grad_keys, grad_values], -1)
    grad_norm_one = keep_rows * jnp.einsum(
        "nf,df->nd", grad_mixed, qkv_w, preferred_element_type=jnp.float32
    )
    grad_ln1_g = jnp.sum(grad_norm_one * hat_one, 0)
    grad_ln1_b = jnp.sum(grad_norm_one, 0)
    grad_input = grad_branch + norm_back(
        grad_norm_one * ln1_g.astype(jnp.float32), hat_one, scale_one
    )
    factors = (
        normed_one,
        grad_query,
        grad_keys,
        grad_values,
        attended,
        grad_proj,
        normed_two,
        grad_pre,
        activation,
        grad_out,
    )
    tail = (grad_ln1_g, grad_ln1_b, grad_ln2_g, grad_ln2_b, grad_table_h, grad_table_w)
    block_part = result.reshape(win_count, tok_count, feature).astype(jnp.bfloat16)
    input_part = grad_input.reshape(win_count, tok_count, feature).astype(jnp.bfloat16)
    return (block_part, input_part, factors, tail)


def swap(values, axis, bit):
    return lax.ppermute(values, axis, [(i, i ^ bit) for i in range(lax.axis_size(axis))])


def wide_bits(count):
    place = lax.axis_index("wide")
    return [(place >> bit) & 1 for bit in range(count)]


def splits(part_rows):
    return lax.axis_size("grp") == 2 and lax.axis_size("wide") % 8 == 0 and part_rows % 64 == 0


def eighth_index(core, cross, deep):
    return (core * 2 + cross) * 2 + deep


def gather_groups(mine, diagonal, finish):
    core, cross, deep = wide_bits(3)
    first = swap(mine, "grp", 1)
    diagonal, first = lax.optimization_barrier((diagonal, first))
    last = swap(diagonal, "grp", 1)
    side = swap(first, "wide", 2)
    back = swap(first, "wide", 4)
    near = (first, side, back, last)
    far = [swap(part, "wide", 1) for part in near]
    group = lax.axis_index("grp")
    out = finish(first)
    rows = out.shape[0] * out.shape[1]
    out = out.reshape((2, 8) + mine.shape)
    for parts, which in ((near, core), (far, 1 - core)):
        for part, flip_cross, flip_deep in zip(parts, (0, 1, 0, 1), (0, 0, 1, 1)):
            at = eighth_index(which, cross ^ flip_cross, deep ^ flip_deep)
            out = lax.dynamic_update_slice(out, part[None, None], (1 - group, at, 0, 0))
    return out.reshape(rows, 128)


def joined(kept, sent):
    return (kept.astype(jnp.float32) + sent.astype(jnp.float32)).astype(kept.dtype)


def reduce_shares(packed):
    if len(packed) == 1:
        rows = packed[0].reshape(-1, 128)
        return lax.psum_scatter(rows, ("grp", "wide"), scatter_dimension=0, tiled=True)
    moves = {
        "x": lambda v: swap(v, "wide", 2),
        "near": lambda v: swap(v, "wide", 4),
        "far": lambda v: swap(v, "wide", 8),
        "y": lambda v: swap(v, "grp", 1),
    }
    done = []
    for kept, sent, order in zip(packed[:3], packed[3:], ORDERS):
        arrived = swap(sent, "wide", 1)
        for name in order + ("far",):
            leaving = joined(kept[1], arrived[1])
            kept = joined(kept[0], arrived[0])
            arrived = moves[name](leaving)
        done.append(joined(kept, arrived))
    return jnp.concatenate(done, 0)


def own_eighths(rows):
    core, cross, deep = wide_bits(3)
    parts = rows.reshape(8, -1, 128)
    spots = (eighth_index(core, cross, deep), eighth_index(core, 1 - cross, 1 - deep))
    return [lax.dynamic_index_in_dim(parts, spot, keepdims=False) for spot in spots]


def first_step(grads, first_moment):
    return BETA_ONE * first_moment + (1.0 - BETA_ONE) * grads


def second_step(grads, master, moment_next, second_moment):
    second_next = BETA_TWO * second_moment + (1.0 - BETA_TWO) * grads * grads
    fix_one = 1.0 - BETA_ONE**ADAM_STEP
    fix_two = 1.0 - BETA_TWO**ADAM_STEP
    update = (
        moment_next / fix_one / (jnp.sqrt(second_next / fix_two) + ADAM_EPS) + DECAY_RATE * master
    )
    return (master - LEARN_RATE * update, second_next)


BLOCK_ROWS = 2048


def place_kernel(group_ref, master_ref, out_ref):
    out_ref[0] = master_ref[...].astype(jnp.bfloat16)


def place_own(master):
    rows = master.shape[0]
    return pl.pallas_call(
        place_kernel,
        grid_spec=pltpu.PrefetchScalarGridSpec(
            num_scalar_prefetch=1,
            grid=(pl.cdiv(rows, BLOCK_ROWS),),
            in_specs=[pl.BlockSpec((BLOCK_ROWS, 128), lambda i, g: (i, 0))],
            out_specs=pl.BlockSpec((1, BLOCK_ROWS, 128), lambda i, g: (g[0], i, 0)),
        ),
        out_shape=jax.ShapeDtypeStruct((2, rows, 128), jnp.bfloat16),
        name="place_own",
    )(lax.axis_index("grp").reshape(1), master)


def eighth_kernel(spot_ref, total_ref, master_ref, first_ref, second_ref, out_ref, *, factor):
    grads = total_ref[...].astype(jnp.float32) * factor
    moment = first_step(grads, first_ref[...])
    out_ref[0] = second_step(grads, master_ref[...], moment, second_ref[...])[0].astype(jnp.bfloat16)


def eighth_weights(totals, state, factor):
    size = state[0].shape[0] // 8
    core, cross, deep = wide_bits(3)
    spots = (eighth_index(core, cross, deep), eighth_index(core, 1 - cross, 1 - deep))
    both = pl.pallas_call(
        functools.partial(eighth_kernel, factor=factor),
        grid_spec=pltpu.PrefetchScalarGridSpec(
            num_scalar_prefetch=1,
            grid=(2,),
            in_specs=[pl.BlockSpec((size, 128), lambda i, spot: (spot[i], 0))] * 4,
            out_specs=pl.BlockSpec((1, size, 128), lambda i, spot: (i, 0, 0)),
        ),
        out_shape=jax.ShapeDtypeStruct((2, size, 128), jnp.bfloat16),
        name="eighth_weights",
    )(jnp.stack(spots).astype(jnp.int32), totals, *state)
    return both[0], both[1]


def adam_kernel(group_ref, total_ref, master_ref, first_ref, second_ref, *refs, factor):
    grads_ref, master_out, first_out, second_out, weights_ref = refs[-5:]
    grads = total_ref[...].astype(jnp.float32) * factor
    moment = first_step(grads, first_ref[...])
    master_next, second_next = second_step(grads, master_ref[...], moment, second_ref[...])
    grads_ref[...] = grads
    master_out[...] = master_next
    first_out[...] = moment
    second_out[...] = second_next
    weights_ref[0] = master_next.astype(jnp.bfloat16)


def adam_rows(totals, state, factor, first_block, last_block, onto, after):
    rows = state[0].shape[0]
    row_spec = pl.BlockSpec((BLOCK_ROWS, 128), lambda i, g: (first_block + i, 0))
    anywhere = pl.BlockSpec(memory_space=pl.ANY)
    wide = jax.ShapeDtypeStruct((rows, 128), jnp.float32)
    spare = 5 - len(onto)
    return pl.pallas_call(
        functools.partial(adam_kernel, factor=factor),
        grid_spec=pltpu.PrefetchScalarGridSpec(
            num_scalar_prefetch=1,
            grid=(last_block - first_block,),
            in_specs=[row_spec] * 4 + [anywhere] * (len(onto) + len(after)),
            out_specs=[row_spec] * 4
            + [pl.BlockSpec((1, BLOCK_ROWS, 128), lambda i, g: (g[0], first_block + i, 0))],
        ),
        out_shape=[wide] * 4 + [jax.ShapeDtypeStruct((2, rows, 128), jnp.bfloat16)],
        input_output_aliases={5 + i: spare + i for i in range(len(onto))},
        name="adam_rows",
    )(lax.axis_index("grp").reshape(1), totals, *state, *onto, *after)


def body(tokens, cotangent, window_place, master, first_moment, second_moment):
    part_rows = master.shape[0]
    wide_size = lax.axis_size("wide")
    group_size = lax.axis_size("grp")
    feature = tokens.shape[-1]
    micro_count, slots, tok_count, _ = tokens.shape
    masks = token_mask(window_place)
    if splits(part_rows):
        mine, diagonal = (part.astype(jnp.bfloat16) for part in own_eighths(master))
        gathered = gather_groups(mine, diagonal, lambda first: place_own(master))
    else:
        gathered = lax.all_gather(master.astype(jnp.bfloat16), "grp", axis=0, tiled=True)
    weights = unpack(gathered, feature)
    wins = micro_count * slots
    extra = -tok_count % 16

    def padded(values):
        values = values.reshape((wins,) + values.shape[2:])
        return jnp.pad(values, ((0, 0), (0, extra)) + ((0, 0),) * (values.ndim - 2))

    block_part, input_part, factors, tail = window_pass(
        padded(tokens), padded(cotangent), padded(masks), weights
    )
    filled = sum(math.prod(dims_of) for dims_of in layout(feature)[:8]) // 128
    tail = jnp.concatenate([member.reshape(-1) for member in tail])
    tail_rows = part_rows * group_size - filled
    tail = jnp.pad(tail, (0, tail_rows * 128 - tail.shape[0])).reshape(tail_rows, 128)
    packed = pack_shares(factors, tail, part_rows, group_size, wide_size)
    owned = reduce_shares(packed)
    block_out = block_part[:, :tok_count].reshape(tokens.shape)
    input_grad = input_part[:, :tok_count].reshape(tokens.shape)
    owned, block_out, input_grad = lax.optimization_barrier((owned, block_out, input_grad))
    totals = lax.all_gather(owned, "wide", axis=0, tiled=True)
    factor = 1.0 / (micro_count * wide_size * group_size)
    bias_total = totals[part_rows : part_rows + feature // 128]
    proj_bias_grad = bias_total.astype(jnp.float32).reshape(-1) * factor
    state = (master, first_moment, second_moment)
    if splits(part_rows):
        updated = []

        def finish(first):
            blocks = pl.cdiv(part_rows, BLOCK_ROWS)
            half = blocks // 2
            held = gathered.reshape(2, part_rows, 128)
            begun = adam_rows(totals, state, factor, 0, half, (held,), ())
            updated.extend(adam_rows(totals, state, factor, half, blocks, begun, (first,)))
            return updated.pop()

        mine, diagonal = eighth_weights(totals, state, factor)
        weights_next = gather_groups(mine, diagonal, finish)
        grads, master_next, moment_next, second_next = updated
    else:
        grads = totals[:part_rows].astype(jnp.float32) * factor
        moment_next = first_step(grads, first_moment)
        master_next, second_next = second_step(grads, master, moment_next, second_moment)
        own_weights = master_next.astype(jnp.bfloat16)
        weights_next = lax.all_gather(own_weights, "grp", axis=0, tiled=True)
    return (
        block_out,
        input_grad,
        grads,
        master_next,
        moment_next,
        second_next,
        weights_next,
        proj_bias_grad,
    )


def solution(mesh):
    return jax.shard_map(
        body,
        mesh=mesh,
        in_specs=(
            P(None, ("wide", "grp"), None, None),
            P(None, ("wide", "grp"), None, None),
            P(None, ("wide", "grp")),
            P("grp", None),
            P("grp", None),
            P("grp", None),
        ),
        out_specs=(
            P(None, ("wide", "grp"), None, None),
            P(None, ("wide", "grp"), None, None),
            P("grp", None),
            P("grp", None),
            P("grp", None),
            P("grp", None),
            P(),
            P(),
        ),
        check_vma=False,
    )
```
